32 devices in a mesh: dp: 8 (over y, x, core), tensor: 4 (over z).
Axes of the slice: x: 2, y: 2, z: 4, core: 2. Of those that a mesh axis runs over, the one named last changes fastest.
Arguments:
- hidden_in: bfloat16 [2, 8, 1024, 2048], P(None, None, ('dp', 'tensor')), may hold values from -6 to 6
- lengths: int32 [2, 8], replicated, may hold values from 1 to 1024, 6144 in all within a row
- dealing: int32 [2, 8], replicated, may hold values from 0 to 7, each once within a row
- cotangent: bfloat16 [2, 8, 1024, 2048], P(None, None, ('dp', 'tensor')), may hold values from -6 to 6
- attn_gain: bfloat16 [2048], P(('dp', 'tensor')), may hold values from 0.5 to 1.5
- attn_shift: bfloat16 [2048], P(('dp', 'tensor')), may hold values from -1.5 to 1.5
- ffn_gain: bfloat16 [2048], P(('dp', 'tensor')), may hold values from 0.5 to 1.5
- ffn_shift: bfloat16 [2048], P(('dp', 'tensor')), may hold values from -1.5 to 1.5
- qkv_weight: bfloat16 [2048, 8, 768], P('dp', 'tensor'), may hold values from -0.125 to 0.125
- qkv_bias: bfloat16 [8, 768], P('tensor', 'dp'), may hold values from -0.25 to 0.25
- dense_weight: bfloat16 [8, 256, 2048], P('tensor', 'dp'), may hold values from -1.5 to 1.5
- dense_bias: bfloat16 [2048], P(('dp', 'tensor')), may hold values from -1.5 to 1.5
- fc1_weight: bfloat16 [2048, 8192], P('dp', 'tensor'), may hold values from -0.125 to 0.125
- fc1_bias: bfloat16 [8, 1024], P('tensor', 'dp'), may hold values from -1.5 to 1.5
- fc2_weight: bfloat16 [8192, 2048], P('tensor', 'dp'), may hold values from -0.0625 to 0.0625
- fc2_bias: bfloat16 [2048], P(('dp', 'tensor')), may hold values from -1.5 to 1.5
Outputs:
- output: bfloat16 [2, 8, 1024, 2048], P(None, None, ('dp', 'tensor'))
- input_grad: bfloat16 [2, 8, 1024, 2048], P(None, None, ('dp', 'tensor'))
- attngain_grad: float32 [2048], P(('dp', 'tensor'))
- attnshift_grad: float32 [2048], P(('dp', 'tensor'))
- ffngain_grad: float32 [2048], P(('dp', 'tensor'))
- ffnshift_grad: float32 [2048], P(('dp', 'tensor'))
- qkvweight_grad: float32 [2048, 8, 768], P('dp', 'tensor')
- qkvbias_grad: float32 [8, 768], P('tensor', 'dp')
- denseweight_grad: float32 [8, 256, 2048], P('tensor', 'dp')
- densebias_grad: float32 [2048], P(('dp', 'tensor'))
- fc1weight_grad: float32 [2048, 8192], P('dp', 'tensor')
- fc1bias_grad: float32 [8, 1024], P('tensor', 'dp')
- fc2weight_grad: float32 [8192, 2048], P('tensor', 'dp')
- fc2bias_grad: float32 [2048], P(('dp', 'tensor'))
The draws below stay inside these ranges and needn't reach their ends.
Inputs may be any that keep to these rules, and one draw needn't show every extreme that they name: lengths[m, j] belongs to the sequence in input slot dealing[m, j]; in each micro-batch the lengths sum to 6144 and the longest is 1024. Each row of dealing holds every slot number once.
All inputs are finite; a program needn't handle non-finite values.
Results may differ from the reference program's by a relative error of at most 0.013.
Values may be sent and summed in bfloat16 or wider, within the bound.
No kernel may reach another device: no remote copies, remote signals or barrier semaphores. Data moves between devices by JAX's collectives and lax.ppermute only.
A program may use at most 320 MiB of HBM per device.

```python
import math
import jax
import jax.numpy as jnp
import numpy as np
from jax import lax

D = 2048
HEADS = 8
HD = 256
ROT = 64
FF = 8192
SEQ_LEN = 1024
MICRO = 2
SEQS_MB = 8


def raised(drawn, own_key, source, target, parts, factor):
    owner, partner = [(jnp.arange(drawn.shape[dim]) // (drawn.shape[dim] // parts)).reshape([-1 if axis == dim else 1 for axis in range(drawn.ndim)]) for dim in (source, target)]
    chosen = jax.random.permutation(own_key, parts)[partner]
    strong = (owner == chosen) | (owner == (partner + parts // 2) % parts)
    return jnp.where(strong, factor * drawn, drawn)


def steps_of(key, extent, split, least, top_value):
    def one(position, blocks):
        steps = jax.random.uniform(jax.random.fold_in(jax.random.fold_in(key, 6), position), (blocks,), jnp.float32, least / len(split), top_value / len(split))
        return jnp.repeat(jnp.exp(steps), extent[position] // blocks).reshape((-1,) + (1,) * (len(extent) - position - 1))

    loudness = one(*split[0])
    for cut in split[1:]:
        loudness = loudness * one(*cut)
    return loudness


def length_profile(amount, total, reach, slope):
    weights = [(1 << 20) // math.isqrt(standing ** slope) + 1 for standing in range(2, amount + 1)]
    surplus, holding = total - reach - (amount - 1), [1] * (amount - 1)
    while surplus > 0:
        candidates = [i for i in range(amount - 1) if holding[i] < reach]
        mass, remaining = sum([weights[i] for i in candidates]), surplus
        for i in candidates:
            addition = min(reach - holding[i], max(1, remaining * weights[i] // mass), surplus)
            holding[i] = holding[i] + addition
            surplus = surplus - addition
    return np.array([reach] + holding)


def uneven_parts(key, amount, total, bound, skew):
    if amount == 2:
        one = jax.random.randint(key, (), max(1, total - bound), min(bound, total - 1) + 1)
        return jnp.stack([one, total - one])
    sizes = jnp.asarray(length_profile(amount, total, bound, skew), jnp.int32)
    pairs = (amount - 1) // 2
    giver, receiver = sizes[1:1 + 2 * pairs:2], sizes[2:2 + 2 * pairs:2]
    room = jnp.minimum(giver - 1, bound - receiver)
    moved = jax.random.randint(jax.random.fold_in(key, 1), (pairs,), 0, 1 << 20) % (room + 1)
    sizes = sizes.at[1:1 + 2 * pairs:2].set(giver - moved).at[2:2 + 2 * pairs:2].set(receiver + moved)
    return sizes[jax.random.permutation(jax.random.fold_in(key, 2), amount)]


def bell_draw(stream_key, dims, scale, limit, shards=(), held_as=jnp.bfloat16):
    values = scale * jax.random.normal(stream_key, dims, jnp.float32)
    if shards:
        values = values * steps_of(stream_key, dims, shards, -0.22, 0.18)
    return jnp.clip(values, -limit, limit).astype(held_as)


def gaussian_with(own_key, extent, deviation, bound, split, heavy, held_as=jnp.bfloat16):
    array = deviation * jax.random.normal(own_key, extent, jnp.float32)
    if split:
        array = array * steps_of(own_key, extent, split, -0.22, 0.18)
    return jnp.clip(raised(array, jax.random.fold_in(own_key, 3), *heavy), -bound, bound).astype(held_as)


def setup_inputs(seed: int = 0) -> dict:
    arg_keys = jax.random.split(jax.random.key(seed), 17)
    return {
        "hidden_in": bell_draw(arg_keys[0], (MICRO, SEQS_MB, SEQ_LEN, D), 1.0, 6.0, ((2, 32),)),
        "lengths": jax.vmap(lambda own: uneven_parts(own, SEQS_MB, SEQS_MB * SEQ_LEN * 3 // 4, SEQ_LEN, 2))(jax.random.split(arg_keys[1], MICRO)).reshape((MICRO, SEQS_MB)).astype(jnp.int32),
        "dealing": jax.vmap(lambda own: jax.random.permutation(own, SEQS_MB))(jax.random.split(arg_keys[2], MICRO)).reshape((MICRO, SEQS_MB)).astype(jnp.int32),
        "cotangent": gaussian_with(arg_keys[3], (MICRO, SEQS_MB, SEQ_LEN, D), 1.0, 6.0, ((2, 32),), (2, 3, 32, 2.75)),
        "attn_gain": jnp.clip(1.0 + 0.1 * jax.random.normal(arg_keys[4], (D,), jnp.float32), 0.5, 1.5).astype(jnp.bfloat16),
        "attn_shift": bell_draw(arg_keys[5], (D,), 0.3, 1.5, ((0, 32),)),
        "ffn_gain": jnp.clip(1.0 + 0.1 * jax.random.normal(arg_keys[6], (D,), jnp.float32), 0.5, 1.5).astype(jnp.bfloat16),
        "ffn_shift": bell_draw(arg_keys[7], (D,), 0.3, 1.5, ((0, 32),)),
        "qkv_weight": bell_draw(arg_keys[8], (D, HEADS, 3 * HD), D ** -0.5, 0.125, ((0, 8), (1, 4))),
        "qkv_bias": bell_draw(arg_keys[9], (HEADS, 3 * HD), 0.05, 0.25, ((0, 4), (1, 8))),
        "dense_weight": bell_draw(arg_keys[10], (HEADS, HD, D), (D // 128) ** -0.5, 1.5, ((0, 4), (1, 8))),
        "dense_bias": bell_draw(arg_keys[11], (D,), 0.3, 1.5, ((0, 32),)),
        "fc1_weight": bell_draw(arg_keys[12], (D, FF), D ** -0.5, 0.125, ((0, 8), (1, 4))),
        "fc1_bias": bell_draw(arg_keys[13], (HEADS, FF // HEADS), 0.3, 1.5, ((0, 4), (1, 8))),
        "fc2_weight": bell_draw(arg_keys[14], (FF, D), FF ** -0.5, 0.0625, ((0, 4), (1, 8))),
        "fc2_bias": bell_draw(arg_keys[15], (D,), 0.3, 1.5, ((0, 32),)),
    }


@jax.custom_vjp
def low(v):
    return lax.optimization_barrier(v.astype(jnp.bfloat16)).astype(jnp.float32)

@jax.custom_vjp
def low_back(v):
    return v

def low_keep(v):
    return (low(v), None)

def low_pass(kept, grad):
    return (grad,)

def back_keep(v):
    return (v, None)

def back_low(kept, grad):
    return (low(grad),)
low.defvjp(low_keep, low_pass)
low_back.defvjp(back_keep, back_low)
EPSILON = 1e-05
ROPE_BASE = 10000.0
NEG_FILL = -1e+30
HIGHEST = lax.Precision.HIGHEST

def layer_norm(hidden, gain, shift):
    centred = hidden - lax.optimization_barrier(jnp.mean(hidden, axis=-1, keepdims=True))
    scaling = lax.rsqrt(lax.optimization_barrier(jnp.mean(centred * centred, axis=-1, keepdims=True)) + EPSILON)
    return centred * scaling * gain + shift

def angles(positions):
    freqs = jnp.exp(jnp.arange(ROT // 2, dtype=jnp.float32) * (-2.0 * math.log(ROPE_BASE) / ROT))
    phases = positions.astype(jnp.float32)[:, None] * freqs[None, :]
    return (jnp.cos(phases), jnp.sin(phases))

def rotate(heads, cosines, sines):
    half_rot = ROT // 2
    lead_part = heads[..., :half_rot]
    trail_part = heads[..., half_rot:ROT]
    cos_rows = cosines[:, None, :]
    sin_rows = sines[:, None, :]
    return jnp.concatenate([lead_part * cos_rows - trail_part * sin_rows, trail_part * cos_rows + lead_part * sin_rows, heads[..., ROT:]], axis=-1)

def sequence_forward(hidden, seq_length, params):
    attn_gain, attn_shift, ffn_gain, ffn_shift, qkv_weight, qkv_bias, dense_weight, dense_bias, fc1_weight, fc1_bias, fc2_weight, fc2_bias = params
    normed_one = low(layer_norm(hidden, attn_gain, attn_shift))
    normed_two = low(layer_norm(hidden, ffn_gain, ffn_shift))
    projected = low_back(jnp.einsum('ld,dhe->lhe', normed_one, qkv_weight, precision=HIGHEST) + qkv_bias)
    positions = jnp.arange(SEQ_LEN, dtype=jnp.int32)
    cosines, sines = angles(positions)
    queries = low(rotate(projected[..., :HD], cosines, sines))
    key_rows = low(rotate(projected[..., HD:2 * HD], cosines, sines))
    value_rows = low(projected[..., 2 * HD:])
    block_rows = min(512, SEQ_LEN)
    scale = 1.0 / math.sqrt(HD)

    def attend(row_start):
        q_block = lax.dynamic_slice_in_dim(queries, row_start, block_rows, 0)
        scores = low_back(jnp.einsum('qhe,khe->hqk', q_block, key_rows, precision=HIGHEST) * scale)
        q_pos = row_start + jnp.arange(block_rows, dtype=jnp.int32)
        allowed = (positions[None, :] <= q_pos[:, None]) & (positions[None, :] < seq_length)
        scores = jnp.where(allowed[None], scores, NEG_FILL)
        row_max = lax.optimization_barrier(jnp.max(scores, axis=-1, keepdims=True))
        expo = jnp.exp(scores - row_max)
        softmax_w = low(expo / lax.optimization_barrier(jnp.sum(expo, axis=-1, keepdims=True)))
        return jnp.einsum('hqk,khe->qhe', softmax_w, value_rows, precision=HIGHEST)
    starts = jnp.arange(SEQ_LEN // block_rows, dtype=jnp.int32) * block_rows
    mixed = lax.map(jax.checkpoint(attend), starts).reshape(SEQ_LEN, HEADS, HD)
    mixed = low(low_back(mixed))
    attn_out = jnp.einsum('lhe,hed->ld', mixed, dense_weight, precision=HIGHEST)
    preact = low_back(jnp.dot(normed_two, fc1_weight, precision=HIGHEST, preferred_element_type=jnp.float32) + fc1_bias.reshape(FF))
    activation = low(jax.nn.gelu(preact, approximate=False))
    ffn_out = jnp.dot(activation, fc2_weight, precision=HIGHEST, preferred_element_type=jnp.float32)
    return hidden + attn_out + dense_bias + ffn_out + fc2_bias

def reference(hidden_in, lengths, dealing, cotangent, attn_gain, attn_shift, ffn_gain, ffn_shift, qkv_weight, qkv_bias, dense_weight, dense_bias, fc1_weight, fc1_bias, fc2_weight, fc2_bias):
    slots = jnp.arange(SEQS_MB, dtype=jnp.int32)
    picked = dealing[:, :, None] == slots[None, None, :]
    slot_len = lax.optimization_barrier(jnp.sum(jnp.where(picked, lengths[:, :, None], 0), axis=1)).astype(jnp.int32).reshape(MICRO * SEQS_MB)
    params = tuple((param.astype(jnp.float32) for param in (attn_gain, attn_shift, ffn_gain, ffn_shift, qkv_weight, qkv_bias, dense_weight, dense_bias, fc1_weight, fc1_bias, fc2_weight, fc2_bias)))
    inputs = hidden_in.astype(jnp.float32).reshape(MICRO * SEQS_MB, SEQ_LEN, D)
    seq_fn = jax.checkpoint(sequence_forward)

    def forward(all_rows, all_params):

        def step(carry, item):
            return (carry, seq_fn(item[0], item[1], all_params))
        return lax.scan(step, jnp.zeros((), jnp.float32), (all_rows, slot_len))[1]
    outputs, pullback = jax.vjp(forward, inputs, params)
    input_grad, param_grads = pullback(cotangent.astype(jnp.float32).reshape(MICRO * SEQS_MB, SEQ_LEN, D))
    full_shape = hidden_in.shape
    return (outputs.reshape(full_shape).astype(jnp.bfloat16), input_grad.reshape(full_shape).astype(jnp.bfloat16), param_grads[0], param_grads[1], param_grads[2], param_grads[3], param_grads[4], param_grads[5], param_grads[6], param_grads[7], param_grads[8], param_grads[9], param_grads[10], param_grads[11])
```

```python
import functools
import math

import jax
import jax.numpy as jnp
from jax import lax
from jax.experimental import pallas as pl
from jax.experimental.pallas import tpu as pltpu
from jax.sharding import PartitionSpec as P

HD = 256
ROT = 64
EPSILON = 1e-05
ROPE_BASE = 10000.0
NEG_FILL = -1e30
SQRT_HALF = 0.7071067811865476
INV_ROOT_TWO_PI = 0.3989422804014327
BF = jnp.bfloat16
F32 = jnp.float32
FAR = 1 << 20


def line_gather(x, axis, n):
    left, right = [None], [None]
    cur = x
    for s in range(1, n):
        cur = lax.ppermute(cur, axis, [(k, k + 1) for k in range(s - 1, n - 1)])
        left.append(cur)
    cur = x
    for s in range(1, n):
        cur = lax.ppermute(cur, axis, [(k, k - 1) for k in range(1, n - s + 1)])
        right.append(cur)
    return [x] + [left[s] + right[n - s] for s in range(1, n)]


def line_scatter(parts, axis, n):
    got_right = got_left = None
    for s in range(n - 1, 0, -1):
        val = parts[n - s] if got_right is None else parts[n - s] + got_right.astype(F32)
        got_right = lax.ppermute(val.astype(BF), axis, [(k, k + 1) for k in range(n - s)])
        val = parts[s] if got_left is None else parts[s] + got_left.astype(F32)
        got_left = lax.ppermute(val.astype(BF), axis, [(k, k - 1) for k in range(s, n)])
    return parts[0] + got_right.astype(F32) + got_left.astype(F32)


def small_gather(x, axis, n):
    me = lax.axis_index(axis)
    out = x[None]
    bit = 1
    while bit < n:
        other = lax.ppermute(out, axis, [(i, i ^ bit) for i in range(n)])
        mine_high = (me & bit) != 0
        out = jnp.concatenate(
            [jnp.where(mine_high, other, out), jnp.where(mine_high, out, other)], axis=0
        )
        bit *= 2
    return out


def small_scatter(x, axis, n):
    me = lax.axis_index(axis)
    bit = n // 2
    while bit:
        low, high = x[:bit], x[bit:]
        mine_high = (me & bit) != 0
        sent = jnp.where(mine_high, low, high)
        kept = jnp.where(mine_high, high, low)
        x = kept + lax.ppermute(sent, axis, [(i, i ^ bit) for i in range(n)])
        bit //= 2
    return x[0]


def rotated(x, cosines, sines):
    lanes = lax.broadcasted_iota(jnp.int32, x.shape, 1)
    partner = jnp.where(lanes < ROT // 2, pltpu.roll(x, 128 - ROT // 2, 1), pltpu.roll(x, ROT // 2, 1))
    return x * cosines + partner * sines


def scores_of(q, k, posq, posk):
    s = lax.dot_general(q, k, (((1,), (1,)), ((), ())), preferred_element_type=F32)
    return jnp.where(posk <= posq, s * (1.0 / math.sqrt(HD)), NEG_FILL)


def attend_kernel(n_blocks, posq_ref, posk_ref, cos_ref, sin_ref, qkv_ref, low_ref, mixed_ref):
    n_slots, rows, _ = qkv_ref.shape
    span = rows // n_blocks
    for t in range(n_slots):
        for base in (0, HD):
            lead = rotated(qkv_ref[t, :, base : base + 128], cos_ref[t], sin_ref[t])
            low_ref[t, :, base : base + 128] = lead.astype(BF)
            low_ref[t, :, base + 128 : base + HD] = qkv_ref[t, :, base + 128 : base + HD].astype(BF)
        low_ref[t, :, 2 * HD :] = qkv_ref[t, :, 2 * HD :].astype(BF)
    for b in range(n_blocks):
        own, seen = pl.ds(b * span, span), span * (b + 1)
        n_q, n_k = n_slots * span, n_slots * seen
        q = low_ref[:, own, :HD].reshape(n_q, HD)
        k = low_ref[:, :seen, HD : 2 * HD].reshape(n_k, HD)
        v = low_ref[:, :seen, 2 * HD :].reshape(n_k, HD)
        posq = posq_ref[:, own, :].reshape(n_q, 1)
        s = scores_of(q, k, posq, posk_ref[b, :, :n_k])
        e = jnp.exp(s - jnp.max(s, axis=-1, keepdims=True))
        p = e * (1.0 / jnp.sum(e, axis=-1, keepdims=True))
        mixed = jnp.dot(p.astype(BF), v, preferred_element_type=F32)
        mixed_ref[:, own, :] = mixed.astype(BF).reshape(n_slots, span, HD)


def attend_back_kernel(
    n_blocks, posq_ref, posk_ref, cos_ref, sin_ref, low_ref, dmix_ref, grad_ref, dk_ref, dv_ref
):
    n_slots, rows, _ = low_ref.shape
    span = rows // n_blocks
    scale = 1.0 / math.sqrt(HD)
    for b in reversed(range(n_blocks)):
        own, seen = pl.ds(b * span, span), span * (b + 1)
        n_q, n_k = n_slots * span, n_slots * seen
        q = low_ref[:, own, :HD].reshape(n_q, HD)
        k = low_ref[:, :seen, HD : 2 * HD].reshape(n_k, HD)
        v = low_ref[:, :seen, 2 * HD :].reshape(n_k, HD)
        dmix = dmix_ref[:, own, :].reshape(n_q, HD)
        posq = posq_ref[:, own, :].reshape(n_q, 1)
        s = scores_of(q, k, posq, posk_ref[b, :, :n_k])
        e = jnp.exp(s - jnp.max(s, axis=-1, keepdims=True))
        p = e * (1.0 / jnp.sum(e, axis=-1, keepdims=True))
        dp = lax.dot_general(dmix, v, (((1,), (1,)), ((), ())), preferred_element_type=F32)
        ds = (p * (dp - jnp.sum(p * dp, axis=-1, keepdims=True))).astype(BF)
        dq = jnp.dot(ds, k, preferred_element_type=F32) * scale
        dk = lax.dot_general(ds, q, (((0,), (0,)), ((), ())), preferred_element_type=F32)
        dv = lax.dot_general(p.astype(BF), dmix, (((0,), (0,)), ((), ())), preferred_element_type=F32)
        dk, dv = dk.reshape(n_slots, seen, HD), dv.reshape(n_slots, seen, HD)
        if b == n_blocks - 1:
            dk_ref[...] = dk
            dv_ref[...] = dv
        else:
            dk_ref[:, :seen, :] += dk
            dv_ref[:, :seen, :] += dv
        dq = dq.reshape(n_slots, span, HD)
        for t in range(n_slots):
            lead = rotated(dq[t, :, :128], cos_ref[t, own, :], -sin_ref[t, own, :])
            grad_ref[t, own, :128] = lead.astype(BF)
            grad_ref[t, own, 128:HD] = dq[t, :, 128:].astype(BF)
    for t in range(n_slots):
        lead = rotated(dk_ref[t, :, :128] * scale, cos_ref[t], -sin_ref[t])
        grad_ref[t, :, HD : HD + 128] = lead.astype(BF)
        grad_ref[t, :, HD + 128 : 2 * HD] = (dk_ref[t, :, 128:] * scale).astype(BF)
        grad_ref[t, :, 2 * HD :] = dv_ref[t].astype(BF)


def whole_spec(shape):
    return pl.BlockSpec(shape, lambda h: (0,) * len(shape))


def head_spec(n_slots, rows, width):
    return pl.BlockSpec((n_slots, rows, width), lambda h: (0, 0, h))


def attend(tables, qkv):
    posq, posk, cosines, sines = tables
    n_slots, rows, width = qkv.shape
    heads = width // (3 * HD)
    pairs = (n_slots * rows) ** 2 // 2 * heads
    return pl.pallas_call(
        functools.partial(attend_kernel, posk.shape[0]),
        grid=(heads,),
        in_specs=[whole_spec(t.shape) for t in tables] + [head_spec(n_slots, rows, 3 * HD)],
        out_specs=[head_spec(n_slots, rows, 3 * HD), head_spec(n_slots, rows, HD)],
        out_shape=[
            jax.ShapeDtypeStruct(qkv.shape, BF),
            jax.ShapeDtypeStruct((n_slots, rows, heads * HD), BF),
        ],
        cost_estimate=pl.CostEstimate(
            flops=4 * pairs * HD, bytes_accessed=qkv.size * 8, transcendentals=pairs
        ),
        compiler_params=pltpu.CompilerParams(vmem_limit_bytes=48 << 20),
        name="attend",
    )(posq, posk, cosines, sines, qkv)


def attend_back(tables, low, dmix):
    n_slots, rows, width = low.shape
    heads = width // (3 * HD)
    pairs = (n_slots * rows) ** 2 // 2 * heads
    return pl.pallas_call(
        functools.partial(attend_back_kernel, tables[1].shape[0]),
        grid=(heads,),
        in_specs=[whole_spec(t.shape) for t in tables]
        + [head_spec(n_slots, rows, 3 * HD), head_spec(n_slots, rows, HD)],
        out_specs=head_spec(n_slots, rows, 3 * HD),
        out_shape=jax.ShapeDtypeStruct(low.shape, BF),
        scratch_shapes=[pltpu.VMEM((n_slots, rows, HD), F32)] * 2,
        cost_estimate=pl.CostEstimate(
            flops=10 * pairs * HD, bytes_accessed=low.size * 5, transcendentals=pairs
        ),
        compiler_params=pltpu.CompilerParams(vmem_limit_bytes=48 << 20),
        name="attend_back",
    )(*tables, low, dmix)


def unit_of(rows):
    centred = rows - jnp.mean(rows, axis=-1, keepdims=True)
    scaling = lax.rsqrt(jnp.mean(centred * centred, axis=-1, keepdims=True) + EPSILON)
    return centred * scaling, scaling


def dot(a, b, dims, out=F32):
    return lax.dot_general(a, b, (dims, ((), ())), preferred_element_type=F32).astype(out)


def per_device(
    hidden_in,
    lengths,
    dealing,
    cotangent,
    attn_gain,
    attn_shift,
    ffn_gain,
    ffn_shift,
    qkv_weight,
    qkv_bias,
    dense_weight,
    dense_bias,
    fc1_weight,
    fc1_bias,
    fc2_weight,
    fc2_bias,
):
    n_t, n_d = lax.axis_size("tensor"), lax.axis_size("dp")
    my_t, my_d = lax.axis_index("tensor"), lax.axis_index("dp")
    micros, seqs, piece, width = hidden_in.shape
    heads = qkv_weight.shape[1]
    units = fc1_weight.shape[1]
    rows = n_d * piece
    n_blocks = 4

    def deal(x):
        return lax.all_to_all(x, "dp", split_axis=0, concat_axis=0, tiled=True).reshape(rows, width)

    def undeal(x):
        return lax.all_to_all(
            x.reshape(seqs, piece, width), "dp", split_axis=0, concat_axis=0, tiled=True
        )

    own_x = [deal(hidden_in[m]) for m in range(micros)]
    own_g = [deal(cotangent[m]) for m in range(micros)]

    eighth = width // (n_d * n_t)
    packed = jnp.concatenate(
        [attn_gain, attn_shift, ffn_gain, ffn_shift, dense_bias, fc2_bias]
        + [qkv_bias.reshape(-1), fc1_bias.reshape(-1)]
    )
    packed = small_gather(packed, "dp", n_d)
    vectors = small_gather(packed[:, : 6 * eighth], "tensor", n_t)
    vectors = vectors.reshape(n_t, n_d, 6, eighth).transpose(2, 1, 0, 3).reshape(6, width)
    vectors = vectors.astype(F32)
    gain_one, shift_one, gain_two, shift_two = vectors[0], vectors[1], vectors[2], vectors[3]
    out_shift = vectors[4] + vectors[5]
    rest = packed[:, 6 * eighth :].astype(F32)
    n_qb = qkv_bias.size
    qkv_shift = rest[:, :n_qb].reshape(n_d, heads, -1).transpose(1, 0, 2).reshape(-1)
    fc1_shift = rest[:, n_qb:].reshape(n_d, heads, -1).transpose(1, 0, 2).reshape(-1)

    w_qkv = lax.all_gather(qkv_weight.reshape(-1, heads * 3 * HD), "dp", axis=0, tiled=True)
    w_fc1 = lax.all_gather(fc1_weight, "dp", axis=0, tiled=True)
    w_dense = lax.all_gather(dense_weight, "dp", axis=1, tiled=True).reshape(heads * HD, width)
    w_fc2 = lax.all_gather(fc2_weight, "dp", axis=1, tiled=True)

    slots = jnp.arange(n_t, dtype=jnp.int32)
    part = (my_t - slots) % n_t
    local = jnp.arange(rows, dtype=jnp.int32)
    positions = ((local // piece) * n_t + part[:, None]) * piece + local % piece
    freqs = jnp.exp(
        jnp.arange(ROT // 2, dtype=F32) * (-2.0 * math.log(ROPE_BASE) / ROT)
    )
    phases = positions.astype(F32)[..., None] * freqs
    flat = jnp.zeros((n_t, rows, 128 - ROT), F32)
    cosines = jnp.concatenate([jnp.cos(phases), jnp.cos(phases), flat + 1.0], axis=-1)
    sines = jnp.concatenate([-jnp.sin(phases), jnp.sin(phases), flat], axis=-1)
    picked = dealing == my_d
    seq_lens = jnp.sum(jnp.where(picked, lengths, 0), axis=1)
    posq = positions[..., None]

    def tables(m):
        keyed = jnp.where(positions < seq_lens[m], positions, FAR)
        span = rows // n_blocks
        lists = []
        for b in range(n_blocks):
            seen = keyed[:, : span * (b + 1)].reshape(1, -1)
            lists.append(jnp.pad(seen, ((0, 0), (0, n_t * rows - seen.shape[1]))))
        return (posq, jnp.stack(lists), cosines, sines)

    all_tables = [tables(m) for m in range(micros)]
    sum_g = jnp.sum(cotangent.astype(F32), axis=(0, 1, 2))

    def gather_rows(x):
        return jnp.concatenate(line_gather(x, "tensor", n_t), axis=0)

    def scatter_rows(x):
        return line_scatter(list(x.reshape(n_t, rows, width)), "tensor", n_t)

    saved = []
    outputs = []
    for m in range(micros):
        x = gather_rows(own_x[m])
        unit, _ = unit_of(x.astype(F32))
        normed_one = (unit * gain_one + shift_one).astype(BF)
        normed_two = (unit * gain_two + shift_two).astype(BF)
        qkv = dot(normed_one, w_qkv, ((1,), (0,))) + qkv_shift
        low, mixed = attend(all_tables[m], qkv.reshape(n_t, rows, -1))
        mixed = mixed.reshape(n_t * rows, -1)
        preact = dot(normed_two, w_fc1, ((1,), (0,))) + fc1_shift
        cdf = 0.5 * (1.0 + lax.erf(preact * SQRT_HALF))
        act = (preact * cdf).astype(BF)
        slope = (cdf + preact * jnp.exp(-0.5 * preact * preact) * INV_ROOT_TWO_PI).astype(BF)
        branch = dot(mixed, w_dense, ((1,), (0,))) + dot(act, w_fc2, ((1,), (0,)))
        total = scatter_rows(branch)
        out = (own_x[m].astype(F32) + total + out_shift).astype(BF)
        outputs.append(undeal(out))
        saved.append((x, normed_one, normed_two, low, mixed, act, slope))

    backs = []
    for m in range(micros):
        x, normed_one, normed_two, low, mixed, act, slope = saved[m]
        g = gather_rows(own_g[m])
        d_mixed = dot(g, w_dense, ((1,), (1,)), BF)
        d_act = dot(g, w_fc2, ((1,), (1,)))
        d_pre = (d_act * slope.astype(F32)).astype(BF)
        d_qkv = attend_back(all_tables[m], low, d_mixed.reshape(n_t, rows, -1))
        d_qkv = d_qkv.reshape(n_t * rows, -1)
        backs.append((g, d_pre, d_qkv))

    def both(fn):
        total = fn(0)
        for m in range(1, micros):
            total = total + fn(m)
        return total

    rows_dim = ((0,), (0,))
    grad_fc2 = both(lambda m: dot(backs[m][0], saved[m][5], rows_dim)).astype(BF)
    grad_fc2 = lax.psum_scatter(grad_fc2, "dp", scatter_dimension=0, tiled=True)
    grad_fc2 = grad_fc2.astype(F32).T
    grad_dense = both(lambda m: dot(saved[m][4], backs[m][0], rows_dim)).astype(BF)
    grad_dense = lax.psum_scatter(
        grad_dense.reshape(heads, HD, width), "dp", scatter_dimension=1, tiled=True
    ).astype(F32)
    grad_fc1 = both(lambda m: dot(saved[m][2], backs[m][1], rows_dim)).astype(BF)
    grad_fc1 = lax.psum_scatter(grad_fc1, "dp", scatter_dimension=0, tiled=True).astype(F32)
    grad_qkv = both(lambda m: dot(saved[m][1], backs[m][2], rows_dim)).astype(BF)
    grad_qkv = lax.psum_scatter(grad_qkv, "dp", scatter_dimension=0, tiled=True)
    grad_qkv = grad_qkv.astype(F32).reshape(-1, heads, 3 * HD)

    grads_in = []
    norm_sums = []
    for m in range(micros):
        x = saved[m][0]
        g, d_pre, d_qkv = backs[m]
        d_one = dot(d_qkv, w_qkv, ((1,), (1,)))
        d_two = dot(d_pre, w_fc1, ((1,), (1,)))
        unit, _ = unit_of(x.astype(F32))
        norm_sums.append(
            jnp.stack(
                [
                    jnp.sum(d_one * unit, axis=0),
                    jnp.sum(d_one, axis=0),
                    jnp.sum(d_two * unit, axis=0),
                    jnp.sum(d_two, axis=0),
                ]
            )
        )
        total = scatter_rows(d_one * gain_one + d_two * gain_two)
        unit, scaling = unit_of(own_x[m].astype(F32))
        back = scaling * (
            total
            - jnp.mean(total, axis=-1, keepdims=True)
            - unit * jnp.mean(total * unit, axis=-1, keepdims=True)
        )
        grads_in.append(undeal((own_g[m].astype(F32) + back).astype(BF)))

    sums = jnp.concatenate([sum(norm_sums), sum_g[None]], axis=0)
    sums = sums.reshape(5, n_d, n_t, eighth).transpose(1, 2, 0, 3).reshape(n_d, -1)
    qkvb = both(lambda m: jnp.sum(backs[m][2].astype(F32), axis=0))
    fc1b = both(lambda m: jnp.sum(backs[m][1].astype(F32), axis=0))
    qkvb = qkvb.reshape(heads, n_d, -1).transpose(1, 0, 2).reshape(n_d, -1)
    fc1b = fc1b.reshape(heads, n_d, -1).transpose(1, 0, 2).reshape(n_d, -1)
    small = small_scatter(jnp.concatenate([sums, qkvb, fc1b], axis=1), "dp", n_d)
    n_sum = 5 * n_t * eighth
    mine = small_scatter(small[:n_sum].reshape(n_t, 5 * eighth), "tensor", n_t).reshape(5, eighth)
    qkvb = small[n_sum : n_sum + n_qb].reshape(heads, -1)
    fc1b = small[n_sum + n_qb :].reshape(heads, -1)

    return (
        jnp.stack(outputs),
        jnp.stack(grads_in),
        mine[0],
        mine[1],
        mine[2],
        mine[3],
        grad_qkv,
        qkvb,
        grad_dense,
        mine[4],
        grad_fc1,
        fc1b,
        grad_fc2,
        mine[4],
    )


def solution(mesh):
    rows = P(None, None, ("dp", "tensor"), None)
    vector = P(("dp", "tensor"))
    return jax.shard_map(
        per_device,
        mesh=mesh,
        in_specs=(
            rows,
            P(),
            P(),
            rows,
            vector,
            vector,
            vector,
            vector,
            P("dp", "tensor", None),
            P("tensor", "dp"),
            P("tensor", "dp", None),
            vector,
            P("dp", "tensor"),
            P("tensor", "dp"),
            P("tensor", "dp"),
            vector,
        ),
        out_specs=(
            rows,
            rows,
            vector,
            vector,
            vector,
            vector,
            P("dp", "tensor", None),
            P("tensor", "dp"),
            P("tensor", "dp", None),
            vector,
            P("dp", "tensor"),
            P("tensor", "dp"),
            P("tensor", "dp"),
            vector,
        ),
        check_vma=False,
    )
```

```python
import functools
import math

import jax
import jax.numpy as jnp
from jax import lax
from jax.experimental import pallas as pl
from jax.experimental.pallas import tpu as pltpu
from jax.sharding import PartitionSpec as P

HD = 256
ROT = 64
EPSILON = 1e-05
ROPE_BASE = 10000.0
NEG_FILL = -1e30
SQRT_HALF = 0.7071067811865476
INV_ROOT_TWO_PI = 0.3989422804014327
BF = jnp.bfloat16
F32 = jnp.float32
FAR = 1 << 20


class GatherChain:
    def __init__(self, x, axis, n):
        self.x, self.axis, self.n, self.step_no = x, axis, n, 0
        self.me = lax.axis_index(axis)
        self.left, self.right = [], []

    def steps(self):
        return self.n - 1

    def step(self):
        n = self.n
        s = self.step_no = self.step_no + 1
        to_right = self.left[-1] if self.left else self.x
        to_left = self.right[-1] if self.right else self.x
        pairs = [(k, k + 1) for k in range(s - 1, n - 1)]
        self.left.append(lax.ppermute(to_right, self.axis, pairs))
        pairs = [(k, k - 1) for k in range(1, n - s + 1)]
        self.right.append(lax.ppermute(to_left, self.axis, pairs))

    def live(self):
        return [self.left[-1], self.right[-1]]

    def set_live(self, values):
        self.left[-1], self.right[-1] = values


class SmallGather:
    def __init__(self, x, axis, n):
        self.out, self.axis, self.n, self.bit = x[None], axis, n, 1
        self.me = lax.axis_index(axis)

    def steps(self):
        return self.n.bit_length() - 1

    def step(self):
        bit, out = self.bit, self.out
        other = lax.ppermute(out, self.axis, [(i, i ^ bit) for i in range(self.n)])
        high = (self.me & bit) != 0
        self.out = jnp.concatenate(
            [jnp.where(high, other, out), jnp.where(high, out, other)], axis=0
        )
        self.bit *= 2

    def live(self):
        return [self.out]

    def set_live(self, values):
        self.out = values[0]


class SmallScatter:
    def __init__(self, x, axis, n):
        self.out, self.axis, self.n, self.bit = x, axis, n, n // 2
        self.me = lax.axis_index(axis)

    def steps(self):
        return self.n.bit_length() - 1

    def step(self):
        bit, x = self.bit, self.out
        low, high = x[:bit], x[bit:]
        mine_high = (self.me & bit) != 0
        sent = jnp.where(mine_high, low, high)
        kept = jnp.where(mine_high, high, low)
        self.out = kept + lax.ppermute(sent, self.axis, [(i, i ^ bit) for i in range(self.n)])
        self.bit //= 2

    def live(self):
        return [self.out]

    def set_live(self, values):
        self.out = values[0]


def shifts(n):
    return [[(k, (k + s) % n) for k in range(n)] for s in range(1, n)]


def direct_gather(x, axis, n):
    me = lax.axis_index(axis)
    got = jnp.stack([x] + [lax.ppermute(x, axis, pairs) for pairs in shifts(n)])
    order = (me - jnp.arange(n)) % n
    chosen = order[None, :] == jnp.arange(n)[:, None]
    return jnp.sum(jnp.where(chosen[:, :, None], got[None], 0), axis=1).astype(x.dtype)


def direct_scatter(x, axis, n):
    me = lax.axis_index(axis)
    total = lax.dynamic_index_in_dim(x, me, 0, keepdims=False)
    for s, pairs in enumerate(shifts(n), 1):
        sent = lax.dynamic_index_in_dim(x, (me + s) % n, 0, keepdims=False)
        total = total + lax.ppermute(sent, axis, pairs)
    return total


def rotated(x, cosines, sines):
    lanes = lax.broadcasted_iota(jnp.int32, x.shape, 1)
    partner = jnp.where(lanes < ROT // 2, pltpu.roll(x, 128 - ROT // 2, 1), pltpu.roll(x, ROT // 2, 1))
    return x * cosines + partner * sines


def scores_of(q, k, posq, posk):
    s = lax.dot_general(q, k, (((1,), (1,)), ((), ())), preferred_element_type=F32)
    return jnp.where(posk <= posq, s * (1.0 / math.sqrt(HD)), NEG_FILL)


def attend_kernel(n_blocks, posq_ref, posk_ref, cos_ref, sin_ref, qkv_ref, low_ref, mixed_ref):
    n_slots, rows, _ = qkv_ref.shape
    span = rows // n_blocks
    for t in range(n_slots):
        for base in (0, HD):
            lead = rotated(qkv_ref[t, :, base : base + 128], cos_ref[t], sin_ref[t])
            low_ref[t, :, base : base + 128] = lead.astype(BF)
            low_ref[t, :, base + 128 : base + HD] = qkv_ref[t, :, base + 128 : base + HD].astype(BF)
        low_ref[t, :, 2 * HD :] = qkv_ref[t, :, 2 * HD :].astype(BF)
    for b in range(n_blocks):
        own, seen = pl.ds(b * span, span), span * (b + 1)
        n_q, n_k = n_slots * span, n_slots * seen
        q = low_ref[:, own, :HD].reshape(n_q, HD)
        k = low_ref[:, :seen, HD : 2 * HD].reshape(n_k, HD)
        v = low_ref[:, :seen, 2 * HD :].reshape(n_k, HD)
        posq = posq_ref[:, own, :].reshape(n_q, 1)
        s = scores_of(q, k, posq, posk_ref[b, :, :n_k])
        e = jnp.exp(s - jnp.max(s, axis=-1, keepdims=True))
        p = e * (1.0 / jnp.sum(e, axis=-1, keepdims=True))
        mixed = jnp.dot(p.astype(BF), v, preferred_element_type=F32)
        mixed_ref[:, own, :] = mixed.astype(BF).reshape(n_slots, span, HD)


def attend_back_kernel(
    n_blocks,
    posq_ref,
    posk_ref,
    cos_ref,
    sin_ref,
    low_ref,
    dmix_ref,
    grad_ref,
    bias_ref,
    dk_ref,
    dv_ref,
):
    n_slots, rows, _ = low_ref.shape
    span = rows // n_blocks
    scale = 1.0 / math.sqrt(HD)
    for b in reversed(range(n_blocks)):
        own, seen = pl.ds(b * span, span), span * (b + 1)
        n_q, n_k = n_slots * span, n_slots * seen
        q = low_ref[:, own, :HD].reshape(n_q, HD)
        k = low_ref[:, :seen, HD : 2 * HD].reshape(n_k, HD)
        v = low_ref[:, :seen, 2 * HD :].reshape(n_k, HD)
        dmix = dmix_ref[:, own, :].reshape(n_q, HD)
        posq = posq_ref[:, own, :].reshape(n_q, 1)
        s = scores_of(q, k, posq, posk_ref[b, :, :n_k])
        e = jnp.exp(s - jnp.max(s, axis=-1, keepdims=True))
        p = e * (1.0 / jnp.sum(e, axis=-1, keepdims=True))
        dp = lax.dot_general(dmix, v, (((1,), (1,)), ((), ())), preferred_element_type=F32)
        ds = (p * (dp - jnp.sum(p * dp, axis=-1, keepdims=True))).astype(BF)
        dq = jnp.dot(ds, k, preferred_element_type=F32) * scale
        dk = lax.dot_general(ds, q, (((0,), (0,)), ((), ())), preferred_element_type=F32)
        dv = lax.dot_general(p.astype(BF), dmix, (((0,), (0,)), ((), ())), preferred_element_type=F32)
        dk, dv = dk.reshape(n_slots, seen, HD), dv.reshape(n_slots, seen, HD)
        if b == n_blocks - 1:
            dk_ref[...] = dk
            dv_ref[...] = dv
        else:
            dk_ref[:, :seen, :] += dk
            dv_ref[:, :seen, :] += dv
        dq = dq.reshape(n_slots, span, HD)
        for t in range(n_slots):
            lead = rotated(dq[t, :, :128], cos_ref[t, own, :], -sin_ref[t, own, :])
            grad_ref[t, own, :128] = lead.astype(BF)
            grad_ref[t, own, 128:HD] = dq[t, :, 128:].astype(BF)
    for t in range(n_slots):
        lead = rotated(dk_ref[t, :, :128] * scale, cos_ref[t], -sin_ref[t])
        grad_ref[t, :, HD : HD + 128] = lead.astype(BF)
        grad_ref[t, :, HD + 128 : 2 * HD] = (dk_ref[t, :, 128:] * scale).astype(BF)
        grad_ref[t, :, 2 * HD :] = dv_ref[t].astype(BF)
        summed = jnp.sum(grad_ref[t].astype(F32), axis=0, keepdims=True)
        bias_ref[0] = summed if t == 0 else bias_ref[0] + summed


def whole_spec(shape):
    return pl.BlockSpec(shape, lambda h: (0,) * len(shape))


def head_spec(n_slots, rows, width):
    return pl.BlockSpec((n_slots, rows, width), lambda h: (0, 0, h))


def attend(tables, qkv):
    posq, posk, cosines, sines = tables
    n_slots, rows, width = qkv.shape
    heads = width // (3 * HD)
    pairs = (n_slots * rows) ** 2 // 2 * heads
    return pl.pallas_call(
        functools.partial(attend_kernel, posk.shape[0]),
        grid=(heads,),
        in_specs=[whole_spec(t.shape) for t in tables] + [head_spec(n_slots, rows, 3 * HD)],
        out_specs=[head_spec(n_slots, rows, 3 * HD), head_spec(n_slots, rows, HD)],
        out_shape=[
            jax.ShapeDtypeStruct(qkv.shape, BF),
            jax.ShapeDtypeStruct((n_slots, rows, heads * HD), BF),
        ],
        cost_estimate=pl.CostEstimate(
            flops=4 * pairs * HD, bytes_accessed=qkv.size * 8, transcendentals=pairs
        ),
        compiler_params=pltpu.CompilerParams(vmem_limit_bytes=48 << 20),
        name="attend",
    )(posq, posk, cosines, sines, qkv)


def attend_back(tables, low, dmix):
    n_slots, rows, width = low.shape
    heads = width // (3 * HD)
    pairs = (n_slots * rows) ** 2 // 2 * heads
    return pl.pallas_call(
        functools.partial(attend_back_kernel, tables[1].shape[0]),
        grid=(heads,),
        in_specs=[whole_spec(t.shape) for t in tables]
        + [head_spec(n_slots, rows, 3 * HD), head_spec(n_slots, rows, HD)],
        out_specs=[
            head_spec(n_slots, rows, 3 * HD),
            pl.BlockSpec((1, 1, 3 * HD), lambda h: (h, 0, 0)),
        ],
        out_shape=[
            jax.ShapeDtypeStruct(low.shape, BF),
            jax.ShapeDtypeStruct((heads, 1, 3 * HD), F32),
        ],
        scratch_shapes=[pltpu.VMEM((n_slots, rows, HD), F32)] * 2,
        cost_estimate=pl.CostEstimate(
            flops=10 * pairs * HD, bytes_accessed=low.size * 5, transcendentals=pairs
        ),
        compiler_params=pltpu.CompilerParams(vmem_limit_bytes=48 << 20),
        name="attend_back",
    )(*tables, low, dmix)


def slot_rows(blocks, s):
    n = (len(blocks) + 1) // 2
    if s == 0:
        return blocks[0][...].astype(F32)
    return blocks[s][...].astype(F32) + blocks[2 * n - 1 - s][...].astype(F32)


def part_of(me_ref, s):
    return lax.rem(me_ref[0] - s + me_ref[1], me_ref[1])


def cdf_and_slope(x):
    size = jnp.abs(x)
    bell = jnp.exp(-0.5 * x * x)
    t = 1.0 / (1.0 + (0.3275911 * SQRT_HALF) * size)
    poly = ((((1.061405429 * t - 1.453152027) * t) + 1.421413741) * t - 0.284496736) * t + 0.254829592
    tail = 0.5 * poly * t * bell
    cdf = jnp.where(x >= 0, 1.0 - tail, tail)
    return cdf, cdf + x * bell * INV_ROOT_TWO_PI


def norm_qkv_kernel(n_blocks, me_ref, vectors_ref, bias_ref, *refs):
    blocks, w_hbm = refs[:n_blocks], refs[n_blocks]
    one_ref, two_ref, unit_ref, qkv_ref, w_ref, sem = refs[n_blocks + 1 :]
    n_slots, block, width = one_ref.shape
    n_qkv = w_ref.shape[1]
    first = pl.program_id(0) == 0
    copy = pltpu.make_async_copy(w_hbm.at[:, pl.ds(0, n_qkv)], w_ref, sem)

    @pl.when(first)
    def _():
        copy.start()

    for s in range(n_slots):
        rows = slot_rows(blocks, s)
        centred = rows - jnp.mean(rows, axis=-1, keepdims=True)
        unit = centred * lax.rsqrt(jnp.mean(centred * centred, axis=-1, keepdims=True) + EPSILON)
        part = part_of(me_ref, s)
        one_ref[part] = (unit * vectors_ref[0:1] + vectors_ref[1:2]).astype(BF)
        two_ref[part] = (unit * vectors_ref[2:3] + vectors_ref[3:4]).astype(BF)
        unit_ref[part] = unit.astype(BF)

    @pl.when(first)
    def _():
        copy.wait()

    one = one_ref[...].reshape(n_slots * block, width)
    tile = 768
    for c in range(0, n_qkv, tile):
        out = jnp.dot(one, w_ref[:, c : c + tile], preferred_element_type=F32)
        out = out + bias_ref[:, c : c + tile]
        qkv_ref[:, :, c : c + tile] = out.reshape(n_slots, block, tile)


def hidden_kernel(two_ref, w_ref, bias_ref, act_ref, slope_ref):
    pre = jnp.dot(two_ref[...], w_ref[...], preferred_element_type=F32) + bias_ref[...]
    cdf, slope = cdf_and_slope(pre)
    act_ref[...] = (pre * cdf).astype(BF)
    slope_ref[...] = slope.astype(BF)


def big(limit=56):
    return pltpu.CompilerParams(vmem_limit_bytes=limit << 20)


def cost(flops, moved, special=0):
    return pl.CostEstimate(flops=int(flops) // 16, bytes_accessed=int(moved) // 16, transcendentals=int(special) // 16)


def norm_qkv(chain, vectors, bias, w, n_qkv):
    n = chain.n
    rows, width = chain.x.shape
    block = 64
    me = jnp.stack([chain.me, jnp.int32(n)])
    blocks = [chain.x] + chain.left + chain.right

    def out(cols, dtype):
        return (
            jax.ShapeDtypeStruct((n, rows, cols), dtype),
            pl.BlockSpec((n, block, cols), lambda i, me: (0, i, 0)),
        )

    shapes, specs = zip(out(width, BF), out(width, BF), out(width, BF), out(n_qkv, F32))
    total = n * rows
    return pl.pallas_call(
        functools.partial(norm_qkv_kernel, len(blocks)),
        grid_spec=pltpu.PrefetchScalarGridSpec(
            num_scalar_prefetch=1,
            grid=(rows // block,),
            in_specs=[
                pl.BlockSpec(vectors.shape, lambda i, me: (0, 0)),
                pl.BlockSpec(bias.shape, lambda i, me: (0, 0)),
            ]
            + [pl.BlockSpec((block, width), lambda i, me: (i, 0))] * len(blocks)
            + [pl.BlockSpec(memory_space=pl.ANY)],
            out_specs=list(specs),
            scratch_shapes=[pltpu.VMEM((width, n_qkv), BF), pltpu.SemaphoreType.DMA],
        ),
        out_shape=list(shapes),
        cost_estimate=cost(2 * total * width * n_qkv, 10 * total * width + width * n_qkv * 2),
        compiler_params=big(),
        name="norm_qkv",
    )(me, vectors, bias, *blocks, w)


def hidden_of(two, w, bias, n_qkv):
    total, width = two.shape
    n_ff, tile = w.shape[1] - n_qkv, 256
    skip = n_qkv // tile
    columns = pl.BlockSpec((total, tile), lambda j: (0, j))
    return pl.pallas_call(
        hidden_kernel,
        grid=(n_ff // tile,),
        in_specs=[
            resident(two.shape),
            pl.BlockSpec((width, tile), lambda j: (0, j + skip)),
            pl.BlockSpec((1, tile), lambda j: (0, j + skip)),
        ],
        out_specs=[columns, columns],
        out_shape=[jax.ShapeDtypeStruct((total, n_ff), BF)] * 2,
        cost_estimate=cost(2 * total * width * n_ff, 2 * width * n_ff + 8 * total * n_ff, total * n_ff),
        compiler_params=big(),
        name="hidden",
    )(two, w, bias)


def arrange_kernel(me_ref, *refs):
    blocks, out_ref = refs[:-1], refs[-1]
    n = (len(blocks) + 1) // 2
    for s in range(n):
        part = part_of(me_ref, s)
        if s == 0:
            out_ref[part] = blocks[0][...]
        else:
            out_ref[part] = blocks[s][...] + blocks[2 * n - 1 - s][...]


def arrange(chain):
    n = chain.n
    rows, width = chain.x.shape
    block = 64
    me = jnp.stack([chain.me, jnp.int32(n)])
    blocks = [chain.x] + chain.left + chain.right
    return pl.pallas_call(
        arrange_kernel,
        grid_spec=pltpu.PrefetchScalarGridSpec(
            num_scalar_prefetch=1,
            grid=(rows // block,),
            in_specs=[pl.BlockSpec((block, width), lambda i, me: (i, 0))] * len(blocks),
            out_specs=pl.BlockSpec((n, block, width), lambda i, me: (0, i, 0)),
        ),
        out_shape=jax.ShapeDtypeStruct((n, rows, width), BF),
        cost_estimate=cost(0, 6 * n * rows * width),
        compiler_params=big(),
        name="arrange",
    )(me, *blocks)


def nt(a, b):
    return lax.dot_general(a, b, (((1,), (1,)), ((), ())), preferred_element_type=F32)


def tn(a, b):
    return lax.dot_general(a, b, (((0,), (0,)), ((), ())), preferred_element_type=F32)


def resident(shape):
    return pl.BlockSpec(shape, lambda j: (0,) * len(shape), pipeline_mode=pl.Buffered(1))


def head_rows(dense_ref, h):
    n, _, e, cols = dense_ref.shape
    return dense_ref[:, h].reshape(n * e, cols)


def branch_kernel(mixed_ref, act_ref, dense_ref, w_ref, out_ref):
    total = nt(act_ref[...], w_ref[...])
    for h in range(dense_ref.shape[1]):
        total += jnp.dot(
            mixed_ref[:, h * HD : (h + 1) * HD],
            head_rows(dense_ref, h),
            preferred_element_type=F32,
        )
    out_ref[...] = total.astype(BF)


def branch_of(mixed, act, dense, w_fc2):
    total, width, tile = act.shape[0], w_fc2.shape[0], 512
    return pl.pallas_call(
        branch_kernel,
        grid=(width // tile,),
        in_specs=[
            resident(mixed.shape),
            resident(act.shape),
            pl.BlockSpec(dense.shape[:3] + (tile,), lambda j: (0, 0, 0, j)),
            pl.BlockSpec((tile, w_fc2.shape[1]), lambda j: (j, 0)),
        ],
        out_specs=pl.BlockSpec((total, tile), lambda j: (0, j)),
        out_shape=jax.ShapeDtypeStruct((total, width), BF),
        cost_estimate=cost(2 * total * (dense.size + w_fc2.size), 2 * (act.size * 3 + w_fc2.size)),
        compiler_params=big(),
        name="branch",
    )(mixed, act, dense, w_fc2)


def back_in_kernel(g_ref, dense_ref, w_ref, slope_ref, dmix_ref, pre_ref, bias_ref):
    @pl.when(pl.program_id(0) == 0)
    def _():
        for h in range(dense_ref.shape[1]):
            dmix_ref[:, h * HD : (h + 1) * HD] = nt(g_ref[...], head_rows(dense_ref, h)).astype(BF)

    d_act = jnp.dot(g_ref[...], w_ref[...], preferred_element_type=F32)
    d_pre = (d_act * slope_ref[...].astype(F32)).astype(BF)
    pre_ref[...] = d_pre
    bias_ref[...] = jnp.sum(d_pre.astype(F32), axis=0, keepdims=True)


def back_in_of(g, dense, w_fc2, slope):
    total, width = g.shape
    n_ff, tile = w_fc2.shape[1], 512
    heads = dense.shape[1]
    columns = pl.BlockSpec((total, tile), lambda j: (0, j))
    return pl.pallas_call(
        back_in_kernel,
        grid=(n_ff // tile,),
        in_specs=[
            resident(g.shape),
            resident(dense.shape),
            pl.BlockSpec((width, tile), lambda j: (0, j)),
            columns,
        ],
        out_specs=[
            pl.BlockSpec((total, heads * HD), lambda j: (0, 0)),
            columns,
            pl.BlockSpec((1, tile), lambda j: (0, j)),
        ],
        out_shape=[
            jax.ShapeDtypeStruct((total, heads * HD), BF),
            jax.ShapeDtypeStruct((total, n_ff), BF),
            jax.ShapeDtypeStruct((1, n_ff), F32),
        ],
        cost_estimate=cost(2 * total * (dense.size + w_fc2.size), 2 * (g.size * 3 + w_fc2.size)),
        compiler_params=big(),
        name="back_in",
    )(g, dense, w_fc2, slope)


def back_out_kernel(vectors_ref, dqkv_ref, pre_ref, w_ref, unit_ref, e_ref, sums_ref):
    n_qkv = dqkv_ref.shape[1]
    one = nt(dqkv_ref[...], w_ref[:, :n_qkv])
    two = nt(pre_ref[...], w_ref[:, n_qkv:])
    unit = unit_ref[...].astype(F32)
    e_ref[...] = (one * vectors_ref[0:1] + two * vectors_ref[2:3]).astype(BF)
    sums_ref[0:1] = jnp.sum(one * unit, axis=0, keepdims=True)
    sums_ref[1:2] = jnp.sum(one, axis=0, keepdims=True)
    sums_ref[2:3] = jnp.sum(two * unit, axis=0, keepdims=True)
    sums_ref[3:4] = jnp.sum(two, axis=0, keepdims=True)


def back_out_of(vectors, dqkv, pre, w, unit):
    total, width = unit.shape
    tile = 256
    columns = pl.BlockSpec((total, tile), lambda j: (0, j))
    return pl.pallas_call(
        back_out_kernel,
        grid=(width // tile,),
        in_specs=[
            pl.BlockSpec((vectors.shape[0], tile), lambda j: (0, j)),
            resident(dqkv.shape),
            resident(pre.shape),
            pl.BlockSpec((tile, w.shape[1]), lambda j: (j, 0)),
            columns,
        ],
        out_specs=[columns, pl.BlockSpec((4, tile), lambda j: (0, j))],
        out_shape=[
            jax.ShapeDtypeStruct((total, width), BF),
            jax.ShapeDtypeStruct((4, width), F32),
        ],
        cost_estimate=cost(2 * total * w.size, 2 * (unit.size * 4 + w.size)),
        compiler_params=big(),
        name="back_out",
    )(vectors, dqkv, pre, w, unit)


def grad_kernel(count, me_ref, *refs):
    lhs, rhs, (sent_ref, kept_ref) = refs[:count], refs[count : 2 * count], refs[-2:]
    total = tn(lhs[0][...], rhs[0][...])
    for a, b in zip(lhs[1:], rhs[1:]):
        total += tn(a[...], b[...])
    step, half = pl.program_id(0), pl.num_programs(0) // 2

    @pl.when(step < half)
    def _():
        sent_ref[0] = total.astype(BF)

    @pl.when(step >= half)
    def _():
        kept_ref[0] = total.astype(BF)


def grad_of(parity, lhs, rhs, cuts, name):
    total, m = lhs[0].shape
    n, tile, half = rhs[0].shape[1], m // cuts, cuts // 2
    shape = jax.ShapeDtypeStruct((half, tile, n), BF)

    def left(j, me):
        return (0, jnp.where(j < half, 2 * j + 1 - me[0], 2 * (j - half) + me[0]))

    return pl.pallas_call(
        functools.partial(grad_kernel, len(lhs)),
        grid_spec=pltpu.PrefetchScalarGridSpec(
            num_scalar_prefetch=1,
            grid=(cuts,),
            in_specs=[pl.BlockSpec((total, tile), left)] * len(lhs)
            + [
                pl.BlockSpec(r.shape, lambda j, me: (0, 0), pipeline_mode=pl.Buffered(1))
                for r in rhs
            ],
            out_specs=[
                pl.BlockSpec((1, tile, n), lambda j, me: (jnp.minimum(j, half - 1), 0, 0)),
                pl.BlockSpec((1, tile, n), lambda j, me: (jnp.maximum(j - half, 0), 0, 0)),
            ],
        ),
        out_shape=[shape, shape],
        cost_estimate=cost(2 * len(lhs) * total * m * n, 4 * total * (m + n) + 2 * m * n),
        compiler_params=big(),
        name=name,
    )(parity, *lhs, *rhs)


def head_grad_kernel(count, me_ref, *refs):
    lhs, rhs, (sent_ref, kept_ref) = refs[:count], refs[count : 2 * count], refs[-2:]
    total = tn(lhs[0][...], rhs[0][...])
    for a, b in zip(lhs[1:], rhs[1:]):
        total += tn(a[...], b[...])
    half, _, e, n = sent_ref.shape
    total = total.astype(BF).reshape(half, 2, e, n)
    even = me_ref[0] == 0
    kept_ref[:, 0] = jnp.where(even, total[:, 0], total[:, 1])
    sent_ref[:, 0] = jnp.where(even, total[:, 1], total[:, 0])


def head_grad_of(parity, lhs, rhs, cuts, name):
    total, m = lhs[0].shape
    n, e = rhs[0].shape[1], HD // cuts
    shape = jax.ShapeDtypeStruct((cuts // 2, m // HD, e, n), BF)
    return pl.pallas_call(
        functools.partial(head_grad_kernel, len(lhs)),
        grid_spec=pltpu.PrefetchScalarGridSpec(
            num_scalar_prefetch=1,
            grid=(m // HD,),
            in_specs=[pl.BlockSpec((total, HD), lambda j, me: (0, j))] * len(lhs)
            + [
                pl.BlockSpec(r.shape, lambda j, me: (0, 0), pipeline_mode=pl.Buffered(1))
                for r in rhs
            ],
            out_specs=[pl.BlockSpec((cuts // 2, 1, e, n), lambda j, me: (0, j, 0, 0))] * 2,
        ),
        out_shape=[shape, shape],
        cost_estimate=cost(2 * len(lhs) * total * m * n, 4 * total * (m + n) + 2 * m * n),
        compiler_params=big(),
        name=name,
    )(parity, *lhs, *rhs)


def unit_of(rows):
    centred = rows - jnp.mean(rows, axis=-1, keepdims=True)
    scaling = lax.rsqrt(jnp.mean(centred * centred, axis=-1, keepdims=True) + EPSILON)
    return centred * scaling, scaling


def per_device(
    hidden_in,
    lengths,
    dealing,
    cotangent,
    attn_gain,
    attn_shift,
    ffn_gain,
    ffn_shift,
    qkv_weight,
    qkv_bias,
    dense_weight,
    dense_bias,
    fc1_weight,
    fc1_bias,
    fc2_weight,
    fc2_bias,
):
    n_t, n_d = lax.axis_size("tensor"), lax.axis_size("dp")
    my_t, my_d = lax.axis_index("tensor"), lax.axis_index("dp")
    micros, seqs, piece, width = hidden_in.shape
    heads = qkv_weight.shape[1]
    rows = n_d * piece
    n_blocks = 4

    def deal(x):
        return lax.all_to_all(x, "dp", split_axis=0, concat_axis=0, tiled=True).reshape(rows, width)

    def undeal(x):
        return lax.all_to_all(
            x.reshape(seqs, piece, width), "dp", split_axis=0, concat_axis=0, tiled=True
        )

    env = {}

    def stage(chains, computes=()):
        for chain in chains:
            chain.step()
        for fn in computes:
            fn()
        keys = list(env)
        values = [env[k] for k in keys]
        for chain in chains:
            values += chain.live()
        out = list(lax.optimization_barrier(tuple(values)))
        env.update(zip(keys, out))
        at = len(keys)
        for chain in chains:
            count = len(chain.live())
            chain.set_live(out[at : at + count])
            at += count

    def after(x):
        return lax.optimization_barrier((x, env["mark"]))[0]

    eighth = width // (n_d * n_t)
    n_six = 6 * n_t * eighth
    env["x0"] = deal(hidden_in[0])
    env["mark"] = jnp.concatenate(
        [attn_gain, attn_shift, ffn_gain, ffn_shift, dense_bias, fc2_bias]
    )
    stage([])

    n_qkv = heads * 3 * HD
    near = jnp.concatenate([after(qkv_weight).reshape(-1, n_qkv), after(fc1_weight)], axis=1)
    w_near = lax.all_gather(near, "dp", axis=0, tiled=True)

    parts = jnp.arange(n_t, dtype=jnp.int32)
    local = jnp.arange(rows, dtype=jnp.int32)
    positions = ((local // piece) * n_t + parts[:, None]) * piece + local % piece
    freqs = jnp.exp(jnp.arange(ROT // 2, dtype=F32) * (-2.0 * math.log(ROPE_BASE) / ROT))
    phases = positions.astype(F32)[..., None] * freqs
    flat = jnp.zeros((n_t, rows, 128 - ROT), F32)
    cosines = jnp.concatenate([jnp.cos(phases), jnp.cos(phases), flat + 1.0], axis=-1)
    sines = jnp.concatenate([-jnp.sin(phases), jnp.sin(phases), flat], axis=-1)
    picked = dealing == my_d
    seq_lens = jnp.sum(jnp.where(picked, lengths, 0), axis=1)
    posq = positions[..., None]

    def tables(m):
        keyed = jnp.where(positions < seq_lens[m], positions, FAR)
        span = rows // n_blocks
        lists = []
        for b in range(n_blocks):
            seen = keyed[:, : span * (b + 1)].reshape(1, -1)
            lists.append(jnp.pad(seen, ((0, 0), (0, n_t * rows - seen.shape[1]))))
        return (posq, jnp.stack(lists), cosines, sines)

    all_tables = [tables(m) for m in range(micros)]
    sum_g = jnp.sum(cotangent.astype(F32), axis=(0, 1, 2))

    chains = {"x0": GatherChain(env["x0"], "tensor", n_t)}
    pending = {}

    def join(*keys):
        def fn():
            for key in keys:
                env[key] = pending.pop(key)

        return fn

    def vectors_over_tensor():
        vectors = direct_gather(env["mark"], "tensor", n_t)
        env["six"] = jnp.concatenate(
            [vectors.reshape(-1), qkv_bias.reshape(-1), fc1_bias.reshape(-1)]
        )

    def vectors_over_dp():
        env["six"] = direct_gather(env["six"], "dp", n_d)

    def deal_x1():
        pending["x1"] = deal(after(hidden_in[1]))

    last = n_t - 2

    def at(i, *plan):
        if i < last:
            return list(plan[i]) if i < len(plan) else []
        return [fn for entry in plan[i:] for fn in entry]

    for i in range(n_t - 1):
        stage(
            [chains["x0"]],
            at(i, [vectors_over_tensor, deal_x1], [vectors_over_dp, join("x1")]),
        )
    w_fc2 = lax.all_gather(after(fc2_weight.T), "dp", axis=0, tiled=True)
    w_dense = lax.all_gather(after(dense_weight), "dp", axis=0, tiled=False)
    own_x = [env.pop("x0"), env.pop("x1")]
    six = env.pop("six")
    vectors = six[:, :n_six].reshape(n_d, n_t, 6, eighth).transpose(2, 0, 1, 3)
    vectors = vectors.reshape(6, width).astype(F32)
    out_shift = vectors[4] + vectors[5]
    rest = six[:, n_six:].astype(F32)
    n_qb = qkv_bias.size
    bias = jnp.concatenate(
        [
            rest[:, :n_qb].reshape(n_d, heads, -1).transpose(1, 0, 2).reshape(1, -1),
            rest[:, n_qb:].reshape(n_d, heads, -1).transpose(1, 0, 2).reshape(1, -1),
        ],
        axis=1,
    )
    env["mark"], env["bias"] = vectors, bias

    def norm_qkv_of(m):
        def fn():
            outs = norm_qkv(chains[f"x{m}"], env["mark"], env["bias"], w_near, n_qkv)
            for key, value in zip(("one", "two", "unit", "qkv"), outs):
                env[f"{key}{m}"] = value if key == "qkv" else value.reshape(n_t * rows, -1)

        return fn

    def hidden(m):
        def fn():
            env[f"act{m}"], env[f"slope{m}"] = hidden_of(
                env[f"two{m}"], w_near, env["bias"], n_qkv
            )

        return fn

    def attend_of(m):
        def fn():
            low, mixed = attend(all_tables[m], env.pop(f"qkv{m}"))
            env[f"low{m}"], env[f"mixed{m}"] = low, mixed.reshape(n_t * rows, -1)

        return fn

    def branch(m):
        def fn():
            parts = branch_of(env[f"mixed{m}"], env[f"act{m}"], w_dense, w_fc2)
            env[f"branch{m}"] = parts

        return fn

    def scattered_rows(name):
        return lax.psum_scatter(env.pop(name), "tensor", scatter_dimension=0, tiled=True)

    def output_of(m):
        def fn():
            total = env.pop(f"so{m}").astype(F32)
            out = (own_x[m].astype(F32) + total + out_shift).astype(BF)
            env[f"output{m}"] = undeal(out)

        return fn

    def arrange_g(m):
        def fn():
            env[f"g{m}"] = arrange(chains[f"g{m}"]).reshape(n_t * rows, width)

        return fn

    def back_in(m):
        def fn():
            if f"g{m}" not in env:
                arrange_g(m)()
            dmix, env[f"pre{m}"], env[f"b1{m}"] = back_in_of(
                env[f"g{m}"], w_dense, w_fc2, env.pop(f"slope{m}")
            )
            env[f"dmix{m}"] = dmix.reshape(n_t, rows, -1)

        return fn

    def back_attend(m):
        def fn():
            d_qkv, env[f"bq{m}"] = attend_back(
                all_tables[m], env.pop(f"low{m}"), env.pop(f"dmix{m}")
            )
            env[f"dqkv{m}"] = d_qkv.reshape(n_t * rows, -1)

        return fn

    def back_out(m):
        def fn():
            env[f"e{m}"], env[f"sums{m}"] = back_out_of(
                env["mark"], env[f"dqkv{m}"], env[f"pre{m}"], w_near, env.pop(f"unit{m}")
            )

        return fn

    def input_of(m):
        def fn():
            total = env.pop(f"si{m}").astype(F32)
            unit, scaling = unit_of(own_x[m].astype(F32))
            back = scaling * (
                total
                - jnp.mean(total, axis=-1, keepdims=True)
                - unit * jnp.mean(total * unit, axis=-1, keepdims=True)
            )
            env[f"input{m}"] = undeal((own_g[m].astype(F32) + back).astype(BF))

        return fn

    def pair(key):
        return [env[f"{key}{m}"] for m in range(micros)]

    parity = (my_d % 2)[None]
    swap = [(i, i ^ 1) for i in range(n_d)]
    same_parity = [list(range(p, n_d, 2)) for p in range(2)]

    def fc2_grads():
        env["w2_sent"], env["w2_kept"] = grad_of(parity, pair("g"), pair("act"), n_d, "grad_fc2")

    def dense_grads():
        halves = head_grad_of(parity, pair("mixed"), pair("g"), n_d, "grad_dense")
        env["wd_sent"], env["wd_kept"] = (h.reshape(n_d // 2, -1, width) for h in halves)

    def fc1_grads():
        env["w1_sent"], env["w1_kept"] = grad_of(parity, pair("two"), pair("pre"), n_d, "grad_fc1")

    def qkv_grads():
        env["wq_sent"], env["wq_kept"] = grad_of(parity, pair("one"), pair("dqkv"), n_d, "grad_qkv")

    def swapped(key):
        def fn():
            env[f"{key}_got"] = lax.ppermute(env.pop(f"{key}_sent"), "dp", swap)

        return fn

    def spread(key):
        both_cores = env.pop(f"{key}_kept").astype(F32) + env.pop(f"{key}_got").astype(F32)
        return lax.all_to_all(
            both_cores.astype(BF),
            "dp",
            split_axis=0,
            concat_axis=0,
            axis_index_groups=same_parity,
            tiled=True,
        )

    def both(*fns):
        def fn():
            for each in fns:
                each()

        return fn

    def summed(key):
        return jnp.sum(env.pop(key).astype(F32), axis=0)

    def fc2_final():
        env["grad_fc2"] = summed("w2").T

    def fc1_final():
        env["grad_fc1"] = summed("w1")

    def qkv_final():
        env["grad_qkv"] = summed("wq").reshape(-1, heads, 3 * HD)

    def dense_final():
        env["grad_dense"] = summed("wd").reshape(heads, -1, width)

    def gather_chain(name, x):
        chains[name] = GatherChain(after(x), "tensor", n_t)
        return chains[name]

    def deal_g():
        pending["g"] = lax.all_to_all(after(cotangent), "dp", split_axis=1, concat_axis=1, tiled=True)

    def spread_later(*keys):
        for key in keys:
            pending[key] = spread(key)

    def steps_of(chain, *plan):
        for i in range(chain.steps()):
            stage([chain], at(i, *plan))

    steps_of(
        gather_chain("x1", own_x[1]), [norm_qkv_of(0)], [attend_of(0), hidden(0), deal_g], [join("g")]
    )
    own_g = list(env.pop("g").reshape(micros, rows, width))
    steps_of(
        gather_chain("g0", own_g[0]), [branch(0)], [norm_qkv_of(1)], [attend_of(1), hidden(1)]
    )
    pending["so0"] = scattered_rows("branch0")
    steps_of(
        gather_chain("g1", own_g[1]),
        [branch(1), arrange_g(0)],
        [back_in(0), back_attend(0)],
        [back_out(0), join("so0")],
    )
    pending["so1"] = scattered_rows("branch1")
    pending["si0"] = scattered_rows("e0")
    stage([], [arrange_g(1), fc2_grads, swapped("w2"), back_in(1), output_of(0)])
    spread_later("w2")
    stage([], [fc1_grads, swapped("w1"), back_attend(1), back_out(1), join("w2", "so1")])
    pending["si1"] = scattered_rows("e1")
    spread_later("w1")
    sums = jnp.concatenate([env["sums0"] + env["sums1"], sum_g[None]], axis=0)
    sums = sums.reshape(5, n_d, n_t, eighth).transpose(1, 2, 0, 3).reshape(n_d, -1)
    qkvb = (env["bq0"] + env["bq1"]).reshape(heads, n_d, -1).transpose(1, 0, 2).reshape(n_d, -1)
    fc1b = (env["b10"] + env["b11"]).reshape(heads, n_d, -1).transpose(1, 0, 2).reshape(n_d, -1)
    small = SmallScatter(jnp.concatenate([sums, qkvb, fc1b], axis=1), "dp", n_d)
    stage([small], [qkv_grads, swapped("wq"), dense_grads, swapped("wd"), fc2_final, join("w1")])
    spread_later("wq")
    stage([small], [output_of(1), fc1_final, join("wq")])
    spread_later("wd")
    stage([small], [qkv_final, join("wd", "si0")])
    while small.bit:
        stage([small])
    small_out = small.out[0]
    n_sum = 5 * n_t * eighth
    env["mine"] = direct_scatter(small_out[:n_sum].reshape(n_t, 5 * eighth), "tensor", n_t)
    stage([], [input_of(0), dense_final, join("si1")])
    input_of(1)()

    outputs = pair("output")
    grads_in = pair("input")

    small = small_out
    mine = env["mine"].reshape(5, eighth)
    qkvb = small[n_sum : n_sum + n_qb].reshape(heads, -1)
    fc1b = small[n_sum + n_qb :].reshape(heads, -1)

    return (
        jnp.stack(outputs),
        jnp.stack(grads_in),
        mine[0],
        mine[1],
        mine[2],
        mine[3],
        env["grad_qkv"],
        qkvb,
        env["grad_dense"],
        mine[4],
        env["grad_fc1"],
        fc1b,
        env["grad_fc2"],
        mine[4],
    )


def solution(mesh):
    rows = P(None, None, ("dp", "tensor"), None)
    vector = P(("dp", "tensor"))
    return jax.shard_map(
        per_device,
        mesh=mesh,
        in_specs=(
            rows,
            P(),
            P(),
            rows,
            vector,
            vector,
            vector,
            vector,
            P("dp", "tensor", None),
            P("tensor", "dp"),
            P("tensor", "dp", None),
            vector,
            P("dp", "tensor"),
            P("tensor", "dp"),
            P("tensor", "dp"),
            vector,
        ),
        out_specs=(
            rows,
            rows,
            vector,
            vector,
            vector,
            vector,
            P("dp", "tensor", None),
            P("tensor", "dp"),
            P("tensor", "dp", None),
            vector,
            P("dp", "tensor"),
            P("tensor", "dp"),
            P("tensor", "dp"),
            vector,
        ),
        check_vma=False,
    )
```

```python
import functools
import math

import jax
import jax.numpy as jnp
from jax import lax
from jax.experimental import pallas as pl
from jax.experimental.pallas import tpu as pltpu
from jax.sharding import PartitionSpec as P

HD = 256
ROT = 64
EPSILON = 1e-05
ROPE_BASE = 10000.0
NEG_FILL = -1e30
SQRT_HALF = 0.7071067811865476
INV_ROOT_TWO_PI = 0.3989422804014327
BF = jnp.bfloat16
F32 = jnp.float32
FAR = 1 << 20
SHARE = 4096


class GatherChain:
    def __init__(self, x, axis, n):
        self.x, self.axis, self.n, self.step_no = x, axis, n, 0
        self.me = lax.axis_index(axis)
        self.left, self.right = [], []

    def steps(self):
        return self.n - 1

    def step(self):
        n = self.n
        s = self.step_no = self.step_no + 1
        to_right = self.left[-1] if self.left else self.x
        to_left = self.right[-1] if self.right else self.x
        pairs = [(k, k + 1) for k in range(s - 1, n - 1)]
        self.left.append(lax.ppermute(to_right, self.axis, pairs))
        pairs = [(k, k - 1) for k in range(1, n - s + 1)]
        self.right.append(lax.ppermute(to_left, self.axis, pairs))

    def live(self):
        return [self.left[-1], self.right[-1]]

    def set_live(self, values):
        self.left[-1], self.right[-1] = values


def shifts(n):
    return [[(k, (k + s) % n) for k in range(n)] for s in range(1, n)]


def direct_gather(x, axis, n):
    me = lax.axis_index(axis)
    got = jnp.stack([x] + [lax.ppermute(x, axis, pairs) for pairs in shifts(n)])
    order = (me - jnp.arange(n)) % n
    chosen = order[None, :] == jnp.arange(n)[:, None]
    return jnp.sum(jnp.where(chosen[:, :, None], got[None], 0), axis=1).astype(x.dtype)


def direct_scatter(x, axis, n):
    me = lax.axis_index(axis)
    total = lax.dynamic_index_in_dim(x, me, 0, keepdims=False)
    for s, pairs in enumerate(shifts(n), 1):
        sent = lax.dynamic_index_in_dim(x, (me + s) % n, 0, keepdims=False)
        total = total + lax.ppermute(sent, axis, pairs)
    return total


def rotated(x, cosines, sines):
    lanes = lax.broadcasted_iota(jnp.int32, x.shape, 1)
    partner = jnp.where(lanes < ROT // 2, pltpu.roll(x, 128 - ROT // 2, 1), pltpu.roll(x, ROT // 2, 1))
    return x * cosines + partner * sines


def scores_of(q, k, posq, posk):
    s = lax.dot_general(q, k, (((1,), (1,)), ((), ())), preferred_element_type=F32)
    return jnp.where(posk <= posq, s * (1.0 / math.sqrt(HD)), NEG_FILL)


def attend_kernel(n_blocks, posq_ref, posk_ref, cos_ref, sin_ref, qkv_ref, low_ref, mixed_ref):
    n_slots, rows, _ = qkv_ref.shape
    span = rows // n_blocks
    for t in range(n_slots):
        for base in (0, HD):
            lead = rotated(qkv_ref[t, :, base : base + 128], cos_ref[t], sin_ref[t])
            low_ref[t, :, base : base + 128] = lead.astype(BF)
            low_ref[t, :, base + 128 : base + HD] = qkv_ref[t, :, base + 128 : base + HD].astype(BF)
        low_ref[t, :, 2 * HD :] = qkv_ref[t, :, 2 * HD :].astype(BF)
    for b in range(n_blocks):
        own, seen = pl.ds(b * span, span), span * (b + 1)
        n_q, n_k = n_slots * span, n_slots * seen
        q = low_ref[:, own, :HD].reshape(n_q, HD)
        k = low_ref[:, :seen, HD : 2 * HD].reshape(n_k, HD)
        v = low_ref[:, :seen, 2 * HD :].reshape(n_k, HD)
        posq = posq_ref[:, own, :].reshape(n_q, 1)
        s = scores_of(q, k, posq, posk_ref[b, :, :n_k])
        e = jnp.exp(s - jnp.max(s, axis=-1, keepdims=True))
        p = e * (1.0 / jnp.sum(e, axis=-1, keepdims=True))
        mixed = jnp.dot(p.astype(BF), v, preferred_element_type=F32)
        mixed_ref[:, own, :] = mixed.astype(BF).reshape(n_slots, span, HD)


def attend_back_kernel(
    n_blocks,
    posq_ref,
    posk_ref,
    cos_ref,
    sin_ref,
    low_ref,
    dmix_ref,
    grad_ref,
    bias_ref,
    dk_ref,
    dv_ref,
):
    n_slots, rows, _ = low_ref.shape
    span = rows // n_blocks
    scale = 1.0 / math.sqrt(HD)
    for b in reversed(range(n_blocks)):
        own, seen = pl.ds(b * span, span), span * (b + 1)
        n_q, n_k = n_slots * span, n_slots * seen
        q = low_ref[:, own, :HD].reshape(n_q, HD)
        k = low_ref[:, :seen, HD : 2 * HD].reshape(n_k, HD)
        v = low_ref[:, :seen, 2 * HD :].reshape(n_k, HD)
        dmix = dmix_ref[:, own, :].reshape(n_q, HD)
        posq = posq_ref[:, own, :].reshape(n_q, 1)
        s = scores_of(q, k, posq, posk_ref[b, :, :n_k])
        e = jnp.exp(s - jnp.max(s, axis=-1, keepdims=True))
        p = e * (1.0 / jnp.sum(e, axis=-1, keepdims=True))
        dp = lax.dot_general(dmix, v, (((1,), (1,)), ((), ())), preferred_element_type=F32)
        ds = (p * (dp - jnp.sum(p * dp, axis=-1, keepdims=True))).astype(BF)
        dq = jnp.dot(ds, k, preferred_element_type=F32) * scale
        dk = lax.dot_general(ds, q, (((0,), (0,)), ((), ())), preferred_element_type=F32)
        dv = lax.dot_general(p.astype(BF), dmix, (((0,), (0,)), ((), ())), preferred_element_type=F32)
        dk, dv = dk.reshape(n_slots, seen, HD), dv.reshape(n_slots, seen, HD)
        if b == n_blocks - 1:
            dk_ref[...] = dk
            dv_ref[...] = dv
        else:
            dk_ref[:, :seen, :] += dk
            dv_ref[:, :seen, :] += dv
        dq = dq.reshape(n_slots, span, HD)
        for t in range(n_slots):
            lead = rotated(dq[t, :, :128], cos_ref[t, own, :], -sin_ref[t, own, :])
            grad_ref[t, own, :128] = lead.astype(BF)
            grad_ref[t, own, 128:HD] = dq[t, :, 128:].astype(BF)
    for t in range(n_slots):
        lead = rotated(dk_ref[t, :, :128] * scale, cos_ref[t], -sin_ref[t])
        grad_ref[t, :, HD : HD + 128] = lead.astype(BF)
        grad_ref[t, :, HD + 128 : 2 * HD] = (dk_ref[t, :, 128:] * scale).astype(BF)
        grad_ref[t, :, 2 * HD :] = dv_ref[t].astype(BF)
        summed = jnp.sum(grad_ref[t].astype(F32), axis=0, keepdims=True)
        bias_ref[0] = summed if t == 0 else bias_ref[0] + summed


def whole_spec(shape):
    return pl.BlockSpec(shape, lambda h: (0,) * len(shape))


def head_spec(n_slots, rows, width):
    return pl.BlockSpec((n_slots, rows, width), lambda h: (0, 0, h))


def attend(tables, qkv):
    posq, posk, cosines, sines = tables
    n_slots, rows, width = qkv.shape
    heads = width // (3 * HD)
    pairs = (n_slots * rows) ** 2 // 2 * heads
    return pl.pallas_call(
        functools.partial(attend_kernel, posk.shape[0]),
        grid=(heads,),
        in_specs=[whole_spec(t.shape) for t in tables] + [head_spec(n_slots, rows, 3 * HD)],
        out_specs=[head_spec(n_slots, rows, 3 * HD), head_spec(n_slots, rows, HD)],
        out_shape=[
            jax.ShapeDtypeStruct(qkv.shape, BF),
            jax.ShapeDtypeStruct((n_slots, rows, heads * HD), BF),
        ],
        cost_estimate=pl.CostEstimate(
            flops=4 * pairs * HD, bytes_accessed=qkv.size * 8, transcendentals=pairs
        ),
        compiler_params=pltpu.CompilerParams(vmem_limit_bytes=48 << 20),
        name="attend",
    )(posq, posk, cosines, sines, qkv)


def attend_back(tables, low, dmix):
    n_slots, rows, width = low.shape
    heads = width // (3 * HD)
    pairs = (n_slots * rows) ** 2 // 2 * heads
    return pl.pallas_call(
        functools.partial(attend_back_kernel, tables[1].shape[0]),
        grid=(heads,),
        in_specs=[whole_spec(t.shape) for t in tables]
        + [head_spec(n_slots, rows, 3 * HD), head_spec(n_slots, rows, HD)],
        out_specs=[
            head_spec(n_slots, rows, 3 * HD),
            pl.BlockSpec((1, 1, 3 * HD), lambda h: (h, 0, 0)),
        ],
        out_shape=[
            jax.ShapeDtypeStruct(low.shape, BF),
            jax.ShapeDtypeStruct((heads, 1, 3 * HD), F32),
        ],
        scratch_shapes=[pltpu.VMEM((n_slots, rows, HD), F32)] * 2,
        cost_estimate=pl.CostEstimate(
            flops=10 * pairs * HD, bytes_accessed=low.size * 5, transcendentals=pairs
        ),
        compiler_params=pltpu.CompilerParams(vmem_limit_bytes=48 << 20),
        name="attend_back",
    )(*tables, low, dmix)


def slot_rows(blocks, s):
    n = (len(blocks) + 1) // 2
    if s == 0:
        return blocks[0][...].astype(F32)
    return blocks[s][...].astype(F32) + blocks[2 * n - 1 - s][...].astype(F32)


def part_of(me_ref, s):
    return lax.rem(me_ref[0] - s + me_ref[1], me_ref[1])


def cdf_and_slope(x):
    size = jnp.abs(x)
    bell = jnp.exp(-0.5 * x * x)
    t = 1.0 / (1.0 + (0.3275911 * SQRT_HALF) * size)
    poly = ((((1.061405429 * t - 1.453152027) * t) + 1.421413741) * t - 0.284496736) * t + 0.254829592
    tail = 0.5 * poly * t * bell
    cdf = jnp.where(x >= 0, 1.0 - tail, tail)
    return cdf, cdf + x * bell * INV_ROOT_TWO_PI


def norm_qkv_kernel(n_blocks, me_ref, vectors_ref, bias_ref, *refs):
    blocks, w_hbm = refs[:n_blocks], refs[n_blocks]
    one_ref, two_ref, unit_ref, qkv_ref, w_ref, sem = refs[n_blocks + 1 :]
    n_slots, block, width = one_ref.shape
    n_qkv = w_ref.shape[1]
    first = pl.program_id(0) == 0
    copy = pltpu.make_async_copy(w_hbm.at[:, pl.ds(0, n_qkv)], w_ref, sem)

    @pl.when(first)
    def _():
        copy.start()

    for s in range(n_slots):
        rows = slot_rows(blocks, s)
        centred = rows - jnp.mean(rows, axis=-1, keepdims=True)
        unit = centred * lax.rsqrt(jnp.mean(centred * centred, axis=-1, keepdims=True) + EPSILON)
        part = part_of(me_ref, s)
        one_ref[part] = (unit * vectors_ref[0:1] + vectors_ref[1:2]).astype(BF)
        two_ref[part] = (unit * vectors_ref[2:3] + vectors_ref[3:4]).astype(BF)
        unit_ref[part] = unit.astype(BF)

    @pl.when(first)
    def _():
        copy.wait()

    one = one_ref[...].reshape(n_slots * block, width)
    tile = 768
    for c in range(0, n_qkv, tile):
        out = jnp.dot(one, w_ref[:, c : c + tile], preferred_element_type=F32)
        out = out + bias_ref[:, c : c + tile]
        qkv_ref[:, :, c : c + tile] = out.reshape(n_slots, block, tile)


def hidden_kernel(two_ref, w_ref, bias_ref, act_ref, slope_ref):
    pre = jnp.dot(two_ref[...], w_ref[...], preferred_element_type=F32) + bias_ref[...]
    cdf, slope = cdf_and_slope(pre)
    act_ref[...] = (pre * cdf).astype(BF)
    slope_ref[...] = slope.astype(BF)


def big(limit=56):
    return pltpu.CompilerParams(vmem_limit_bytes=limit << 20)


def cost(flops, moved, special=0):
    return pl.CostEstimate(
        flops=int(flops) // SHARE,
        bytes_accessed=int(moved) // SHARE,
        transcendentals=int(special) // SHARE,
    )


def norm_qkv(chain, vectors, bias, w, n_qkv):
    n = chain.n
    rows, width = chain.x.shape
    block = 64
    me = jnp.stack([chain.me, jnp.int32(n)])
    blocks = [chain.x] + chain.left + chain.right

    def out(cols, dtype):
        return (
            jax.ShapeDtypeStruct((n, rows, cols), dtype),
            pl.BlockSpec((n, block, cols), lambda i, me: (0, i, 0)),
        )

    shapes, specs = zip(out(width, BF), out(width, BF), out(width, BF), out(n_qkv, F32))
    total = n * rows
    return pl.pallas_call(
        functools.partial(norm_qkv_kernel, len(blocks)),
        grid_spec=pltpu.PrefetchScalarGridSpec(
            num_scalar_prefetch=1,
            grid=(rows // block,),
            in_specs=[
                pl.BlockSpec(vectors.shape, lambda i, me: (0, 0)),
                pl.BlockSpec(bias.shape, lambda i, me: (0, 0)),
            ]
            + [pl.BlockSpec((block, width), lambda i, me: (i, 0))] * len(blocks)
            + [pl.BlockSpec(memory_space=pl.ANY)],
            out_specs=list(specs),
            scratch_shapes=[pltpu.VMEM((width, n_qkv), BF), pltpu.SemaphoreType.DMA],
        ),
        out_shape=list(shapes),
        cost_estimate=cost(2 * total * width * n_qkv, 10 * total * width + width * n_qkv * 2),
        compiler_params=big(),
        name="norm_qkv",
    )(me, vectors, bias, *blocks, w)


def hidden_of(two, w, bias, n_qkv):
    total, width = two.shape
    n_ff, tile = w.shape[1] - n_qkv, 256
    skip = n_qkv // tile
    columns = pl.BlockSpec((total, tile), lambda j: (0, j))
    return pl.pallas_call(
        hidden_kernel,
        grid=(n_ff // tile,),
        in_specs=[
            resident(two.shape),
            pl.BlockSpec((width, tile), lambda j: (0, j + skip)),
            pl.BlockSpec((1, tile), lambda j: (0, j + skip)),
        ],
        out_specs=[columns, columns],
        out_shape=[jax.ShapeDtypeStruct((total, n_ff), BF)] * 2,
        cost_estimate=cost(2 * total * width * n_ff, 2 * width * n_ff + 8 * total * n_ff, total * n_ff),
        compiler_params=big(),
        name="hidden",
    )(two, w, bias)


def arrange_kernel(me_ref, *refs):
    blocks, out_ref = refs[:-1], refs[-1]
    n = (len(blocks) + 1) // 2
    for s in range(n):
        part = part_of(me_ref, s)
        if s == 0:
            out_ref[part] = blocks[0][...]
        else:
            out_ref[part] = blocks[s][...] + blocks[2 * n - 1 - s][...]


def arrange(chain):
    n = chain.n
    rows, width = chain.x.shape
    block = 64
    me = jnp.stack([chain.me, jnp.int32(n)])
    blocks = [chain.x] + chain.left + chain.right
    return pl.pallas_call(
        arrange_kernel,
        grid_spec=pltpu.PrefetchScalarGridSpec(
            num_scalar_prefetch=1,
            grid=(rows // block,),
            in_specs=[pl.BlockSpec((block, width), lambda i, me: (i, 0))] * len(blocks),
            out_specs=pl.BlockSpec((n, block, width), lambda i, me: (0, i, 0)),
        ),
        out_shape=jax.ShapeDtypeStruct((n, rows, width), BF),
        cost_estimate=cost(0, 6 * n * rows * width),
        compiler_params=big(),
        name="arrange",
    )(me, *blocks)


def nt(a, b):
    return lax.dot_general(a, b, (((1,), (1,)), ((), ())), preferred_element_type=F32)


def tn(a, b):
    return lax.dot_general(a, b, (((0,), (0,)), ((), ())), preferred_element_type=F32)


def resident(shape):
    return pl.BlockSpec(shape, lambda j: (0,) * len(shape), pipeline_mode=pl.Buffered(1))


def head_rows(dense_ref, h):
    n, _, e, cols = dense_ref.shape
    return dense_ref[:, h].reshape(n * e, cols)


def branch_kernel(mixed_ref, act_ref, dense_ref, w_ref, out_ref):
    total = nt(act_ref[...], w_ref[...])
    for h in range(dense_ref.shape[1]):
        total += jnp.dot(
            mixed_ref[:, h * HD : (h + 1) * HD],
            head_rows(dense_ref, h),
            preferred_element_type=F32,
        )
    out_ref[...] = total.astype(BF)


def branch_of(mixed, act, dense, w_fc2):
    total, width, tile = act.shape[0], w_fc2.shape[0], 512
    return pl.pallas_call(
        branch_kernel,
        grid=(width // tile,),
        in_specs=[
            resident(mixed.shape),
            resident(act.shape),
            pl.BlockSpec(dense.shape[:3] + (tile,), lambda j: (0, 0, 0, j)),
            pl.BlockSpec((tile, w_fc2.shape[1]), lambda j: (j, 0)),
        ],
        out_specs=pl.BlockSpec((total, tile), lambda j: (0, j)),
        out_shape=jax.ShapeDtypeStruct((total, width), BF),
        cost_estimate=cost(2 * total * (dense.size + w_fc2.size), 2 * (act.size * 3 + w_fc2.size)),
        compiler_params=big(),
        name="branch",
    )(mixed, act, dense, w_fc2)


def back_in_kernel(g_ref, dense_ref, w_ref, slope_ref, dmix_ref, pre_ref, bias_ref):
    @pl.when(pl.program_id(0) == 0)
    def _():
        for h in range(dense_ref.shape[1]):
            dmix_ref[:, h * HD : (h + 1) * HD] = nt(g_ref[...], head_rows(dense_ref, h)).astype(BF)

    d_act = jnp.dot(g_ref[...], w_ref[...], preferred_element_type=F32)
    d_pre = (d_act * slope_ref[...].astype(F32)).astype(BF)
    pre_ref[...] = d_pre
    bias_ref[...] = jnp.sum(d_pre.astype(F32), axis=0, keepdims=True)


def back_in_of(g, dense, w_fc2, slope):
    total, width = g.shape
    n_ff, tile = w_fc2.shape[1], 512
    heads = dense.shape[1]
    columns = pl.BlockSpec((total, tile), lambda j: (0, j))
    return pl.pallas_call(
        back_in_kernel,
        grid=(n_ff // tile,),
        in_specs=[
            resident(g.shape),
            resident(dense.shape),
            pl.BlockSpec((width, tile), lambda j: (0, j)),
            columns,
        ],
        out_specs=[
            pl.BlockSpec((total, heads * HD), lambda j: (0, 0)),
            columns,
            pl.BlockSpec((1, tile), lambda j: (0, j)),
        ],
        out_shape=[
            jax.ShapeDtypeStruct((total, heads * HD), BF),
            jax.ShapeDtypeStruct((total, n_ff), BF),
            jax.ShapeDtypeStruct((1, n_ff), F32),
        ],
        cost_estimate=cost(2 * total * (dense.size + w_fc2.size), 2 * (g.size * 3 + w_fc2.size)),
        compiler_params=big(),
        name="back_in",
    )(g, dense, w_fc2, slope)


def back_out_kernel(vectors_ref, dqkv_ref, pre_ref, w_ref, unit_ref, e_ref, sums_ref):
    n_qkv = dqkv_ref.shape[1]
    one = nt(dqkv_ref[...], w_ref[:, :n_qkv])
    two = nt(pre_ref[...], w_ref[:, n_qkv:])
    unit = unit_ref[...].astype(F32)
    e_ref[...] = (one * vectors_ref[0:1] + two * vectors_ref[2:3]).astype(BF)
    sums_ref[0:1] = jnp.sum(one * unit, axis=0, keepdims=True)
    sums_ref[1:2] = jnp.sum(one, axis=0, keepdims=True)
    sums_ref[2:3] = jnp.sum(two * unit, axis=0, keepdims=True)
    sums_ref[3:4] = jnp.sum(two, axis=0, keepdims=True)


def back_out_of(vectors, dqkv, pre, w, unit):
    total, width = unit.shape
    tile = 256
    columns = pl.BlockSpec((total, tile), lambda j: (0, j))
    return pl.pallas_call(
        back_out_kernel,
        grid=(width // tile,),
        in_specs=[
            pl.BlockSpec((vectors.shape[0], tile), lambda j: (0, j)),
            resident(dqkv.shape),
            resident(pre.shape),
            pl.BlockSpec((tile, w.shape[1]), lambda j: (j, 0)),
            columns,
        ],
        out_specs=[columns, pl.BlockSpec((4, tile), lambda j: (0, j))],
        out_shape=[
            jax.ShapeDtypeStruct((total, width), BF),
            jax.ShapeDtypeStruct((4, width), F32),
        ],
        cost_estimate=cost(2 * total * w.size, 2 * (unit.size * 4 + w.size)),
        compiler_params=big(),
        name="back_out",
    )(vectors, dqkv, pre, w, unit)


def grad_kernel(count, me_ref, *refs):
    lhs, rhs, (sent_ref, kept_ref) = refs[:count], refs[count : 2 * count], refs[-2:]
    total = tn(lhs[0][...], rhs[0][...])
    for a, b in zip(lhs[1:], rhs[1:]):
        total += tn(a[...], b[...])
    step, half = pl.program_id(0), pl.num_programs(0) // 2

    @pl.when(step < half)
    def _():
        sent_ref[0] = total.astype(BF)

    @pl.when(step >= half)
    def _():
        kept_ref[0] = total.astype(BF)


def grad_of(parity, lhs, rhs, cuts, name):
    total, m = lhs[0].shape
    n, tile, half = rhs[0].shape[1], m // cuts, cuts // 2
    shape = jax.ShapeDtypeStruct((half, tile, n), BF)

    def left(j, me):
        return (0, jnp.where(j < half, 2 * j + 1 - me[0], 2 * (j - half) + me[0]))

    return pl.pallas_call(
        functools.partial(grad_kernel, len(lhs)),
        grid_spec=pltpu.PrefetchScalarGridSpec(
            num_scalar_prefetch=1,
            grid=(cuts,),
            in_specs=[pl.BlockSpec((total, tile), left)] * len(lhs)
            + [
                pl.BlockSpec(r.shape, lambda j, me: (0, 0), pipeline_mode=pl.Buffered(1))
                for r in rhs
            ],
            out_specs=[
                pl.BlockSpec((1, tile, n), lambda j, me: (jnp.minimum(j, half - 1), 0, 0)),
                pl.BlockSpec((1, tile, n), lambda j, me: (jnp.maximum(j - half, 0), 0, 0)),
            ],
        ),
        out_shape=[shape, shape],
        cost_estimate=cost(2 * len(lhs) * total * m * n, 4 * total * (m + n) + 2 * m * n),
        compiler_params=big(),
        name=name,
    )(parity, *lhs, *rhs)


def head_grad_kernel(count, me_ref, *refs):
    lhs, rhs, (sent_ref, kept_ref) = refs[:count], refs[count : 2 * count], refs[-2:]
    total = tn(lhs[0][...], rhs[0][...])
    for a, b in zip(lhs[1:], rhs[1:]):
        total += tn(a[...], b[...])
    half, _, e, n = sent_ref.shape
    total = total.astype(BF).reshape(half, 2, e, n)
    even = me_ref[0] == 0
    kept_ref[:, 0] = jnp.where(even, total[:, 0], total[:, 1])
    sent_ref[:, 0] = jnp.where(even, total[:, 1], total[:, 0])


def head_grad_of(parity, lhs, rhs, cuts, name):
    total, m = lhs[0].shape
    n, e = rhs[0].shape[1], HD // cuts
    shape = jax.ShapeDtypeStruct((cuts // 2, m // HD, e, n), BF)
    return pl.pallas_call(
        functools.partial(head_grad_kernel, len(lhs)),
        grid_spec=pltpu.PrefetchScalarGridSpec(
            num_scalar_prefetch=1,
            grid=(m // HD,),
            in_specs=[pl.BlockSpec((total, HD), lambda j, me: (0, j))] * len(lhs)
            + [
                pl.BlockSpec(r.shape, lambda j, me: (0, 0), pipeline_mode=pl.Buffered(1))
                for r in rhs
            ],
            out_specs=[pl.BlockSpec((cuts // 2, 1, e, n), lambda j, me: (0, j, 0, 0))] * 2,
        ),
        out_shape=[shape, shape],
        cost_estimate=cost(2 * len(lhs) * total * m * n, 4 * total * (m + n) + 2 * m * n),
        compiler_params=big(),
        name=name,
    )(parity, *lhs, *rhs)


def unit_of(rows):
    centred = rows - jnp.mean(rows, axis=-1, keepdims=True)
    scaling = lax.rsqrt(jnp.mean(centred * centred, axis=-1, keepdims=True) + EPSILON)
    return centred * scaling, scaling


def per_device(
    hidden_in,
    lengths,
    dealing,
    cotangent,
    attn_gain,
    attn_shift,
    ffn_gain,
    ffn_shift,
    qkv_weight,
    qkv_bias,
    dense_weight,
    dense_bias,
    fc1_weight,
    fc1_bias,
    fc2_weight,
    fc2_bias,
):
    n_t, n_d = lax.axis_size("tensor"), lax.axis_size("dp")
    my_t, my_d = lax.axis_index("tensor"), lax.axis_index("dp")
    micros, seqs, piece, width = hidden_in.shape
    heads = qkv_weight.shape[1]
    rows = n_d * piece
    n_blocks = 4

    def deal(x):
        return lax.all_to_all(x, "dp", split_axis=0, concat_axis=0, tiled=True).reshape(rows, width)

    def undeal(x):
        x = x.reshape(x.shape[0], seqs, piece, width)
        return lax.all_to_all(x, "dp", split_axis=1, concat_axis=1, tiled=True)

    env = {}

    def stage(chains, computes=()):
        for chain in chains:
            chain.step()
        for fn in computes:
            fn()
        keys = list(env)
        values = [env[k] for k in keys]
        for chain in chains:
            values += chain.live()
        out = list(lax.optimization_barrier(tuple(values)))
        env.update(zip(keys, out))
        at = len(keys)
        for chain in chains:
            count = len(chain.live())
            chain.set_live(out[at : at + count])
            at += count

    def after(x):
        return lax.optimization_barrier((x, env["mark"]))[0]

    eighth = width // (n_d * n_t)
    n_six = 6 * eighth
    env["x0"] = deal(hidden_in[0])
    env["mark"] = jnp.concatenate(
        [attn_gain, attn_shift, ffn_gain, ffn_shift, dense_bias, fc2_bias]
        + [qkv_bias.reshape(-1), fc1_bias.reshape(-1)]
    )
    stage([])

    n_qkv = heads * 3 * HD
    near = jnp.concatenate([after(qkv_weight).reshape(-1, n_qkv), after(fc1_weight)], axis=1)
    w_near = lax.all_gather(near, "dp", axis=0, tiled=True)

    parts = jnp.arange(n_t, dtype=jnp.int32)
    local = jnp.arange(rows, dtype=jnp.int32)
    positions = ((local // piece) * n_t + parts[:, None]) * piece + local % piece
    freqs = jnp.exp(jnp.arange(ROT // 2, dtype=F32) * (-2.0 * math.log(ROPE_BASE) / ROT))
    phases = positions.astype(F32)[..., None] * freqs
    flat = jnp.zeros((n_t, rows, 128 - ROT), F32)
    cosines = jnp.concatenate([jnp.cos(phases), jnp.cos(phases), flat + 1.0], axis=-1)
    sines = jnp.concatenate([-jnp.sin(phases), jnp.sin(phases), flat], axis=-1)
    picked = dealing == my_d
    seq_lens = jnp.sum(jnp.where(picked, lengths, 0), axis=1)
    posq = positions[..., None]

    def tables(m):
        keyed = jnp.where(positions < seq_lens[m], positions, FAR)
        span = rows // n_blocks
        lists = []
        for b in range(n_blocks):
            seen = keyed[:, : span * (b + 1)].reshape(1, -1)
            lists.append(jnp.pad(seen, ((0, 0), (0, n_t * rows - seen.shape[1]))))
        return (posq, jnp.stack(lists), cosines, sines)

    all_tables = [tables(m) for m in range(micros)]
    sum_g = jnp.sum(cotangent.astype(F32), axis=(0, 1, 2))

    chains = {"x0": GatherChain(env["x0"], "tensor", n_t)}
    pending = {}

    def join(*keys):
        def fn():
            for key in keys:
                env[key] = pending.pop(key)

        return fn

    def vectors_over_dp():
        env["small"] = direct_gather(env["mark"], "dp", n_d)

    def vectors_over_tensor():
        six = env["small"][:, :n_six].reshape(-1)
        env["six"] = direct_gather(six, "tensor", n_t)

    def vectors_whole():
        vectors = env.pop("six").reshape(n_t, n_d, 6, eighth).transpose(2, 1, 0, 3)
        env["vectors"] = vectors.reshape(6, width).astype(F32)
        rest = env.pop("small")[:, n_six:].astype(F32)
        n_qb = qkv_bias.size
        env["bias"] = jnp.concatenate(
            [
                rest[:, :n_qb].reshape(n_d, heads, -1).transpose(1, 0, 2).reshape(1, -1),
                rest[:, n_qb:].reshape(n_d, heads, -1).transpose(1, 0, 2).reshape(1, -1),
            ],
            axis=1,
        )

    def deal_two():
        two = jnp.stack([after(hidden_in[1]), cotangent[0]])
        pending["two"] = lax.all_to_all(two, "dp", split_axis=1, concat_axis=1, tiled=True)

    last = n_t - 2

    def at(i, *plan):
        if i < last:
            return list(plan[i]) if i < len(plan) else []
        return [fn for entry in plan[i:] for fn in entry]

    for i in range(n_t - 1):
        stage(
            [chains["x0"]],
            at(i, [vectors_over_dp], [vectors_over_tensor, deal_two], [vectors_whole, join("two")]),
        )
    w_fc2 = lax.all_gather(after(fc2_weight.T), "dp", axis=0, tiled=True)
    w_dense = lax.all_gather(after(dense_weight), "dp", axis=0, tiled=False)
    two = env.pop("two").reshape(2, rows, width)
    own_x, own_g = [env.pop("x0"), two[0]], [two[1], None]
    env["mark"] = vectors = env.pop("vectors")
    out_shift = vectors[4] + vectors[5]
    n_qb = qkv_bias.size

    def norm_qkv_of(m):
        def fn():
            outs = norm_qkv(chains[f"x{m}"], env["mark"], env["bias"], w_near, n_qkv)
            for key, value in zip(("one", "two", "unit", "qkv"), outs):
                env[f"{key}{m}"] = value if key == "qkv" else value.reshape(n_t * rows, -1)

        return fn

    def hidden(m):
        def fn():
            env[f"act{m}"], env[f"slope{m}"] = hidden_of(
                env[f"two{m}"], w_near, env["bias"], n_qkv
            )

        return fn

    def attend_of(m):
        def fn():
            low, mixed = attend(all_tables[m], env.pop(f"qkv{m}"))
            env[f"low{m}"], env[f"mixed{m}"] = low, mixed.reshape(n_t * rows, -1)

        return fn

    def branch(m):
        def fn():
            parts = branch_of(env[f"mixed{m}"], env[f"act{m}"], w_dense, w_fc2)
            env[f"branch{m}"] = parts

        return fn

    def scattered_rows(name):
        return lax.psum_scatter(env.pop(name), "tensor", scatter_dimension=0, tiled=True)

    def output_of(m):
        total = env.pop(f"so{m}").astype(F32)
        return (own_x[m].astype(F32) + total + out_shift).astype(BF)

    def arrange_g(m):
        def fn():
            env[f"g{m}"] = arrange(chains[f"g{m}"]).reshape(n_t * rows, width)

        return fn

    def back_in(m):
        def fn():
            if f"g{m}" not in env:
                arrange_g(m)()
            dmix, env[f"pre{m}"], env[f"b1{m}"] = back_in_of(
                env[f"g{m}"], w_dense, w_fc2, env.pop(f"slope{m}")
            )
            env[f"dmix{m}"] = dmix.reshape(n_t, rows, -1)

        return fn

    def back_attend(m):
        def fn():
            d_qkv, env[f"bq{m}"] = attend_back(
                all_tables[m], env.pop(f"low{m}"), env.pop(f"dmix{m}")
            )
            env[f"dqkv{m}"] = d_qkv.reshape(n_t * rows, -1)

        return fn

    def back_out(m):
        def fn():
            env[f"e{m}"], env[f"sums{m}"] = back_out_of(
                env["mark"], env[f"dqkv{m}"], env[f"pre{m}"], w_near, env.pop(f"unit{m}")
            )

        return fn

    def input_of(m):
        total = env.pop(f"si{m}").astype(F32)
        unit, scaling = unit_of(own_x[m].astype(F32))
        back = scaling * (
            total
            - jnp.mean(total, axis=-1, keepdims=True)
            - unit * jnp.mean(total * unit, axis=-1, keepdims=True)
        )
        return (own_g[m].astype(F32) + back).astype(BF)

    def output_rows():
        pending["rows"] = undeal(jnp.stack([output_of(0), output_of(1)]))

    def pair(key):
        return [env[f"{key}{m}"] for m in range(micros)]

    parity = (my_d % 2)[None]
    swap = [(i, i ^ 1) for i in range(n_d)]
    same_parity = [list(range(p, n_d, 2)) for p in range(2)]

    def fc2_grads():
        env["w2_sent"], env["w2_kept"] = grad_of(parity, pair("g"), pair("act"), n_d, "grad_fc2")

    def dense_grads():
        halves = head_grad_of(parity, pair("mixed"), pair("g"), n_d, "grad_dense")
        env["wd_sent"], env["wd_kept"] = (h.reshape(n_d // 2, -1, width) for h in halves)

    def fc1_grads():
        env["w1_sent"], env["w1_kept"] = grad_of(parity, pair("two"), pair("pre"), n_d, "grad_fc1")

    def qkv_grads():
        env["wq_sent"], env["wq_kept"] = grad_of(parity, pair("one"), pair("dqkv"), n_d, "grad_qkv")

    def swapped(key):
        def fn():
            env[f"{key}_got"] = lax.ppermute(env.pop(f"{key}_sent"), "dp", swap)

        return fn

    def spread(key):
        both_cores = env.pop(f"{key}_kept").astype(F32) + env.pop(f"{key}_got").astype(F32)
        return lax.all_to_all(
            both_cores.astype(BF),
            "dp",
            split_axis=0,
            concat_axis=0,
            axis_index_groups=same_parity,
            tiled=True,
        )

    def both(*fns):
        def fn():
            for each in fns:
                each()

        return fn

    def summed(key):
        return jnp.sum(env.pop(key).astype(F32), axis=0)

    def fc2_final():
        env["grad_fc2"] = summed("w2").T

    def fc1_final():
        env["grad_fc1"] = summed("w1")

    def qkv_final():
        env["grad_qkv"] = summed("wq").reshape(-1, heads, 3 * HD)

    def dense_final():
        env["grad_dense"] = summed("wd").reshape(heads, -1, width)

    def steps_of(these, *plan):
        for i in range(these[0].steps()):
            stage(these, at(i, *plan))

    def gather_chain(name, x):
        chains[name] = GatherChain(after(x), "tensor", n_t)
        return chains[name]

    def deal_g():
        env["own_g1"] = deal(after(cotangent[1]))

    def spread_later(*keys):
        for key in keys:
            pending[key] = spread(key)

    def steps_of(these, *plan):
        for i in range(these[0].steps()):
            stage(these, at(i, *plan))

    steps_of(
        [gather_chain("x1", own_x[1]), gather_chain("g0", own_g[0])],
        [norm_qkv_of(0), hidden(0)],
        [attend_of(0), deal_g],
        [branch(0)],
    )
    own_g[1] = env.pop("own_g1")
    steps_of(
        [gather_chain("g1", own_g[1])],
        [norm_qkv_of(1)],
        [hidden(1), attend_of(1)],
        [branch(1), arrange_g(0)],
    )
    pending["so0"] = scattered_rows("branch0")
    pending["so1"] = scattered_rows("branch1")
    stage(
        [], [arrange_g(1), dense_grads, swapped("wd"), fc2_grads, swapped("w2"), back_in(0)]
    )
    spread_later("w2")
    stage([], [back_attend(0), back_out(0), back_in(1), join("w2", "so0")])
    pending["si0"] = scattered_rows("e0")
    spread_later("wd")
    stage([], [fc1_grads, swapped("w1"), join("wd")])
    spread_later("w1")
    stage(
        [],
        [
            back_attend(1),
            qkv_grads,
            swapped("wq"),
            back_out(1),
            join("w1", "so1"),
        ],
    )
    pending["si1"] = scattered_rows("e1")
    spread_later("wq")
    sums = jnp.concatenate([env["sums0"] + env["sums1"], sum_g[None]], axis=0)
    sums = sums.reshape(5, n_d, n_t, eighth).transpose(1, 2, 0, 3).reshape(n_d, -1)
    qkvb = (env["bq0"] + env["bq1"]).reshape(heads, n_d, -1).transpose(1, 0, 2).reshape(n_d, -1)
    fc1b = (env["b10"] + env["b11"]).reshape(heads, n_d, -1).transpose(1, 0, 2).reshape(n_d, -1)
    small = jnp.concatenate([sums, qkvb, fc1b], axis=1)
    n_sum = 5 * n_t * eighth

    def small_over_dp():
        env["small"] = direct_scatter(small, "dp", n_d)

    def small_over_tensor():
        env["mine"] = direct_scatter(env["small"][:n_sum].reshape(n_t, -1), "tensor", n_t)

    stage([], [small_over_dp, fc2_final, fc1_final, dense_final, join("wq", "si0")])
    output_rows()
    stage([], [small_over_tensor, qkv_final, join("rows")])
    stage([], [join("si1")])
    grads_in = undeal(jnp.stack([input_of(0), input_of(1)]))
    small_out = env["small"]

    outputs = env["rows"]

    small = small_out
    mine = env["mine"].reshape(5, eighth)
    qkvb = small[n_sum : n_sum + n_qb].reshape(heads, -1)
    fc1b = small[n_sum + n_qb :].reshape(heads, -1)

    return (
        outputs,
        grads_in,
        mine[0],
        mine[1],
        mine[2],
        mine[3],
        env["grad_qkv"],
        qkvb,
        env["grad_dense"],
        mine[4],
        env["grad_fc1"],
        fc1b,
        env["grad_fc2"],
        mine[4],
    )


def solution(mesh):
    rows = P(None, None, ("dp", "tensor"), None)
    vector = P(("dp", "tensor"))
    return jax.shard_map(
        per_device,
        mesh=mesh,
        in_specs=(
            rows,
            P(),
            P(),
            rows,
            vector,
            vector,
            vector,
            vector,
            P("dp", "tensor", None),
            P("tensor", "dp"),
            P("tensor", "dp", None),
            vector,
            P("dp", "tensor"),
            P("tensor", "dp"),
            P("tensor", "dp"),
            vector,
        ),
        out_specs=(
            rows,
            rows,
            vector,
            vector,
            vector,
            vector,
            P("dp", "tensor", None),
            P("tensor", "dp"),
            P("tensor", "dp", None),
            vector,
            P("dp", "tensor"),
            P("tensor", "dp"),
            P("tensor", "dp"),
            vector,
        ),
        check_vma=False,
    )
```

```python
import functools
import math

import jax
import jax.numpy as jnp
from jax import lax
from jax.experimental import pallas as pl
from jax.experimental.pallas import tpu as pltpu
from jax.sharding import PartitionSpec as P

HD = 256
ROT = 64
EPSILON = 1e-05
ROPE_BASE = 10000.0
NEG_FILL = -1e30
SQRT_HALF = 0.7071067811865476
INV_ROOT_TWO_PI = 0.3989422804014327
BF = jnp.bfloat16
F32 = jnp.float32
FAR = 1 << 20
SHARE = 4096


class GatherChain:
    def __init__(self, x, axis, n):
        self.x, self.axis, self.n, self.step_no = x, axis, n, 0
        self.me = lax.axis_index(axis)
        self.left, self.right = [], []

    def steps(self):
        return self.n - 1

    def step(self):
        n = self.n
        s = self.step_no = self.step_no + 1
        to_right = self.left[-1] if self.left else self.x
        to_left = self.right[-1] if self.right else self.x
        pairs = [(k, k + 1) for k in range(s - 1, n - 1)]
        self.left.append(lax.ppermute(to_right, self.axis, pairs))
        pairs = [(k, k - 1) for k in range(1, n - s + 1)]
        self.right.append(lax.ppermute(to_left, self.axis, pairs))

    def live(self):
        return [self.left[-1], self.right[-1]]

    def set_live(self, values):
        self.left[-1], self.right[-1] = values


def shifts(n):
    return [[(k, (k + s) % n) for k in range(n)] for s in range(1, n)]


def direct_gather(x, axis, n):
    me = lax.axis_index(axis)
    got = jnp.stack([x] + [lax.ppermute(x, axis, pairs) for pairs in shifts(n)])
    order = (me - jnp.arange(n)) % n
    chosen = order[None, :] == jnp.arange(n)[:, None]
    return jnp.sum(jnp.where(chosen[:, :, None], got[None], 0), axis=1).astype(x.dtype)


def direct_scatter(x, axis, n):
    me = lax.axis_index(axis)
    total = lax.dynamic_index_in_dim(x, me, 0, keepdims=False)
    for s, pairs in enumerate(shifts(n), 1):
        sent = lax.dynamic_index_in_dim(x, (me + s) % n, 0, keepdims=False)
        total = total + lax.ppermute(sent, axis, pairs)
    return total


def rotated(x, cosines, sines):
    lanes = lax.broadcasted_iota(jnp.int32, x.shape, 1)
    partner = jnp.where(lanes < ROT // 2, pltpu.roll(x, 128 - ROT // 2, 1), pltpu.roll(x, ROT // 2, 1))
    return x * cosines + partner * sines


def scores_of(q, k, posq, posk):
    s = lax.dot_general(q, k, (((1,), (1,)), ((), ())), preferred_element_type=F32)
    return jnp.where(posk <= posq, s * (1.0 / math.sqrt(HD)), NEG_FILL)


def attend_kernel(n_blocks, posq_ref, posk_ref, cos_ref, sin_ref, qkv_ref, low_ref, mixed_ref):
    n_slots, rows, _ = qkv_ref.shape
    span = rows // n_blocks
    for t in range(n_slots):
        for base in (0, HD):
            lead = rotated(qkv_ref[t, :, base : base + 128], cos_ref[t], sin_ref[t])
            low_ref[t, :, base : base + 128] = lead.astype(BF)
            low_ref[t, :, base + 128 : base + HD] = qkv_ref[t, :, base + 128 : base + HD].astype(BF)
        low_ref[t, :, 2 * HD :] = qkv_ref[t, :, 2 * HD :].astype(BF)
    for b in range(n_blocks):
        own, seen = pl.ds(b * span, span), span * (b + 1)
        n_q, n_k = n_slots * span, n_slots * seen
        q = low_ref[:, own, :HD].reshape(n_q, HD)
        k = low_ref[:, :seen, HD : 2 * HD].reshape(n_k, HD)
        v = low_ref[:, :seen, 2 * HD :].reshape(n_k, HD)
        posq = posq_ref[:, own, :].reshape(n_q, 1)
        s = scores_of(q, k, posq, posk_ref[b, :, :n_k])
        e = jnp.exp(s - jnp.max(s, axis=-1, keepdims=True))
        p = e * (1.0 / jnp.sum(e, axis=-1, keepdims=True))
        mixed = jnp.dot(p.astype(BF), v, preferred_element_type=F32)
        mixed_ref[:, own, :] = mixed.astype(BF).reshape(n_slots, span, HD)


def attend_back_kernel(
    n_blocks,
    posq_ref,
    posk_ref,
    cos_ref,
    sin_ref,
    low_ref,
    dmix_ref,
    grad_ref,
    bias_ref,
    dk_ref,
    dv_ref,
):
    n_slots, rows, _ = low_ref.shape
    span = rows // n_blocks
    scale = 1.0 / math.sqrt(HD)
    for b in reversed(range(n_blocks)):
        own, seen = pl.ds(b * span, span), span * (b + 1)
        n_q, n_k = n_slots * span, n_slots * seen
        q = low_ref[:, own, :HD].reshape(n_q, HD)
        k = low_ref[:, :seen, HD : 2 * HD].reshape(n_k, HD)
        v = low_ref[:, :seen, 2 * HD :].reshape(n_k, HD)
        dmix = dmix_ref[:, own, :].reshape(n_q, HD)
        posq = posq_ref[:, own, :].reshape(n_q, 1)
        s = scores_of(q, k, posq, posk_ref[b, :, :n_k])
        e = jnp.exp(s - jnp.max(s, axis=-1, keepdims=True))
        p = e * (1.0 / jnp.sum(e, axis=-1, keepdims=True))
        dp = lax.dot_general(dmix, v, (((1,), (1,)), ((), ())), preferred_element_type=F32)
        ds = (p * (dp - jnp.sum(p * dp, axis=-1, keepdims=True))).astype(BF)
        dq = jnp.dot(ds, k, preferred_element_type=F32) * scale
        dk = lax.dot_general(ds, q, (((0,), (0,)), ((), ())), preferred_element_type=F32)
        dv = lax.dot_general(p.astype(BF), dmix, (((0,), (0,)), ((), ())), preferred_element_type=F32)
        dk, dv = dk.reshape(n_slots, seen, HD), dv.reshape(n_slots, seen, HD)
        if b == n_blocks - 1:
            dk_ref[...] = dk
            dv_ref[...] = dv
        else:
            dk_ref[:, :seen, :] += dk
            dv_ref[:, :seen, :] += dv
        dq = dq.reshape(n_slots, span, HD)
        for t in range(n_slots):
            lead = rotated(dq[t, :, :128], cos_ref[t, own, :], -sin_ref[t, own, :])
            grad_ref[t, own, :128] = lead.astype(BF)
            grad_ref[t, own, 128:HD] = dq[t, :, 128:].astype(BF)
    for t in range(n_slots):
        lead = rotated(dk_ref[t, :, :128] * scale, cos_ref[t], -sin_ref[t])
        grad_ref[t, :, HD : HD + 128] = lead.astype(BF)
        grad_ref[t, :, HD + 128 : 2 * HD] = (dk_ref[t, :, 128:] * scale).astype(BF)
        grad_ref[t, :, 2 * HD :] = dv_ref[t].astype(BF)
        summed = jnp.sum(grad_ref[t].astype(F32), axis=0, keepdims=True)
        bias_ref[0] = summed if t == 0 else bias_ref[0] + summed


def whole_spec(shape):
    return pl.BlockSpec(shape, lambda h: (0,) * len(shape))


def head_spec(n_slots, rows, width):
    return pl.BlockSpec((n_slots, rows, width), lambda h: (0, 0, h))


def attend(tables, qkv):
    posq, posk, cosines, sines = tables
    n_slots, rows, width = qkv.shape
    heads = width // (3 * HD)
    pairs = (n_slots * rows) ** 2 // 2 * heads
    return pl.pallas_call(
        functools.partial(attend_kernel, posk.shape[0]),
        grid=(heads,),
        in_specs=[whole_spec(t.shape) for t in tables] + [head_spec(n_slots, rows, 3 * HD)],
        out_specs=[head_spec(n_slots, rows, 3 * HD), head_spec(n_slots, rows, HD)],
        out_shape=[
            jax.ShapeDtypeStruct(qkv.shape, BF),
            jax.ShapeDtypeStruct((n_slots, rows, heads * HD), BF),
        ],
        cost_estimate=pl.CostEstimate(
            flops=4 * pairs * HD, bytes_accessed=qkv.size * 8, transcendentals=pairs
        ),
        compiler_params=pltpu.CompilerParams(vmem_limit_bytes=48 << 20),
        name="attend",
    )(posq, posk, cosines, sines, qkv)


def attend_back(tables, low, dmix):
    n_slots, rows, width = low.shape
    heads = width // (3 * HD)
    pairs = (n_slots * rows) ** 2 // 2 * heads
    return pl.pallas_call(
        functools.partial(attend_back_kernel, tables[1].shape[0]),
        grid=(heads,),
        in_specs=[whole_spec(t.shape) for t in tables]
        + [head_spec(n_slots, rows, 3 * HD), head_spec(n_slots, rows, HD)],
        out_specs=[
            head_spec(n_slots, rows, 3 * HD),
            pl.BlockSpec((1, 1, 3 * HD), lambda h: (h, 0, 0)),
        ],
        out_shape=[
            jax.ShapeDtypeStruct(low.shape, BF),
            jax.ShapeDtypeStruct((heads, 1, 3 * HD), F32),
        ],
        scratch_shapes=[pltpu.VMEM((n_slots, rows, HD), F32)] * 2,
        cost_estimate=pl.CostEstimate(
            flops=10 * pairs * HD, bytes_accessed=low.size * 5, transcendentals=pairs
        ),
        compiler_params=pltpu.CompilerParams(vmem_limit_bytes=48 << 20),
        name="attend_back",
    )(*tables, low, dmix)


def slot_rows(blocks, s):
    n = (len(blocks) + 1) // 2
    if s == 0:
        return blocks[0][...].astype(F32)
    return blocks[s][...].astype(F32) + blocks[2 * n - 1 - s][...].astype(F32)


def part_of(me_ref, s):
    return lax.rem(me_ref[0] - s + me_ref[1], me_ref[1])


def cdf_and_slope(x):
    size = jnp.abs(x)
    bell = jnp.exp(-0.5 * x * x)
    t = 1.0 / (1.0 + (0.3275911 * SQRT_HALF) * size)
    poly = ((((1.061405429 * t - 1.453152027) * t) + 1.421413741) * t - 0.284496736) * t + 0.254829592
    tail = 0.5 * poly * t * bell
    cdf = jnp.where(x >= 0, 1.0 - tail, tail)
    return cdf, cdf + x * bell * INV_ROOT_TWO_PI


def norm_qkv_kernel(n_blocks, me_ref, vectors_ref, bias_ref, *refs):
    blocks, w_hbm = refs[:n_blocks], refs[n_blocks]
    one_ref, two_ref, unit_ref, qkv_ref, w_ref, sem = refs[n_blocks + 1 :]
    n_slots, block, width = one_ref.shape
    n_qkv = w_ref.shape[1]
    first = pl.program_id(0) == 0
    copy = pltpu.make_async_copy(w_hbm.at[:, pl.ds(0, n_qkv)], w_ref, sem)

    @pl.when(first)
    def _():
        copy.start()

    for s in range(n_slots):
        rows = slot_rows(blocks, s)
        centred = rows - jnp.mean(rows, axis=-1, keepdims=True)
        unit = centred * lax.rsqrt(jnp.mean(centred * centred, axis=-1, keepdims=True) + EPSILON)
        part = part_of(me_ref, s)
        one_ref[part] = (unit * vectors_ref[0:1] + vectors_ref[1:2]).astype(BF)
        two_ref[part] = (unit * vectors_ref[2:3] + vectors_ref[3:4]).astype(BF)
        unit_ref[part] = unit.astype(BF)

    @pl.when(first)
    def _():
        copy.wait()

    one = one_ref[...].reshape(n_slots * block, width)
    tile = 768
    for c in range(0, n_qkv, tile):
        out = jnp.dot(one, w_ref[:, c : c + tile], preferred_element_type=F32)
        out = out + bias_ref[:, c : c + tile]
        qkv_ref[:, :, c : c + tile] = out.reshape(n_slots, block, tile)


def hidden_kernel(two_ref, w_ref, bias_ref, act_ref, slope_ref):
    pre = jnp.dot(two_ref[...], w_ref[...], preferred_element_type=F32) + bias_ref[...]
    cdf, slope = cdf_and_slope(pre)
    act_ref[...] = (pre * cdf).astype(BF)
    slope_ref[...] = slope.astype(BF)


def big(limit=56):
    return pltpu.CompilerParams(vmem_limit_bytes=limit << 20)


def cost(flops, moved, special=0):
    return pl.CostEstimate(
        flops=int(flops) // SHARE,
        bytes_accessed=int(moved) // SHARE,
        transcendentals=int(special) // SHARE,
    )


def norm_qkv(chain, vectors, bias, w, n_qkv):
    n = chain.n
    rows, width = chain.x.shape
    block = 64
    me = jnp.stack([chain.me, jnp.int32(n)])
    blocks = [chain.x] + chain.left + chain.right

    def out(cols, dtype):
        return (
            jax.ShapeDtypeStruct((n, rows, cols), dtype),
            pl.BlockSpec((n, block, cols), lambda i, me: (0, i, 0)),
        )

    shapes, specs = zip(out(width, BF), out(width, BF), out(width, BF), out(n_qkv, F32))
    total = n * rows
    return pl.pallas_call(
        functools.partial(norm_qkv_kernel, len(blocks)),
        grid_spec=pltpu.PrefetchScalarGridSpec(
            num_scalar_prefetch=1,
            grid=(rows // block,),
            in_specs=[
                pl.BlockSpec(vectors.shape, lambda i, me: (0, 0)),
                pl.BlockSpec(bias.shape, lambda i, me: (0, 0)),
            ]
            + [pl.BlockSpec((block, width), lambda i, me: (i, 0))] * len(blocks)
            + [pl.BlockSpec(memory_space=pl.ANY)],
            out_specs=list(specs),
            scratch_shapes=[pltpu.VMEM((width, n_qkv), BF), pltpu.SemaphoreType.DMA],
        ),
        out_shape=list(shapes),
        cost_estimate=cost(2 * total * width * n_qkv, 10 * total * width + width * n_qkv * 2),
        compiler_params=big(),
        name="norm_qkv",
    )(me, vectors, bias, *blocks, w)


def hidden_of(two, w, bias, n_qkv):
    total, width = two.shape
    n_ff, tile = w.shape[1] - n_qkv, 256
    skip = n_qkv // tile
    columns = pl.BlockSpec((total, tile), lambda j: (0, j))
    return pl.pallas_call(
        hidden_kernel,
        grid=(n_ff // tile,),
        in_specs=[
            resident(two.shape),
            pl.BlockSpec((width, tile), lambda j: (0, j + skip)),
            pl.BlockSpec((1, tile), lambda j: (0, j + skip)),
        ],
        out_specs=[columns, columns],
        out_shape=[jax.ShapeDtypeStruct((total, n_ff), BF)] * 2,
        cost_estimate=cost(2 * total * width * n_ff, 2 * width * n_ff + 8 * total * n_ff, total * n_ff),
        compiler_params=big(),
        name="hidden",
    )(two, w, bias)


def arrange_kernel(me_ref, *refs):
    blocks, out_ref = refs[:-1], refs[-1]
    n = (len(blocks) + 1) // 2
    for s in range(n):
        part = part_of(me_ref, s)
        if s == 0:
            out_ref[part] = blocks[0][...]
        else:
            out_ref[part] = blocks[s][...] + blocks[2 * n - 1 - s][...]


def arrange(chain):
    n = chain.n
    rows, width = chain.x.shape
    block = 64
    me = jnp.stack([chain.me, jnp.int32(n)])
    blocks = [chain.x] + chain.left + chain.right
    return pl.pallas_call(
        arrange_kernel,
        grid_spec=pltpu.PrefetchScalarGridSpec(
            num_scalar_prefetch=1,
            grid=(rows // block,),
            in_specs=[pl.BlockSpec((block, width), lambda i, me: (i, 0))] * len(blocks),
            out_specs=pl.BlockSpec((n, block, width), lambda i, me: (0, i, 0)),
        ),
        out_shape=jax.ShapeDtypeStruct((n, rows, width), BF),
        cost_estimate=cost(0, 6 * n * rows * width),
        compiler_params=big(),
        name="arrange",
    )(me, *blocks)


def nt(a, b):
    return lax.dot_general(a, b, (((1,), (1,)), ((), ())), preferred_element_type=F32)


def tn(a, b):
    return lax.dot_general(a, b, (((0,), (0,)), ((), ())), preferred_element_type=F32)


def resident(shape):
    return pl.BlockSpec(shape, lambda j: (0,) * len(shape), pipeline_mode=pl.Buffered(1))


def head_rows(dense_ref, h):
    n, _, e, cols = dense_ref.shape
    return dense_ref[:, h].reshape(n * e, cols)


def branch_kernel(mixed_ref, act_ref, dense_ref, w_ref, *refs):
    out_ref = refs[-1]
    total = nt(act_ref[...], w_ref[...])
    for h in range(dense_ref.shape[1]):
        total += jnp.dot(
            mixed_ref[:, h * HD : (h + 1) * HD],
            head_rows(dense_ref, h),
            preferred_element_type=F32,
        )
    out_ref[...] = total.astype(BF).reshape(out_ref.shape)


def branch_of(mixed, act, dense, w_fc2, slot, shape, before=None):
    total, width, tile = act.shape[0], w_fc2.shape[0], 512
    parts, _, rows, _ = shape
    return pl.pallas_call(
        branch_kernel,
        grid=(width // tile,),
        in_specs=[
            resident(mixed.shape),
            resident(act.shape),
            pl.BlockSpec(dense.shape[:3] + (tile,), lambda j: (0, 0, 0, j)),
            pl.BlockSpec((tile, w_fc2.shape[1]), lambda j: (j, 0)),
        ]
        + ([] if before is None else [pl.BlockSpec(memory_space=pl.ANY)]),
        out_specs=pl.BlockSpec((parts, 1, rows, tile), lambda j: (0, slot, 0, j)),
        out_shape=jax.ShapeDtypeStruct(shape, BF),
        input_output_aliases={} if before is None else {4: 0},
        cost_estimate=cost(2 * total * (dense.size + w_fc2.size), 2 * (act.size * 3 + w_fc2.size)),
        compiler_params=big(),
        name="branch",
    )(mixed, act, dense, w_fc2, *([] if before is None else [before]))


def back_in_kernel(g_ref, dense_ref, w_ref, slope_ref, dmix_ref, pre_ref, bias_ref):
    @pl.when(pl.program_id(0) == 0)
    def _():
        for h in range(dense_ref.shape[1]):
            dmix_ref[:, h * HD : (h + 1) * HD] = nt(g_ref[...], head_rows(dense_ref, h)).astype(BF)

    d_act = jnp.dot(g_ref[...], w_ref[...], preferred_element_type=F32)
    d_pre = (d_act * slope_ref[...].astype(F32)).astype(BF)
    pre_ref[...] = d_pre
    bias_ref[...] = jnp.sum(d_pre.astype(F32), axis=0, keepdims=True)


def back_in_of(g, dense, w_fc2, slope):
    total, width = g.shape
    n_ff, tile = w_fc2.shape[1], 512
    heads = dense.shape[1]
    columns = pl.BlockSpec((total, tile), lambda j: (0, j))
    return pl.pallas_call(
        back_in_kernel,
        grid=(n_ff // tile,),
        in_specs=[
            resident(g.shape),
            resident(dense.shape),
            pl.BlockSpec((width, tile), lambda j: (0, j)),
            columns,
        ],
        out_specs=[
            pl.BlockSpec((total, heads * HD), lambda j: (0, 0)),
            columns,
            pl.BlockSpec((1, tile), lambda j: (0, j)),
        ],
        out_shape=[
            jax.ShapeDtypeStruct((total, heads * HD), BF),
            jax.ShapeDtypeStruct((total, n_ff), BF),
            jax.ShapeDtypeStruct((1, n_ff), F32),
        ],
        cost_estimate=cost(2 * total * (dense.size + w_fc2.size), 2 * (g.size * 3 + w_fc2.size)),
        compiler_params=big(),
        name="back_in",
    )(g, dense, w_fc2, slope)


def back_out_kernel(vectors_ref, dqkv_ref, pre_ref, w_ref, unit_ref, e_ref, sums_ref):
    n_qkv = dqkv_ref.shape[1]
    one = nt(dqkv_ref[...], w_ref[:, :n_qkv])
    two = nt(pre_ref[...], w_ref[:, n_qkv:])
    unit = unit_ref[...].astype(F32)
    e_ref[...] = (one * vectors_ref[0:1] + two * vectors_ref[2:3]).astype(BF)
    sums_ref[0:1] = jnp.sum(one * unit, axis=0, keepdims=True)
    sums_ref[1:2] = jnp.sum(one, axis=0, keepdims=True)
    sums_ref[2:3] = jnp.sum(two * unit, axis=0, keepdims=True)
    sums_ref[3:4] = jnp.sum(two, axis=0, keepdims=True)


def back_out_of(vectors, dqkv, pre, w, unit):
    total, width = unit.shape
    tile = 256
    columns = pl.BlockSpec((total, tile), lambda j: (0, j))
    return pl.pallas_call(
        back_out_kernel,
        grid=(width // tile,),
        in_specs=[
            pl.BlockSpec((vectors.shape[0], tile), lambda j: (0, j)),
            resident(dqkv.shape),
            resident(pre.shape),
            pl.BlockSpec((tile, w.shape[1]), lambda j: (j, 0)),
            columns,
        ],
        out_specs=[columns, pl.BlockSpec((4, tile), lambda j: (0, j))],
        out_shape=[
            jax.ShapeDtypeStruct((total, width), BF),
            jax.ShapeDtypeStruct((4, width), F32),
        ],
        cost_estimate=cost(2 * total * w.size, 2 * (unit.size * 4 + w.size)),
        compiler_params=big(),
        name="back_out",
    )(vectors, dqkv, pre, w, unit)


def grad_kernel(count, me_ref, *refs):
    lhs, rhs, out_ref = refs[:count], refs[count : 2 * count], refs[-1]
    total = tn(lhs[0][...], rhs[0][...])
    for a, b in zip(lhs[1:], rhs[1:]):
        total += tn(a[...], b[...])
    if len(refs) > 2 * count + 1:
        total += refs[2 * count][0].astype(F32)
    out_ref[0] = total.astype(BF)


def grad_of(parity, lhs, rhs, cuts, name, got=None):
    total, m = lhs[0].shape
    n, tile, half = rhs[0].shape[1], m // cuts, cuts // 2
    block = pl.BlockSpec((1, tile, n), lambda j, me: (j, 0, 0))
    return pl.pallas_call(
        functools.partial(grad_kernel, len(lhs)),
        grid_spec=pltpu.PrefetchScalarGridSpec(
            num_scalar_prefetch=1,
            grid=(half,),
            in_specs=[pl.BlockSpec((total, tile), lambda j, me: (0, 2 * j + me[0]))] * len(lhs)
            + [
                pl.BlockSpec(r.shape, lambda j, me: (0, 0), pipeline_mode=pl.Buffered(1))
                for r in rhs
            ]
            + ([] if got is None else [block]),
            out_specs=block,
        ),
        out_shape=jax.ShapeDtypeStruct((half, tile, n), BF),
        cost_estimate=cost(len(lhs) * total * m * n, 4 * total * (m + n) + 2 * m * n),
        compiler_params=big(),
        name=name,
    )(parity, *lhs, *rhs, *([] if got is None else [got]))


def head_grad_kernel(count, me_ref, *refs):
    lhs, rhs, (sent_ref, kept_ref) = refs[:count], refs[count : 2 * count], refs[-2:]
    total = tn(lhs[0][...], rhs[0][...])
    for a, b in zip(lhs[1:], rhs[1:]):
        total += tn(a[...], b[...])
    half, _, e, n = sent_ref.shape
    total = total.astype(BF).reshape(half, 2, e, n)
    even = me_ref[0] == 0
    kept_ref[:, 0] = jnp.where(even, total[:, 0], total[:, 1])
    sent_ref[:, 0] = jnp.where(even, total[:, 1], total[:, 0])


def head_grad_of(parity, lhs, rhs, cuts, name):
    total, m = lhs[0].shape
    n, e = rhs[0].shape[1], HD // cuts
    shape = jax.ShapeDtypeStruct((cuts // 2, m // HD, e, n), BF)
    return pl.pallas_call(
        functools.partial(head_grad_kernel, len(lhs)),
        grid_spec=pltpu.PrefetchScalarGridSpec(
            num_scalar_prefetch=1,
            grid=(m // HD,),
            in_specs=[pl.BlockSpec((total, HD), lambda j, me: (0, j))] * len(lhs)
            + [
                pl.BlockSpec(r.shape, lambda j, me: (0, 0), pipeline_mode=pl.Buffered(1))
                for r in rhs
            ],
            out_specs=[pl.BlockSpec((cuts // 2, 1, e, n), lambda j, me: (0, j, 0, 0))] * 2,
        ),
        out_shape=[shape, shape],
        cost_estimate=cost(2 * len(lhs) * total * m * n, 4 * total * (m + n) + 2 * m * n),
        compiler_params=big(),
        name=name,
    )(parity, *lhs, *rhs)


def unit_of(rows):
    centred = rows - jnp.mean(rows, axis=-1, keepdims=True)
    scaling = lax.rsqrt(jnp.mean(centred * centred, axis=-1, keepdims=True) + EPSILON)
    return centred * scaling, scaling


def per_device(
    hidden_in,
    lengths,
    dealing,
    cotangent,
    attn_gain,
    attn_shift,
    ffn_gain,
    ffn_shift,
    qkv_weight,
    qkv_bias,
    dense_weight,
    dense_bias,
    fc1_weight,
    fc1_bias,
    fc2_weight,
    fc2_bias,
):
    n_t, n_d = lax.axis_size("tensor"), lax.axis_size("dp")
    my_t, my_d = lax.axis_index("tensor"), lax.axis_index("dp")
    micros, seqs, piece, width = hidden_in.shape
    heads = qkv_weight.shape[1]
    rows = n_d * piece
    n_blocks = 4

    def deal(x):
        return lax.all_to_all(x, "dp", split_axis=0, concat_axis=0, tiled=True).reshape(rows, width)

    def undeal(x):
        x = x.reshape(x.shape[0], seqs, piece, width)
        return lax.all_to_all(x, "dp", split_axis=1, concat_axis=1, tiled=True)

    env = {}

    def stage(chains, computes=()):
        for chain in chains:
            chain.step()
        for fn in computes:
            fn()
        keys = list(env)
        values = [env[k] for k in keys]
        for chain in chains:
            values += chain.live()
        out = list(lax.optimization_barrier(tuple(values)))
        env.update(zip(keys, out))
        at = len(keys)
        for chain in chains:
            count = len(chain.live())
            chain.set_live(out[at : at + count])
            at += count

    def after(x):
        return lax.optimization_barrier((x, env["mark"]))[0]

    eighth = width // (n_d * n_t)
    n_six = 6 * eighth
    env["x0"] = deal(hidden_in[0])
    env["mark"] = jnp.concatenate(
        [attn_gain, attn_shift, ffn_gain, ffn_shift, dense_bias, fc2_bias]
        + [qkv_bias.reshape(-1), fc1_bias.reshape(-1)]
    )
    n_qkv = heads * 3 * HD
    env["near"] = jnp.concatenate([qkv_weight.reshape(-1, n_qkv), fc1_weight], axis=1)
    stage([])

    w_near = lax.all_gather(env.pop("near"), "dp", axis=0, tiled=True)

    parts = jnp.arange(n_t, dtype=jnp.int32)
    local = jnp.arange(rows, dtype=jnp.int32)
    positions = ((local // piece) * n_t + parts[:, None]) * piece + local % piece
    freqs = jnp.exp(jnp.arange(ROT // 2, dtype=F32) * (-2.0 * math.log(ROPE_BASE) / ROT))
    phases = positions.astype(F32)[..., None] * freqs
    flat = jnp.zeros((n_t, rows, 128 - ROT), F32)
    cosines = jnp.concatenate([jnp.cos(phases), jnp.cos(phases), flat + 1.0], axis=-1)
    sines = jnp.concatenate([-jnp.sin(phases), jnp.sin(phases), flat], axis=-1)
    picked = dealing == my_d
    seq_lens = jnp.sum(jnp.where(picked, lengths, 0), axis=1)
    posq = positions[..., None]

    def tables(m):
        keyed = jnp.where(positions < seq_lens[m], positions, FAR)
        span = rows // n_blocks
        lists = []
        for b in range(n_blocks):
            seen = keyed[:, : span * (b + 1)].reshape(1, -1)
            lists.append(jnp.pad(seen, ((0, 0), (0, n_t * rows - seen.shape[1]))))
        return (posq, jnp.stack(lists), cosines, sines)

    all_tables = [tables(m) for m in range(micros)]
    sum_g = jnp.sum(cotangent.astype(F32), axis=(0, 1, 2))

    chains = {"x0": GatherChain(env["x0"], "tensor", n_t)}
    pending = {}

    def join(*keys):
        def fn():
            for key in keys:
                env[key] = pending.pop(key)

        return fn

    def vectors_over_dp():
        env["small"] = direct_gather(env["mark"], "dp", n_d)

    def vectors_over_tensor():
        six = env["small"][:, :n_six].reshape(-1)
        env["six"] = direct_gather(six, "tensor", n_t)

    def vectors_whole():
        vectors = env.pop("six").reshape(n_t, n_d, 6, eighth).transpose(2, 1, 0, 3)
        env["vectors"] = vectors.reshape(6, width).astype(F32)
        rest = env.pop("small")[:, n_six:].astype(F32)
        n_qb = qkv_bias.size
        env["bias"] = jnp.concatenate(
            [
                rest[:, :n_qb].reshape(n_d, heads, -1).transpose(1, 0, 2).reshape(1, -1),
                rest[:, n_qb:].reshape(n_d, heads, -1).transpose(1, 0, 2).reshape(1, -1),
            ],
            axis=1,
        )

    def deal_two():
        two = jnp.stack([after(hidden_in[1]), cotangent[0]])
        pending["two"] = lax.all_to_all(two, "dp", split_axis=1, concat_axis=1, tiled=True)

    last = n_t - 2

    def at(i, *plan):
        if i < last:
            return list(plan[i]) if i < len(plan) else []
        return [fn for entry in plan[i:] for fn in entry]

    for i in range(n_t - 1):
        stage(
            [chains["x0"]],
            at(i, [vectors_over_dp], [vectors_over_tensor, deal_two], [vectors_whole, join("two")]),
        )
    w_fc2 = lax.all_gather(after(fc2_weight.T), "dp", axis=0, tiled=True)
    w_dense = lax.all_gather(after(dense_weight), "dp", axis=0, tiled=False)
    two = env.pop("two").reshape(2, rows, width)
    own_x, own_g = [env.pop("x0"), two[0]], [two[1], None]
    env["mark"] = vectors = env.pop("vectors")
    out_shift = vectors[4] + vectors[5]
    n_qb = qkv_bias.size

    def norm_qkv_of(m):
        def fn():
            outs = norm_qkv(chains[f"x{m}"], env["mark"], env["bias"], w_near, n_qkv)
            for key, value in zip(("one", "two", "unit", "qkv"), outs):
                env[f"{key}{m}"] = value if key == "qkv" else value.reshape(n_t * rows, -1)

        return fn

    def hidden(m):
        def fn():
            env[f"act{m}"], env[f"slope{m}"] = hidden_of(
                env[f"two{m}"], w_near, env["bias"], n_qkv
            )

        return fn

    def attend_of(m):
        def fn():
            low, mixed = attend(all_tables[m], env.pop(f"qkv{m}"))
            env[f"low{m}"], env[f"mixed{m}"] = low, mixed.reshape(n_t * rows, -1)

        return fn

    def branch(m):
        def fn():
            env["branch"] = branch_of(
                env[f"mixed{m}"],
                env[f"act{m}"],
                w_dense,
                w_fc2,
                m,
                (n_t, micros, rows, width),
                env.get("branch"),
            )

        return fn

    def scattered_rows(name):
        terms = env.pop(name).reshape(-1, width)
        return lax.psum_scatter(terms, "tensor", scatter_dimension=0, tiled=True)

    def output_of(m):
        total = env["so"].reshape(micros, rows, width)[m].astype(F32)
        return (own_x[m].astype(F32) + total + out_shift).astype(BF)

    def arrange_g(m):
        def fn():
            env[f"g{m}"] = arrange(chains[f"g{m}"]).reshape(n_t * rows, width)

        return fn

    def back_in(m):
        def fn():
            if f"g{m}" not in env:
                arrange_g(m)()
            dmix, env[f"pre{m}"], env[f"b1{m}"] = back_in_of(
                env[f"g{m}"], w_dense, w_fc2, env.pop(f"slope{m}")
            )
            env[f"dmix{m}"] = dmix.reshape(n_t, rows, -1)

        return fn

    def back_attend(m):
        def fn():
            d_qkv, env[f"bq{m}"] = attend_back(
                all_tables[m], env.pop(f"low{m}"), env.pop(f"dmix{m}")
            )
            env[f"dqkv{m}"] = d_qkv.reshape(n_t * rows, -1)

        return fn

    def back_out(m):
        def fn():
            env[f"e{m}"], env[f"sums{m}"] = back_out_of(
                env["mark"], env[f"dqkv{m}"], env[f"pre{m}"], w_near, env.pop(f"unit{m}")
            )

        return fn

    def input_of(m):
        total = env.pop(f"si{m}").astype(F32)
        unit, scaling = unit_of(own_x[m].astype(F32))
        back = scaling * (
            total
            - jnp.mean(total, axis=-1, keepdims=True)
            - unit * jnp.mean(total * unit, axis=-1, keepdims=True)
        )
        return (own_g[m].astype(F32) + back).astype(BF)

    def output_rows():
        pending["rows"] = undeal(jnp.stack([output_of(0), output_of(1)]))

    def pair(key):
        return [env[f"{key}{m}"] for m in range(micros)]

    parity = (my_d % 2)[None]
    swap = [(i, i ^ 1) for i in range(n_d)]
    same_parity = [list(range(p, n_d, 2)) for p in range(2)]

    sides = {"w2": ("g", "act"), "w1": ("two", "pre"), "wq": ("one", "dqkv")}

    def sent_grads(key):
        def fn():
            lhs, rhs = (pair(side) for side in sides[key])
            sent = grad_of(1 - parity, lhs, rhs, n_d, f"grad_{key}_sent")
            env[f"{key}_got"] = lax.ppermute(sent, "dp", swap)

        return fn

    def sent_only(key):
        def fn():
            lhs, rhs = (pair(side) for side in sides[key])
            env[f"{key}_sent"] = grad_of(1 - parity, lhs, rhs, n_d, f"grad_{key}_sent")

        return fn

    def kept_grads(key):
        def fn():
            lhs, rhs = (pair(side) for side in sides[key])
            got = env.pop(f"{key}_got")
            env[f"{key}_pair"] = grad_of(parity, lhs, rhs, n_d, f"grad_{key}_kept", got)

        return fn

    def dense_grads():
        halves = head_grad_of(parity, pair("mixed"), pair("g"), n_d, "grad_dense")
        env["wd_sent"], env["wd_kept"] = (h.reshape(n_d // 2, -1, width) for h in halves)

    def swapped(key):
        def fn():
            env[f"{key}_got"] = lax.ppermute(env.pop(f"{key}_sent"), "dp", swap)

        return fn

    def spread(key):
        if f"{key}_pair" in env:
            pair_sums = env.pop(f"{key}_pair")
        else:
            pair_sums = env.pop(f"{key}_kept").astype(F32) + env.pop(f"{key}_got").astype(F32)
        return lax.all_to_all(
            pair_sums.astype(BF),
            "dp",
            split_axis=0,
            concat_axis=0,
            axis_index_groups=same_parity,
            tiled=True,
        )

    def summed(key):
        return jnp.sum(env.pop(key).astype(F32), axis=0)

    def fc2_final():
        env["grad_fc2"] = summed("w2").T

    def fc1_final():
        env["grad_fc1"] = summed("w1")

    def qkv_final():
        env["grad_qkv"] = summed("wq").reshape(-1, heads, 3 * HD)

    def dense_final():
        env["grad_dense"] = summed("wd").reshape(heads, -1, width)

    def steps_of(these, *plan):
        for i in range(these[0].steps()):
            stage(these, at(i, *plan))

    def gather_chain(name, x):
        chains[name] = GatherChain(after(x), "tensor", n_t)
        return chains[name]

    def deal_g():
        env["own_g1"] = deal(after(cotangent[1]))

    def spread_later(*keys):
        for key in keys:
            pending[key] = spread(key)

    def steps_of(these, *plan):
        for i in range(these[0].steps()):
            stage(these, at(i, *plan))

    steps_of(
        [gather_chain("x1", own_x[1]), gather_chain("g0", own_g[0])],
        [norm_qkv_of(0), hidden(0)],
        [attend_of(0), deal_g],
        [branch(0)],
    )
    own_g[1] = env.pop("own_g1")
    steps_of(
        [gather_chain("g1", own_g[1])],
        [norm_qkv_of(1)],
        [hidden(1), attend_of(1)],
        [branch(1), arrange_g(0)],
    )
    pending["so"] = scattered_rows("branch")
    stage([], [arrange_g(1), sent_grads("w2"), back_in(0)])
    stage([], [kept_grads("w2")])
    spread_later("w2")
    stage([], [back_attend(0), back_out(0), back_in(1), join("w2")])
    pending["si0"] = scattered_rows("e0")
    stage([], [sent_grads("w1"), back_attend(1)])
    stage([], [kept_grads("w1")])
    spread_later("w1")
    stage([], [sent_only("wq"), back_out(1), join("w1", "so")])
    pending["si1"] = scattered_rows("e1")
    output_rows()
    stage([], [swapped("wq"), dense_grads, kept_grads("wq"), join("rows")])
    spread_later("wq")
    sums = jnp.concatenate([env["sums0"] + env["sums1"], sum_g[None]], axis=0)
    sums = sums.reshape(5, n_d, n_t, eighth).transpose(1, 2, 0, 3).reshape(n_d, -1)
    qkvb = (env["bq0"] + env["bq1"]).reshape(heads, n_d, -1).transpose(1, 0, 2).reshape(n_d, -1)
    fc1b = (env["b10"] + env["b11"]).reshape(heads, n_d, -1).transpose(1, 0, 2).reshape(n_d, -1)
    small = jnp.concatenate([sums, qkvb, fc1b], axis=1)
    n_sum = 5 * n_t * eighth

    def small_over_dp():
        for s, pairs in enumerate(shifts(n_d), 1):
            sent = lax.dynamic_index_in_dim(small, (my_d + s) % n_d, 0, keepdims=False)
            env[f"small{s}"] = lax.ppermute(sent, "dp", pairs)
        env["small0"] = lax.dynamic_index_in_dim(small, my_d, 0, keepdims=False)

    def small_over_tensor():
        env["small"] = sum(env.pop(f"small{s}") for s in range(n_d))
        env["mine"] = direct_scatter(env["small"][:n_sum].reshape(n_t, -1), "tensor", n_t)

    stage([], [small_over_dp, swapped("wd"), fc2_final, fc1_final, join("wq", "si0")])
    spread_later("wd")
    stage([], [qkv_final, small_over_tensor, join("wd")])
    stage([], [join("si1")])
    grads_in = undeal(jnp.stack([input_of(0), input_of(1)]))
    dense_final()
    small_out = env["small"]

    outputs = env["rows"]

    small = small_out
    mine = env["mine"].reshape(5, eighth)
    qkvb = small[n_sum : n_sum + n_qb].reshape(heads, -1)
    fc1b = small[n_sum + n_qb :].reshape(heads, -1)

    return (
        outputs,
        grads_in,
        mine[0],
        mine[1],
        mine[2],
        mine[3],
        env["grad_qkv"],
        qkvb,
        env["grad_dense"],
        mine[4],
        env["grad_fc1"],
        fc1b,
        env["grad_fc2"],
        mine[4],
    )


def solution(mesh):
    rows = P(None, None, ("dp", "tensor"), None)
    vector = P(("dp", "tensor"))
    return jax.shard_map(
        per_device,
        mesh=mesh,
        in_specs=(
            rows,
            P(),
            P(),
            rows,
            vector,
            vector,
            vector,
            vector,
            P("dp", "tensor", None),
            P("tensor", "dp"),
            P("tensor", "dp", None),
            vector,
            P("dp", "tensor"),
            P("tensor", "dp"),
            P("tensor", "dp"),
            vector,
        ),
        out_specs=(
            rows,
            rows,
            vector,
            vector,
            vector,
            vector,
            P("dp", "tensor", None),
            P("tensor", "dp"),
            P("tensor", "dp", None),
            vector,
            P("dp", "tensor"),
            P("tensor", "dp"),
            P("tensor", "dp"),
            vector,
        ),
        check_vma=False,
    )
```

```python
import functools
import math

import jax
import jax.numpy as jnp
from jax import lax
from jax.experimental import pallas as pl
from jax.experimental.pallas import tpu as pltpu
from jax.sharding import PartitionSpec as P

HD = 256
ROT = 64
EPSILON = 1e-05
ROPE_BASE = 10000.0
NEG_FILL = -1e30
SQRT_HALF = 0.7071067811865476
INV_ROOT_TWO_PI = 0.3989422804014327
BF = jnp.bfloat16
F32 = jnp.float32
FAR = 1 << 20
SHARE = 4096


class GatherChain:
    def __init__(self, x, axis, n):
        self.x, self.axis, self.n, self.step_no = x, axis, n, 0
        self.me = lax.axis_index(axis)
        self.left, self.right = [], []

    def steps(self):
        return self.n - 1

    def step(self):
        n = self.n
        s = self.step_no = self.step_no + 1
        to_right = self.left[-1] if self.left else self.x
        to_left = self.right[-1] if self.right else self.x
        pairs = [(k, k + 1) for k in range(s - 1, n - 1)]
        self.left.append(lax.ppermute(to_right, self.axis, pairs))
        pairs = [(k, k - 1) for k in range(1, n - s + 1)]
        self.right.append(lax.ppermute(to_left, self.axis, pairs))

    def live(self):
        return [self.left[-1], self.right[-1]]

    def set_live(self, values):
        self.left[-1], self.right[-1] = values


def shifts(n):
    return [[(k, (k + s) % n) for k in range(n)] for s in range(1, n)]


def direct_gather(x, axis, n):
    me = lax.axis_index(axis)
    got = jnp.stack([x] + [lax.ppermute(x, axis, pairs) for pairs in shifts(n)])
    order = (me - jnp.arange(n)) % n
    chosen = order[None, :] == jnp.arange(n)[:, None]
    return jnp.sum(jnp.where(chosen[:, :, None], got[None], 0), axis=1).astype(x.dtype)


def direct_scatter(x, axis, n):
    me = lax.axis_index(axis)
    total = lax.dynamic_index_in_dim(x, me, 0, keepdims=False)
    for s, pairs in enumerate(shifts(n), 1):
        sent = lax.dynamic_index_in_dim(x, (me + s) % n, 0, keepdims=False)
        total = total + lax.ppermute(sent, axis, pairs)
    return total


def rotated(x, cosines, sines):
    lanes = lax.broadcasted_iota(jnp.int32, x.shape, 1)
    partner = jnp.where(lanes < ROT // 2, pltpu.roll(x, 128 - ROT // 2, 1), pltpu.roll(x, ROT // 2, 1))
    return x * cosines + partner * sines


def scores_of(q, k, posq, posk):
    s = lax.dot_general(q, k, (((1,), (1,)), ((), ())), preferred_element_type=F32)
    return jnp.where(posk <= posq, s * (1.0 / math.sqrt(HD)), NEG_FILL)


def attend_kernel(n_blocks, posq_ref, posk_ref, cos_ref, sin_ref, qkv_ref, low_ref, mixed_ref):
    n_slots, rows, _ = qkv_ref.shape
    span = rows // n_blocks
    for t in range(n_slots):
        for base in (0, HD):
            lead = rotated(qkv_ref[t, :, base : base + 128], cos_ref[t], sin_ref[t])
            low_ref[t, :, base : base + 128] = lead.astype(BF)
            low_ref[t, :, base + 128 : base + HD] = qkv_ref[t, :, base + 128 : base + HD].astype(BF)
        low_ref[t, :, 2 * HD :] = qkv_ref[t, :, 2 * HD :].astype(BF)
    for b in range(n_blocks):
        own, seen = pl.ds(b * span, span), span * (b + 1)
        n_q, n_k = n_slots * span, n_slots * seen
        q = low_ref[:, own, :HD].reshape(n_q, HD)
        k = low_ref[:, :seen, HD : 2 * HD].reshape(n_k, HD)
        v = low_ref[:, :seen, 2 * HD :].reshape(n_k, HD)
        posq = posq_ref[:, own, :].reshape(n_q, 1)
        s = scores_of(q, k, posq, posk_ref[b, :, :n_k])
        e = jnp.exp(s - jnp.max(s, axis=-1, keepdims=True))
        p = e * (1.0 / jnp.sum(e, axis=-1, keepdims=True))
        mixed = jnp.dot(p.astype(BF), v, preferred_element_type=F32)
        mixed_ref[:, own, :] = mixed.astype(BF).reshape(n_slots, span, HD)


def attend_back_kernel(
    n_blocks,
    posq_ref,
    posk_ref,
    cos_ref,
    sin_ref,
    low_ref,
    dmix_ref,
    grad_ref,
    bias_ref,
    dk_ref,
    dv_ref,
):
    n_slots, rows, _ = low_ref.shape
    span = rows // n_blocks
    scale = 1.0 / math.sqrt(HD)
    for b in reversed(range(n_blocks)):
        own, seen = pl.ds(b * span, span), span * (b + 1)
        n_q, n_k = n_slots * span, n_slots * seen
        q = low_ref[:, own, :HD].reshape(n_q, HD)
        k = low_ref[:, :seen, HD : 2 * HD].reshape(n_k, HD)
        v = low_ref[:, :seen, 2 * HD :].reshape(n_k, HD)
        dmix = dmix_ref[:, own, :].reshape(n_q, HD)
        posq = posq_ref[:, own, :].reshape(n_q, 1)
        s = scores_of(q, k, posq, posk_ref[b, :, :n_k])
        e = jnp.exp(s - jnp.max(s, axis=-1, keepdims=True))
        p = e * (1.0 / jnp.sum(e, axis=-1, keepdims=True))
        dp = lax.dot_general(dmix, v, (((1,), (1,)), ((), ())), preferred_element_type=F32)
        ds = (p * (dp - jnp.sum(p * dp, axis=-1, keepdims=True))).astype(BF)
        dq = jnp.dot(ds, k, preferred_element_type=F32) * scale
        dk = lax.dot_general(ds, q, (((0,), (0,)), ((), ())), preferred_element_type=F32)
        dv = lax.dot_general(p.astype(BF), dmix, (((0,), (0,)), ((), ())), preferred_element_type=F32)
        dk, dv = dk.reshape(n_slots, seen, HD), dv.reshape(n_slots, seen, HD)
        if b == n_blocks - 1:
            dk_ref[...] = dk
            dv_ref[...] = dv
        else:
            dk_ref[:, :seen, :] += dk
            dv_ref[:, :seen, :] += dv
        dq = dq.reshape(n_slots, span, HD)
        for t in range(n_slots):
            lead = rotated(dq[t, :, :128], cos_ref[t, own, :], -sin_ref[t, own, :])
            grad_ref[t, own, :128] = lead.astype(BF)
            grad_ref[t, own, 128:HD] = dq[t, :, 128:].astype(BF)
    for t in range(n_slots):
        lead = rotated(dk_ref[t, :, :128] * scale, cos_ref[t], -sin_ref[t])
        grad_ref[t, :, HD : HD + 128] = lead.astype(BF)
        grad_ref[t, :, HD + 128 : 2 * HD] = (dk_ref[t, :, 128:] * scale).astype(BF)
        grad_ref[t, :, 2 * HD :] = dv_ref[t].astype(BF)
        summed = jnp.sum(grad_ref[t].astype(F32), axis=0, keepdims=True)
        bias_ref[0] = summed if t == 0 else bias_ref[0] + summed


def whole_spec(shape):
    return pl.BlockSpec(shape, lambda h: (0,) * len(shape))


def head_spec(n_slots, rows, width):
    return pl.BlockSpec((n_slots, rows, width), lambda h: (0, 0, h))


def attend(tables, qkv):
    posq, posk, cosines, sines = tables
    n_slots, rows, width = qkv.shape
    heads = width // (3 * HD)
    pairs = (n_slots * rows) ** 2 // 2 * heads
    return pl.pallas_call(
        functools.partial(attend_kernel, posk.shape[0]),
        grid=(heads,),
        in_specs=[whole_spec(t.shape) for t in tables] + [head_spec(n_slots, rows, 3 * HD)],
        out_specs=[head_spec(n_slots, rows, 3 * HD), head_spec(n_slots, rows, HD)],
        out_shape=[
            jax.ShapeDtypeStruct(qkv.shape, BF),
            jax.ShapeDtypeStruct((n_slots, rows, heads * HD), BF),
        ],
        cost_estimate=pl.CostEstimate(
            flops=4 * pairs * HD, bytes_accessed=qkv.size * 8, transcendentals=pairs
        ),
        compiler_params=pltpu.CompilerParams(vmem_limit_bytes=48 << 20),
        name="attend",
    )(posq, posk, cosines, sines, qkv)


def attend_back(tables, low, dmix):
    n_slots, rows, width = low.shape
    heads = width // (3 * HD)
    pairs = (n_slots * rows) ** 2 // 2 * heads
    return pl.pallas_call(
        functools.partial(attend_back_kernel, tables[1].shape[0]),
        grid=(heads,),
        in_specs=[whole_spec(t.shape) for t in tables]
        + [head_spec(n_slots, rows, 3 * HD), head_spec(n_slots, rows, HD)],
        out_specs=[
            head_spec(n_slots, rows, 3 * HD),
            pl.BlockSpec((1, 1, 3 * HD), lambda h: (h, 0, 0)),
        ],
        out_shape=[
            jax.ShapeDtypeStruct(low.shape, BF),
            jax.ShapeDtypeStruct((heads, 1, 3 * HD), F32),
        ],
        scratch_shapes=[pltpu.VMEM((n_slots, rows, HD), F32)] * 2,
        cost_estimate=pl.CostEstimate(
            flops=10 * pairs * HD, bytes_accessed=low.size * 5, transcendentals=pairs
        ),
        compiler_params=pltpu.CompilerParams(vmem_limit_bytes=48 << 20),
        name="attend_back",
    )(*tables, low, dmix)


def slot_rows(blocks, s):
    n = (len(blocks) + 1) // 2
    if s == 0:
        return blocks[0][...].astype(F32)
    return blocks[s][...].astype(F32) + blocks[2 * n - 1 - s][...].astype(F32)


def part_of(me_ref, s):
    return lax.rem(me_ref[0] - s + me_ref[1], me_ref[1])


def cdf_and_slope(x):
    size = jnp.abs(x)
    bell = jnp.exp(-0.5 * x * x)
    t = 1.0 / (1.0 + (0.3275911 * SQRT_HALF) * size)
    poly = ((((1.061405429 * t - 1.453152027) * t) + 1.421413741) * t - 0.284496736) * t + 0.254829592
    tail = 0.5 * poly * t * bell
    cdf = jnp.where(x >= 0, 1.0 - tail, tail)
    return cdf, cdf + x * bell * INV_ROOT_TWO_PI


def norm_qkv_kernel(n_blocks, me_ref, vectors_ref, bias_ref, *refs):
    blocks, w_hbm = refs[:n_blocks], refs[n_blocks]
    one_ref, two_ref, unit_ref, qkv_ref, w_ref, sem = refs[n_blocks + 1 :]
    n_slots, block, width = one_ref.shape
    n_qkv = w_ref.shape[1]
    first = pl.program_id(0) == 0
    copy = pltpu.make_async_copy(w_hbm.at[:, pl.ds(0, n_qkv)], w_ref, sem)

    @pl.when(first)
    def _():
        copy.start()

    for s in range(n_slots):
        rows = slot_rows(blocks, s)
        centred = rows - jnp.mean(rows, axis=-1, keepdims=True)
        unit = centred * lax.rsqrt(jnp.mean(centred * centred, axis=-1, keepdims=True) + EPSILON)
        part = part_of(me_ref, s)
        one_ref[part] = (unit * vectors_ref[0:1] + vectors_ref[1:2]).astype(BF)
        two_ref[part] = (unit * vectors_ref[2:3] + vectors_ref[3:4]).astype(BF)
        unit_ref[part] = unit.astype(BF)

    @pl.when(first)
    def _():
        copy.wait()

    one = one_ref[...].reshape(n_slots * block, width)
    tile = 768
    for c in range(0, n_qkv, tile):
        out = jnp.dot(one, w_ref[:, c : c + tile], preferred_element_type=F32)
        out = out + bias_ref[:, c : c + tile]
        qkv_ref[:, :, c : c + tile] = out.reshape(n_slots, block, tile)


def hidden_kernel(two_ref, w_ref, bias_ref, act_ref, slope_ref):
    pre = jnp.dot(two_ref[...], w_ref[...], preferred_element_type=F32) + bias_ref[...]
    cdf, slope = cdf_and_slope(pre)
    act_ref[...] = (pre * cdf).astype(BF)
    slope_ref[...] = slope.astype(BF)


def big(limit=56):
    return pltpu.CompilerParams(vmem_limit_bytes=limit << 20)


def cost(flops, moved, special=0):
    return pl.CostEstimate(
        flops=int(flops) // SHARE,
        bytes_accessed=int(moved) // SHARE,
        transcendentals=int(special) // SHARE,
    )


def norm_qkv(chain, vectors, bias, w, n_qkv):
    n = chain.n
    rows, width = chain.x.shape
    block = 64
    me = jnp.stack([chain.me, jnp.int32(n)])
    blocks = [chain.x] + chain.left + chain.right

    def out(cols, dtype):
        return (
            jax.ShapeDtypeStruct((n, rows, cols), dtype),
            pl.BlockSpec((n, block, cols), lambda i, me: (0, i, 0)),
        )

    shapes, specs = zip(out(width, BF), out(width, BF), out(width, BF), out(n_qkv, F32))
    total = n * rows
    return pl.pallas_call(
        functools.partial(norm_qkv_kernel, len(blocks)),
        grid_spec=pltpu.PrefetchScalarGridSpec(
            num_scalar_prefetch=1,
            grid=(rows // block,),
            in_specs=[
                pl.BlockSpec(vectors.shape, lambda i, me: (0, 0)),
                pl.BlockSpec(bias.shape, lambda i, me: (0, 0)),
            ]
            + [pl.BlockSpec((block, width), lambda i, me: (i, 0))] * len(blocks)
            + [pl.BlockSpec(memory_space=pl.ANY)],
            out_specs=list(specs),
            scratch_shapes=[pltpu.VMEM((width, n_qkv), BF), pltpu.SemaphoreType.DMA],
        ),
        out_shape=list(shapes),
        cost_estimate=cost(2 * total * width * n_qkv, 10 * total * width + width * n_qkv * 2),
        compiler_params=big(),
        name="norm_qkv",
    )(me, vectors, bias, *blocks, w)


def hidden_of(two, w, bias, n_qkv):
    total, width = two.shape
    n_ff, tile = w.shape[1] - n_qkv, 256
    skip = n_qkv // tile
    columns = pl.BlockSpec((total, tile), lambda j: (0, j))
    return pl.pallas_call(
        hidden_kernel,
        grid=(n_ff // tile,),
        in_specs=[
            resident(two.shape),
            pl.BlockSpec((width, tile), lambda j: (0, j + skip)),
            pl.BlockSpec((1, tile), lambda j: (0, j + skip)),
        ],
        out_specs=[columns, columns],
        out_shape=[jax.ShapeDtypeStruct((total, n_ff), BF)] * 2,
        cost_estimate=cost(2 * total * width * n_ff, 2 * width * n_ff + 8 * total * n_ff, total * n_ff),
        compiler_params=big(),
        name="hidden",
    )(two, w, bias)


def arrange_kernel(me_ref, *refs):
    blocks, out_ref = refs[:-1], refs[-1]
    n = (len(blocks) + 1) // 2
    for s in range(n):
        part = part_of(me_ref, s)
        if s == 0:
            out_ref[part] = blocks[0][...]
        else:
            out_ref[part] = blocks[s][...] + blocks[2 * n - 1 - s][...]


def arrange(chain):
    n = chain.n
    rows, width = chain.x.shape
    block = 64
    me = jnp.stack([chain.me, jnp.int32(n)])
    blocks = [chain.x] + chain.left + chain.right
    return pl.pallas_call(
        arrange_kernel,
        grid_spec=pltpu.PrefetchScalarGridSpec(
            num_scalar_prefetch=1,
            grid=(rows // block,),
            in_specs=[pl.BlockSpec((block, width), lambda i, me: (i, 0))] * len(blocks),
            out_specs=pl.BlockSpec((n, block, width), lambda i, me: (0, i, 0)),
        ),
        out_shape=jax.ShapeDtypeStruct((n, rows, width), BF),
        cost_estimate=cost(0, 6 * n * rows * width),
        compiler_params=big(),
        name="arrange",
    )(me, *blocks)


def nt(a, b):
    return lax.dot_general(a, b, (((1,), (1,)), ((), ())), preferred_element_type=F32)


def tn(a, b):
    return lax.dot_general(a, b, (((0,), (0,)), ((), ())), preferred_element_type=F32)


def resident(shape):
    return pl.BlockSpec(shape, lambda j: (0,) * len(shape), pipeline_mode=pl.Buffered(1))


def head_rows(dense_ref, h):
    n, _, e, cols = dense_ref.shape
    return dense_ref[:, h].reshape(n * e, cols)


def branch_kernel(mixed_ref, act_ref, dense_ref, w_ref, *refs):
    out_ref = refs[-1]
    total = nt(act_ref[...], w_ref[...])
    for h in range(dense_ref.shape[1]):
        total += jnp.dot(
            mixed_ref[:, h * HD : (h + 1) * HD],
            head_rows(dense_ref, h),
            preferred_element_type=F32,
        )
    out_ref[...] = total.astype(BF).reshape(out_ref.shape)


def branch_of(mixed, act, dense, w_fc2, slot, shape, before=None):
    total, width, tile = act.shape[0], w_fc2.shape[0], 512
    parts, _, rows, _ = shape
    return pl.pallas_call(
        branch_kernel,
        grid=(width // tile,),
        in_specs=[
            resident(mixed.shape),
            resident(act.shape),
            pl.BlockSpec(dense.shape[:3] + (tile,), lambda j: (0, 0, 0, j)),
            pl.BlockSpec((tile, w_fc2.shape[1]), lambda j: (j, 0)),
        ]
        + ([] if before is None else [pl.BlockSpec(memory_space=pl.ANY)]),
        out_specs=pl.BlockSpec((parts, 1, rows, tile), lambda j: (0, slot, 0, j)),
        out_shape=jax.ShapeDtypeStruct(shape, BF),
        input_output_aliases={} if before is None else {4: 0},
        cost_estimate=cost(2 * total * (dense.size + w_fc2.size), 2 * (act.size * 3 + w_fc2.size)),
        compiler_params=big(),
        name="branch",
    )(mixed, act, dense, w_fc2, *([] if before is None else [before]))


def back_in_kernel(g_ref, dense_ref, w_ref, slope_ref, dmix_ref, pre_ref, bias_ref):
    @pl.when(pl.program_id(0) == 0)
    def _():
        for h in range(dense_ref.shape[1]):
            dmix_ref[:, h * HD : (h + 1) * HD] = nt(g_ref[...], head_rows(dense_ref, h)).astype(BF)

    d_act = jnp.dot(g_ref[...], w_ref[...], preferred_element_type=F32)
    d_pre = (d_act * slope_ref[...].astype(F32)).astype(BF)
    pre_ref[...] = d_pre
    bias_ref[...] = jnp.sum(d_pre.astype(F32), axis=0, keepdims=True)


def back_in_of(g, dense, w_fc2, slope):
    total, width = g.shape
    n_ff, tile = w_fc2.shape[1], 512
    heads = dense.shape[1]
    columns = pl.BlockSpec((total, tile), lambda j: (0, j))
    return pl.pallas_call(
        back_in_kernel,
        grid=(n_ff // tile,),
        in_specs=[
            resident(g.shape),
            resident(dense.shape),
            pl.BlockSpec((width, tile), lambda j: (0, j)),
            columns,
        ],
        out_specs=[
            pl.BlockSpec((total, heads * HD), lambda j: (0, 0)),
            columns,
            pl.BlockSpec((1, tile), lambda j: (0, j)),
        ],
        out_shape=[
            jax.ShapeDtypeStruct((total, heads * HD), BF),
            jax.ShapeDtypeStruct((total, n_ff), BF),
            jax.ShapeDtypeStruct((1, n_ff), F32),
        ],
        cost_estimate=cost(2 * total * (dense.size + w_fc2.size), 2 * (g.size * 3 + w_fc2.size)),
        compiler_params=big(),
        name="back_in",
    )(g, dense, w_fc2, slope)


def back_out_kernel(vectors_ref, dqkv_ref, pre_ref, w_ref, unit_ref, e_ref, sums_ref):
    n_qkv = dqkv_ref.shape[1]
    one = nt(dqkv_ref[...], w_ref[:, :n_qkv])
    two = nt(pre_ref[...], w_ref[:, n_qkv:])
    unit = unit_ref[...].astype(F32)
    e_ref[...] = (one * vectors_ref[0:1] + two * vectors_ref[2:3]).astype(BF)
    sums_ref[0:1] = jnp.sum(one * unit, axis=0, keepdims=True)
    sums_ref[1:2] = jnp.sum(one, axis=0, keepdims=True)
    sums_ref[2:3] = jnp.sum(two * unit, axis=0, keepdims=True)
    sums_ref[3:4] = jnp.sum(two, axis=0, keepdims=True)


def back_out_of(vectors, dqkv, pre, w, unit):
    total, width = unit.shape
    tile = 256
    columns = pl.BlockSpec((total, tile), lambda j: (0, j))
    return pl.pallas_call(
        back_out_kernel,
        grid=(width // tile,),
        in_specs=[
            pl.BlockSpec((vectors.shape[0], tile), lambda j: (0, j)),
            resident(dqkv.shape),
            resident(pre.shape),
            pl.BlockSpec((tile, w.shape[1]), lambda j: (j, 0)),
            columns,
        ],
        out_specs=[columns, pl.BlockSpec((4, tile), lambda j: (0, j))],
        out_shape=[
            jax.ShapeDtypeStruct((total, width), BF),
            jax.ShapeDtypeStruct((4, width), F32),
        ],
        cost_estimate=cost(2 * total * w.size, 2 * (unit.size * 4 + w.size)),
        compiler_params=big(),
        name="back_out",
    )(vectors, dqkv, pre, w, unit)


def grad_kernel(count, me_ref, *refs):
    lhs, rhs, out_ref = refs[:count], refs[count : 2 * count], refs[-1]
    total = tn(lhs[0][...], rhs[0][...])
    for a, b in zip(lhs[1:], rhs[1:]):
        total += tn(a[...], b[...])
    if len(refs) > 2 * count + 1:
        total += refs[2 * count][0].astype(F32)
    out_ref[0] = total.astype(BF)


def grad_of(parity, lhs, rhs, cuts, name, got=None):
    total, m = lhs[0].shape
    n, tile, half = rhs[0].shape[1], m // cuts, cuts // 2
    block = pl.BlockSpec((1, tile, n), lambda j, me: (j, 0, 0))
    return pl.pallas_call(
        functools.partial(grad_kernel, len(lhs)),
        grid_spec=pltpu.PrefetchScalarGridSpec(
            num_scalar_prefetch=1,
            grid=(half,),
            in_specs=[pl.BlockSpec((total, tile), lambda j, me: (0, 2 * j + me[0]))] * len(lhs)
            + [
                pl.BlockSpec(r.shape, lambda j, me: (0, 0), pipeline_mode=pl.Buffered(1))
                for r in rhs
            ]
            + ([] if got is None else [block]),
            out_specs=block,
        ),
        out_shape=jax.ShapeDtypeStruct((half, tile, n), BF),
        cost_estimate=cost(len(lhs) * total * m * n, 4 * total * (m + n) + 2 * m * n),
        compiler_params=big(),
        name=name,
    )(parity, *lhs, *rhs, *([] if got is None else [got]))


def head_grad_kernel(count, me_ref, *refs):
    lhs, rhs, (sent_ref, kept_ref) = refs[:count], refs[count : 2 * count], refs[-2:]
    total = tn(lhs[0][...], rhs[0][...])
    for a, b in zip(lhs[1:], rhs[1:]):
        total += tn(a[...], b[...])
    half, _, e, n = sent_ref.shape
    total = total.astype(BF).reshape(half, 2, e, n)
    even = me_ref[0] == 0
    kept_ref[:, 0] = jnp.where(even, total[:, 0], total[:, 1])
    sent_ref[:, 0] = jnp.where(even, total[:, 1], total[:, 0])


def head_grad_of(parity, lhs, rhs, cuts, name):
    total, m = lhs[0].shape
    n, e = rhs[0].shape[1], HD // cuts
    shape = jax.ShapeDtypeStruct((cuts // 2, m // HD, e, n), BF)
    return pl.pallas_call(
        functools.partial(head_grad_kernel, len(lhs)),
        grid_spec=pltpu.PrefetchScalarGridSpec(
            num_scalar_prefetch=1,
            grid=(m // HD,),
            in_specs=[pl.BlockSpec((total, HD), lambda j, me: (0, j))] * len(lhs)
            + [
                pl.BlockSpec(r.shape, lambda j, me: (0, 0), pipeline_mode=pl.Buffered(1))
                for r in rhs
            ],
            out_specs=[pl.BlockSpec((cuts // 2, 1, e, n), lambda j, me: (0, j, 0, 0))] * 2,
        ),
        out_shape=[shape, shape],
        cost_estimate=cost(2 * len(lhs) * total * m * n, 4 * total * (m + n) + 2 * m * n),
        compiler_params=big(),
        name=name,
    )(parity, *lhs, *rhs)


def unit_of(rows):
    centred = rows - jnp.mean(rows, axis=-1, keepdims=True)
    scaling = lax.rsqrt(jnp.mean(centred * centred, axis=-1, keepdims=True) + EPSILON)
    return centred * scaling, scaling


def per_device(
    hidden_in,
    lengths,
    dealing,
    cotangent,
    attn_gain,
    attn_shift,
    ffn_gain,
    ffn_shift,
    qkv_weight,
    qkv_bias,
    dense_weight,
    dense_bias,
    fc1_weight,
    fc1_bias,
    fc2_weight,
    fc2_bias,
):
    n_t, n_d = lax.axis_size("tensor"), lax.axis_size("dp")
    my_t, my_d = lax.axis_index("tensor"), lax.axis_index("dp")
    micros, seqs, piece, width = hidden_in.shape
    heads = qkv_weight.shape[1]
    rows = n_d * piece
    n_blocks = 4

    def deal(x):
        return lax.all_to_all(x, "dp", split_axis=0, concat_axis=0, tiled=True).reshape(rows, width)

    def undeal(x):
        x = x.reshape(x.shape[0], seqs, piece, width)
        return lax.all_to_all(x, "dp", split_axis=1, concat_axis=1, tiled=True)

    env = {}

    def stage(chains, computes=()):
        for chain in chains:
            chain.step()
        for fn in computes:
            fn()
        keys = list(env)
        values = [env[k] for k in keys]
        for chain in chains:
            values += chain.live()
        out = list(lax.optimization_barrier(tuple(values)))
        env.update(zip(keys, out))
        at = len(keys)
        for chain in chains:
            count = len(chain.live())
            chain.set_live(out[at : at + count])
            at += count

    def after(x):
        return lax.optimization_barrier((x, env["mark"]))[0]

    eighth = width // (n_d * n_t)
    n_six = 6 * eighth
    env["x0"] = deal(hidden_in[0])
    env["mark"] = jnp.concatenate(
        [attn_gain, attn_shift, ffn_gain, ffn_shift, dense_bias, fc2_bias]
        + [qkv_bias.reshape(-1), fc1_bias.reshape(-1)]
    )
    n_qkv = heads * 3 * HD
    env["near"] = jnp.concatenate([qkv_weight.reshape(-1, n_qkv), fc1_weight], axis=1)
    stage([])

    w_near = lax.all_gather(env.pop("near"), "dp", axis=0, tiled=True)

    parts = jnp.arange(n_t, dtype=jnp.int32)
    local = jnp.arange(rows, dtype=jnp.int32)
    positions = ((local // piece) * n_t + parts[:, None]) * piece + local % piece
    freqs = jnp.exp(jnp.arange(ROT // 2, dtype=F32) * (-2.0 * math.log(ROPE_BASE) / ROT))
    phases = positions.astype(F32)[..., None] * freqs
    flat = jnp.zeros((n_t, rows, 128 - ROT), F32)
    cosines = jnp.concatenate([jnp.cos(phases), jnp.cos(phases), flat + 1.0], axis=-1)
    sines = jnp.concatenate([-jnp.sin(phases), jnp.sin(phases), flat], axis=-1)
    picked = dealing == my_d
    seq_lens = jnp.sum(jnp.where(picked, lengths, 0), axis=1)
    posq = positions[..., None]

    def tables(m):
        keyed = jnp.where(positions < seq_lens[m], positions, FAR)
        span = rows // n_blocks
        lists = []
        for b in range(n_blocks):
            seen = keyed[:, : span * (b + 1)].reshape(1, -1)
            lists.append(jnp.pad(seen, ((0, 0), (0, n_t * rows - seen.shape[1]))))
        return (posq, jnp.stack(lists), cosines, sines)

    all_tables = [tables(m) for m in range(micros)]
    sum_g = jnp.sum(cotangent.astype(F32), axis=(0, 1, 2))

    chains = {"x0": GatherChain(env["x0"], "tensor", n_t)}
    pending = {}

    def join(*keys):
        def fn():
            for key in keys:
                env[key] = pending.pop(key)

        return fn

    def vectors_over_dp():
        env["small"] = direct_gather(env["mark"], "dp", n_d)

    def vectors_over_tensor():
        six = env["small"][:, :n_six].reshape(-1)
        env["six"] = direct_gather(six, "tensor", n_t)

    def vectors_whole():
        vectors = env.pop("six").reshape(n_t, n_d, 6, eighth).transpose(2, 1, 0, 3)
        env["vectors"] = vectors.reshape(6, width).astype(F32)
        rest = env.pop("small")[:, n_six:].astype(F32)
        n_qb = qkv_bias.size
        env["bias"] = jnp.concatenate(
            [
                rest[:, :n_qb].reshape(n_d, heads, -1).transpose(1, 0, 2).reshape(1, -1),
                rest[:, n_qb:].reshape(n_d, heads, -1).transpose(1, 0, 2).reshape(1, -1),
            ],
            axis=1,
        )

    def deal_two():
        two = jnp.stack([after(hidden_in[1]), cotangent[0]])
        pending["two"] = lax.all_to_all(two, "dp", split_axis=1, concat_axis=1, tiled=True)

    last = n_t - 2

    def at(i, *plan):
        if i < last:
            return list(plan[i]) if i < len(plan) else []
        return [fn for entry in plan[i:] for fn in entry]

    for i in range(n_t - 1):
        stage(
            [chains["x0"]],
            at(i, [vectors_over_dp], [vectors_over_tensor, deal_two], [vectors_whole, join("two")]),
        )
    w_fc2 = lax.all_gather(after(fc2_weight.T), "dp", axis=0, tiled=True)
    w_dense = lax.all_gather(after(dense_weight), "dp", axis=0, tiled=False)
    two = env.pop("two").reshape(2, rows, width)
    own_x, own_g = [env.pop("x0"), two[0]], [two[1], None]
    env["mark"] = vectors = env.pop("vectors")
    out_shift = vectors[4] + vectors[5]
    n_qb = qkv_bias.size

    def norm_qkv_of(m):
        def fn():
            outs = norm_qkv(chains[f"x{m}"], env["mark"], env["bias"], w_near, n_qkv)
            for key, value in zip(("one", "two", "unit", "qkv"), outs):
                env[f"{key}{m}"] = value if key == "qkv" else value.reshape(n_t * rows, -1)

        return fn

    def hidden(m):
        def fn():
            env[f"act{m}"], env[f"slope{m}"] = hidden_of(
                env[f"two{m}"], w_near, env["bias"], n_qkv
            )

        return fn

    def attend_of(m):
        def fn():
            low, mixed = attend(all_tables[m], env.pop(f"qkv{m}"))
            env[f"low{m}"], env[f"mixed{m}"] = low, mixed.reshape(n_t * rows, -1)

        return fn

    def branch(m):
        def fn():
            env["branch"] = branch_of(
                env[f"mixed{m}"],
                env[f"act{m}"],
                w_dense,
                w_fc2,
                m,
                (n_t, micros, rows, width),
                env.get("branch"),
            )

        return fn

    def scattered_rows(name):
        terms = env.pop(name).reshape(-1, width)
        return lax.psum_scatter(terms, "tensor", scatter_dimension=0, tiled=True)

    def output_of(m):
        total = env["so"].reshape(micros, rows, width)[m].astype(F32)
        return (own_x[m].astype(F32) + total + out_shift).astype(BF)

    def arrange_g(m):
        def fn():
            env[f"g{m}"] = arrange(chains[f"g{m}"]).reshape(n_t * rows, width)

        return fn

    def back_in(m):
        def fn():
            if f"g{m}" not in env:
                arrange_g(m)()
            dmix, env[f"pre{m}"], env[f"b1{m}"] = back_in_of(
                env[f"g{m}"], w_dense, w_fc2, env.pop(f"slope{m}")
            )
            env[f"dmix{m}"] = dmix.reshape(n_t, rows, -1)

        return fn

    def back_attend(m):
        def fn():
            d_qkv, env[f"bq{m}"] = attend_back(
                all_tables[m], env.pop(f"low{m}"), env.pop(f"dmix{m}")
            )
            env[f"dqkv{m}"] = d_qkv.reshape(n_t * rows, -1)

        return fn

    def back_out(m):
        def fn():
            env[f"e{m}"], env[f"sums{m}"] = back_out_of(
                env["mark"], env[f"dqkv{m}"], env[f"pre{m}"], w_near, env.pop(f"unit{m}")
            )

        return fn

    def input_of(m):
        total = env.pop(f"si{m}").astype(F32)
        unit, scaling = unit_of(own_x[m].astype(F32))
        back = scaling * (
            total
            - jnp.mean(total, axis=-1, keepdims=True)
            - unit * jnp.mean(total * unit, axis=-1, keepdims=True)
        )
        return (own_g[m].astype(F32) + back).astype(BF)

    def output_rows():
        pending["rows"] = undeal(jnp.stack([output_of(0), output_of(1)]))

    def pair(key):
        return [env[f"{key}{m}"] for m in range(micros)]

    parity = (my_d % 2)[None]
    swap = [(i, i ^ 1) for i in range(n_d)]
    same_parity = [list(range(p, n_d, 2)) for p in range(2)]

    sides = {"w2": ("g", "act"), "w1": ("two", "pre"), "wq": ("one", "dqkv")}

    def sent_grads(key):
        def fn():
            lhs, rhs = (pair(side) for side in sides[key])
            sent = grad_of(1 - parity, lhs, rhs, n_d, f"grad_{key}_sent")
            env[f"{key}_got"] = lax.ppermute(sent, "dp", swap)

        return fn

    def sent_only(key):
        def fn():
            lhs, rhs = (pair(side) for side in sides[key])
            env[f"{key}_sent"] = grad_of(1 - parity, lhs, rhs, n_d, f"grad_{key}_sent")

        return fn

    def kept_grads(key):
        def fn():
            lhs, rhs = (pair(side) for side in sides[key])
            got = env.pop(f"{key}_got")
            env[f"{key}_pair"] = grad_of(parity, lhs, rhs, n_d, f"grad_{key}_kept", got)

        return fn

    def dense_grads():
        halves = head_grad_of(parity, pair("mixed"), pair("g"), n_d, "grad_dense")
        env["wd_sent"], env["wd_kept"] = (h.reshape(n_d // 2, -1, width) for h in halves)

    def swapped(key):
        def fn():
            env[f"{key}_got"] = lax.ppermute(env.pop(f"{key}_sent"), "dp", swap)

        return fn

    def spread(key):
        if f"{key}_pair" in env:
            pair_sums = env.pop(f"{key}_pair")
        else:
            pair_sums = env.pop(f"{key}_kept").astype(F32) + env.pop(f"{key}_got").astype(F32)
        return lax.all_to_all(
            pair_sums.astype(BF),
            "dp",
            split_axis=0,
            concat_axis=0,
            axis_index_groups=same_parity,
            tiled=True,
        )

    def summed(key):
        return jnp.sum(env.pop(key).astype(F32), axis=0)

    def fc2_final():
        env["grad_fc2"] = summed("w2").T

    def fc1_final():
        env["grad_fc1"] = summed("w1")

    def qkv_final():
        env["grad_qkv"] = summed("wq").reshape(-1, heads, 3 * HD)

    def dense_final():
        env["grad_dense"] = summed("wd").reshape(heads, -1, width)

    def steps_of(these, *plan):
        for i in range(these[0].steps()):
            stage(these, at(i, *plan))

    def gather_chain(name, x):
        chains[name] = GatherChain(after(x), "tensor", n_t)
        return chains[name]

    def deal_g():
        env["own_g1"] = deal(after(cotangent[1]))

    def spread_later(*keys):
        for key in keys:
            pending[key] = spread(key)

    def steps_of(these, *plan):
        for i in range(these[0].steps()):
            stage(these, at(i, *plan))

    steps_of(
        [gather_chain("x1", own_x[1]), gather_chain("g0", own_g[0])],
        [norm_qkv_of(0), hidden(0)],
        [attend_of(0), deal_g],
        [branch(0)],
    )
    own_g[1] = env.pop("own_g1")
    steps_of(
        [gather_chain("g1", own_g[1])],
        [norm_qkv_of(1)],
        [hidden(1), attend_of(1)],
        [branch(1), arrange_g(0)],
    )
    pending["so"] = scattered_rows("branch")
    stage([], [arrange_g(1), sent_grads("w2"), back_in(0)])
    stage([], [kept_grads("w2")])
    spread_later("w2")
    stage([], [back_attend(0), back_out(0), back_in(1), dense_grads, join("w2")])
    pending["si0"] = scattered_rows("e0")
    stage([], [sent_grads("w1"), swapped("wd"), back_attend(1)])
    spread_later("wd")
    stage([], [kept_grads("w1"), join("wd")])
    spread_later("w1")
    stage([], [sent_only("wq"), back_out(1), join("w1", "so")])
    pending["si1"] = scattered_rows("e1")
    output_rows()
    stage([], [swapped("wq"), fc2_final, kept_grads("wq"), join("rows")])
    spread_later("wq")
    sums = jnp.concatenate([env["sums0"] + env["sums1"], sum_g[None]], axis=0)
    sums = sums.reshape(5, n_d, n_t, eighth).transpose(1, 2, 0, 3).reshape(n_d, -1)
    qkvb = (env["bq0"] + env["bq1"]).reshape(heads, n_d, -1).transpose(1, 0, 2).reshape(n_d, -1)
    fc1b = (env["b10"] + env["b11"]).reshape(heads, n_d, -1).transpose(1, 0, 2).reshape(n_d, -1)
    small = jnp.concatenate([sums, qkvb, fc1b], axis=1)
    n_sum = 5 * n_t * eighth

    def small_over_dp():
        for s, pairs in enumerate(shifts(n_d), 1):
            sent = lax.dynamic_index_in_dim(small, (my_d + s) % n_d, 0, keepdims=False)
            env[f"small{s}"] = lax.ppermute(sent, "dp", pairs)
        env["small0"] = lax.dynamic_index_in_dim(small, my_d, 0, keepdims=False)

    def small_over_tensor():
        env["small"] = sum(env.pop(f"small{s}") for s in range(n_d))
        env["mine"] = direct_scatter(env["small"][:n_sum].reshape(n_t, -1), "tensor", n_t)

    stage([], [small_over_dp, fc1_final, dense_final, join("wq", "si0")])
    stage([], [join("si1")])
    grads_in = undeal(jnp.stack([input_of(0), input_of(1)]))
    small_over_tensor()
    qkv_final()
    small_out = env["small"]

    outputs = env["rows"]

    small = small_out
    mine = env["mine"].reshape(5, eighth)
    qkvb = small[n_sum : n_sum + n_qb].reshape(heads, -1)
    fc1b = small[n_sum + n_qb :].reshape(heads, -1)

    return (
        outputs,
        grads_in,
        mine[0],
        mine[1],
        mine[2],
        mine[3],
        env["grad_qkv"],
        qkvb,
        env["grad_dense"],
        mine[4],
        env["grad_fc1"],
        fc1b,
        env["grad_fc2"],
        mine[4],
    )


def solution(mesh):
    rows = P(None, None, ("dp", "tensor"), None)
    vector = P(("dp", "tensor"))
    return jax.shard_map(
        per_device,
        mesh=mesh,
        in_specs=(
            rows,
            P(),
            P(),
            rows,
            vector,
            vector,
            vector,
            vector,
            P("dp", "tensor", None),
            P("tensor", "dp"),
            P("tensor", "dp", None),
            vector,
            P("dp", "tensor"),
            P("tensor", "dp"),
            P("tensor", "dp"),
            vector,
        ),
        out_specs=(
            rows,
            rows,
            vector,
            vector,
            vector,
            vector,
            P("dp", "tensor", None),
            P("tensor", "dp"),
            P("tensor", "dp", None),
            vector,
            P("dp", "tensor"),
            P("tensor", "dp"),
            P("tensor", "dp"),
            vector,
        ),
        check_vma=False,
    )
```

```python
import functools
import math

import jax
import jax.numpy as jnp
from jax import lax
from jax.experimental import pallas as pl
from jax.experimental.pallas import tpu as pltpu
from jax.sharding import PartitionSpec as P

HD = 256
ROT = 64
EPSILON = 1e-05
ROPE_BASE = 10000.0
NEG_FILL = -1e30
SQRT_HALF = 0.7071067811865476
INV_ROOT_TWO_PI = 0.3989422804014327
BF = jnp.bfloat16
F32 = jnp.float32
FAR = 1 << 20
SHARE = 4096


class GatherChain:
    def __init__(self, x, axis, n):
        self.x, self.axis, self.n, self.step_no = x, axis, n, 0
        self.me = lax.axis_index(axis)
        self.left, self.right = [], []

    def steps(self):
        return self.n - 1

    def step(self):
        n = self.n
        s = self.step_no = self.step_no + 1
        to_right = self.left[-1] if self.left else self.x
        to_left = self.right[-1] if self.right else self.x
        pairs = [(k, k + 1) for k in range(s - 1, n - 1)]
        self.left.append(lax.ppermute(to_right, self.axis, pairs))
        pairs = [(k, k - 1) for k in range(1, n - s + 1)]
        self.right.append(lax.ppermute(to_left, self.axis, pairs))

    def live(self):
        return [self.left[-1], self.right[-1]]

    def set_live(self, values):
        self.left[-1], self.right[-1] = values


def shifts(n):
    return [[(k, (k + s) % n) for k in range(n)] for s in range(1, n)]


def direct_gather(x, axis, n):
    me = lax.axis_index(axis)
    got = jnp.stack([x] + [lax.ppermute(x, axis, pairs) for pairs in shifts(n)])
    order = (me - jnp.arange(n)) % n
    chosen = order[None, :] == jnp.arange(n)[:, None]
    return jnp.sum(jnp.where(chosen[:, :, None], got[None], 0), axis=1).astype(x.dtype)


def direct_scatter(x, axis, n):
    me = lax.axis_index(axis)
    total = lax.dynamic_index_in_dim(x, me, 0, keepdims=False)
    for s, pairs in enumerate(shifts(n), 1):
        sent = lax.dynamic_index_in_dim(x, (me + s) % n, 0, keepdims=False)
        total = total + lax.ppermute(sent, axis, pairs)
    return total


def rotated(x, cosines, sines):
    lanes = lax.broadcasted_iota(jnp.int32, x.shape, 1)
    partner = jnp.where(lanes < ROT // 2, pltpu.roll(x, 128 - ROT // 2, 1), pltpu.roll(x, ROT // 2, 1))
    return x * cosines + partner * sines


def scores_of(q, k, posq, posk):
    s = lax.dot_general(q, k, (((1,), (1,)), ((), ())), preferred_element_type=F32)
    return jnp.where(posk <= posq, s * (1.0 / math.sqrt(HD)), NEG_FILL)


def attend_kernel(n_blocks, posq_ref, posk_ref, cos_ref, sin_ref, qkv_ref, low_ref, mixed_ref):
    n_slots, rows, _ = qkv_ref.shape
    span = rows // n_blocks
    for t in range(n_slots):
        for base in (0, HD):
            lead = rotated(qkv_ref[t, :, base : base + 128], cos_ref[t], sin_ref[t])
            low_ref[t, :, base : base + 128] = lead.astype(BF)
            low_ref[t, :, base + 128 : base + HD] = qkv_ref[t, :, base + 128 : base + HD].astype(BF)
        low_ref[t, :, 2 * HD :] = qkv_ref[t, :, 2 * HD :].astype(BF)
    for b in range(n_blocks):
        own, seen = pl.ds(b * span, span), span * (b + 1)
        n_q, n_k = n_slots * span, n_slots * seen
        q = low_ref[:, own, :HD].reshape(n_q, HD)
        k = low_ref[:, :seen, HD : 2 * HD].reshape(n_k, HD)
        v = low_ref[:, :seen, 2 * HD :].reshape(n_k, HD)
        posq = posq_ref[:, own, :].reshape(n_q, 1)
        s = scores_of(q, k, posq, posk_ref[b, :, :n_k])
        e = jnp.exp(s - jnp.max(s, axis=-1, keepdims=True))
        p = e * (1.0 / jnp.sum(e, axis=-1, keepdims=True))
        mixed = jnp.dot(p.astype(BF), v, preferred_element_type=F32)
        mixed_ref[:, own, :] = mixed.astype(BF).reshape(n_slots, span, HD)


def attend_back_kernel(
    n_blocks,
    posq_ref,
    posk_ref,
    cos_ref,
    sin_ref,
    low_ref,
    dmix_ref,
    grad_ref,
    bias_ref,
    dk_ref,
    dv_ref,
):
    n_slots, rows, _ = low_ref.shape
    span = rows // n_blocks
    scale = 1.0 / math.sqrt(HD)
    for b in reversed(range(n_blocks)):
        own, seen = pl.ds(b * span, span), span * (b + 1)
        n_q, n_k = n_slots * span, n_slots * seen
        q = low_ref[:, own, :HD].reshape(n_q, HD)
        k = low_ref[:, :seen, HD : 2 * HD].reshape(n_k, HD)
        v = low_ref[:, :seen, 2 * HD :].reshape(n_k, HD)
        dmix = dmix_ref[:, own, :].reshape(n_q, HD)
        posq = posq_ref[:, own, :].reshape(n_q, 1)
        s = scores_of(q, k, posq, posk_ref[b, :, :n_k])
        e = jnp.exp(s - jnp.max(s, axis=-1, keepdims=True))
        p = e * (1.0 / jnp.sum(e, axis=-1, keepdims=True))
        dp = lax.dot_general(dmix, v, (((1,), (1,)), ((), ())), preferred_element_type=F32)
        ds = (p * (dp - jnp.sum(p * dp, axis=-1, keepdims=True))).astype(BF)
        dq = jnp.dot(ds, k, preferred_element_type=F32) * scale
        dk = lax.dot_general(ds, q, (((0,), (0,)), ((), ())), preferred_element_type=F32)
        dv = lax.dot_general(p.astype(BF), dmix, (((0,), (0,)), ((), ())), preferred_element_type=F32)
        dk, dv = dk.reshape(n_slots, seen, HD), dv.reshape(n_slots, seen, HD)
        if b == n_blocks - 1:
            dk_ref[...] = dk
            dv_ref[...] = dv
        else:
            dk_ref[:, :seen, :] += dk
            dv_ref[:, :seen, :] += dv
        dq = dq.reshape(n_slots, span, HD)
        for t in range(n_slots):
            lead = rotated(dq[t, :, :128], cos_ref[t, own, :], -sin_ref[t, own, :])
            grad_ref[t, own, :128] = lead.astype(BF)
            grad_ref[t, own, 128:HD] = dq[t, :, 128:].astype(BF)
    for t in range(n_slots):
        lead = rotated(dk_ref[t, :, :128] * scale, cos_ref[t], -sin_ref[t])
        grad_ref[t, :, HD : HD + 128] = lead.astype(BF)
        grad_ref[t, :, HD + 128 : 2 * HD] = (dk_ref[t, :, 128:] * scale).astype(BF)
        grad_ref[t, :, 2 * HD :] = dv_ref[t].astype(BF)
        summed = jnp.sum(grad_ref[t].astype(F32), axis=0, keepdims=True)
        bias_ref[0] = summed if t == 0 else bias_ref[0] + summed


def whole_spec(shape):
    return pl.BlockSpec(shape, lambda h: (0,) * len(shape))


def head_spec(n_slots, rows, width):
    return pl.BlockSpec((n_slots, rows, width), lambda h: (0, 0, h))


def attend(tables, qkv):
    posq, posk, cosines, sines = tables
    n_slots, rows, width = qkv.shape
    heads = width // (3 * HD)
    pairs = (n_slots * rows) ** 2 // 2 * heads
    return pl.pallas_call(
        functools.partial(attend_kernel, posk.shape[0]),
        grid=(heads,),
        in_specs=[whole_spec(t.shape) for t in tables] + [head_spec(n_slots, rows, 3 * HD)],
        out_specs=[head_spec(n_slots, rows, 3 * HD), head_spec(n_slots, rows, HD)],
        out_shape=[
            jax.ShapeDtypeStruct(qkv.shape, BF),
            jax.ShapeDtypeStruct((n_slots, rows, heads * HD), BF),
        ],
        cost_estimate=pl.CostEstimate(
            flops=4 * pairs * HD, bytes_accessed=qkv.size * 8, transcendentals=pairs
        ),
        compiler_params=pltpu.CompilerParams(vmem_limit_bytes=48 << 20),
        name="attend",
    )(posq, posk, cosines, sines, qkv)


def attend_back(tables, low, dmix):
    n_slots, rows, width = low.shape
    heads = width // (3 * HD)
    pairs = (n_slots * rows) ** 2 // 2 * heads
    return pl.pallas_call(
        functools.partial(attend_back_kernel, tables[1].shape[0]),
        grid=(heads,),
        in_specs=[whole_spec(t.shape) for t in tables]
        + [head_spec(n_slots, rows, 3 * HD), head_spec(n_slots, rows, HD)],
        out_specs=[
            head_spec(n_slots, rows, 3 * HD),
            pl.BlockSpec((1, 1, 3 * HD), lambda h: (h, 0, 0)),
        ],
        out_shape=[
            jax.ShapeDtypeStruct(low.shape, BF),
            jax.ShapeDtypeStruct((heads, 1, 3 * HD), F32),
        ],
        scratch_shapes=[pltpu.VMEM((n_slots, rows, HD), F32)] * 2,
        cost_estimate=pl.CostEstimate(
            flops=10 * pairs * HD, bytes_accessed=low.size * 5, transcendentals=pairs
        ),
        compiler_params=pltpu.CompilerParams(vmem_limit_bytes=48 << 20),
        name="attend_back",
    )(*tables, low, dmix)


def slot_rows(blocks, s):
    n = (len(blocks) + 1) // 2
    if s == 0:
        return blocks[0][...].astype(F32)
    return blocks[s][...].astype(F32) + blocks[2 * n - 1 - s][...].astype(F32)


def part_of(me_ref, s):
    return lax.rem(me_ref[0] - s + me_ref[1], me_ref[1])


def cdf_and_slope(x):
    size = jnp.abs(x)
    bell = jnp.exp(-0.5 * x * x)
    t = 1.0 / (1.0 + (0.3275911 * SQRT_HALF) * size)
    poly = ((((1.061405429 * t - 1.453152027) * t) + 1.421413741) * t - 0.284496736) * t + 0.254829592
    tail = 0.5 * poly * t * bell
    cdf = jnp.where(x >= 0, 1.0 - tail, tail)
    return cdf, cdf + x * bell * INV_ROOT_TWO_PI


def norm_qkv_kernel(n_blocks, me_ref, vectors_ref, bias_ref, *refs):
    blocks, w_hbm = refs[:n_blocks], refs[n_blocks]
    one_ref, two_ref, unit_ref, qkv_ref, w_ref, sem = refs[n_blocks + 1 :]
    n_slots, block, width = one_ref.shape
    n_qkv = w_ref.shape[1]
    first = pl.program_id(0) == 0
    copy = pltpu.make_async_copy(w_hbm.at[:, pl.ds(0, n_qkv)], w_ref, sem)

    @pl.when(first)
    def _():
        copy.start()

    for s in range(n_slots):
        rows = slot_rows(blocks, s)
        centred = rows - jnp.mean(rows, axis=-1, keepdims=True)
        unit = centred * lax.rsqrt(jnp.mean(centred * centred, axis=-1, keepdims=True) + EPSILON)
        part = part_of(me_ref, s)
        one_ref[part] = (unit * vectors_ref[0:1] + vectors_ref[1:2]).astype(BF)
        two_ref[part] = (unit * vectors_ref[2:3] + vectors_ref[3:4]).astype(BF)
        unit_ref[part] = unit.astype(BF)

    @pl.when(first)
    def _():
        copy.wait()

    one = one_ref[...].reshape(n_slots * block, width)
    tile = 768
    for c in range(0, n_qkv, tile):
        out = jnp.dot(one, w_ref[:, c : c + tile], preferred_element_type=F32)
        out = out + bias_ref[:, c : c + tile]
        qkv_ref[:, :, c : c + tile] = out.reshape(n_slots, block, tile)


def hidden_kernel(two_ref, w_ref, bias_ref, act_ref, slope_ref):
    pre = jnp.dot(two_ref[...], w_ref[...], preferred_element_type=F32) + bias_ref[...]
    cdf, slope = cdf_and_slope(pre)
    act_ref[...] = (pre * cdf).astype(BF)
    slope_ref[...] = slope.astype(BF)


def big(limit=56):
    return pltpu.CompilerParams(vmem_limit_bytes=limit << 20)


def cost(flops, moved, special=0):
    return pl.CostEstimate(
        flops=int(flops) // SHARE,
        bytes_accessed=int(moved) // SHARE,
        transcendentals=int(special) // SHARE,
    )


def norm_qkv(chain, vectors, bias, w, n_qkv):
    n = chain.n
    rows, width = chain.x.shape
    block = 64
    me = jnp.stack([chain.me, jnp.int32(n)])
    blocks = [chain.x] + chain.left + chain.right

    def out(cols, dtype):
        return (
            jax.ShapeDtypeStruct((n, rows, cols), dtype),
            pl.BlockSpec((n, block, cols), lambda i, me: (0, i, 0)),
        )

    shapes, specs = zip(out(width, BF), out(width, BF), out(width, BF), out(n_qkv, F32))
    total = n * rows
    return pl.pallas_call(
        functools.partial(norm_qkv_kernel, len(blocks)),
        grid_spec=pltpu.PrefetchScalarGridSpec(
            num_scalar_prefetch=1,
            grid=(rows // block,),
            in_specs=[
                pl.BlockSpec(vectors.shape, lambda i, me: (0, 0)),
                pl.BlockSpec(bias.shape, lambda i, me: (0, 0)),
            ]
            + [pl.BlockSpec((block, width), lambda i, me: (i, 0))] * len(blocks)
            + [pl.BlockSpec(memory_space=pl.ANY)],
            out_specs=list(specs),
            scratch_shapes=[pltpu.VMEM((width, n_qkv), BF), pltpu.SemaphoreType.DMA],
        ),
        out_shape=list(shapes),
        cost_estimate=cost(2 * total * width * n_qkv, 10 * total * width + width * n_qkv * 2),
        compiler_params=big(),
        name="norm_qkv",
    )(me, vectors, bias, *blocks, w)


def hidden_of(two, w, bias, n_qkv):
    total, width = two.shape
    n_ff, tile = w.shape[1] - n_qkv, 256
    skip = n_qkv // tile
    columns = pl.BlockSpec((total, tile), lambda j: (0, j))
    return pl.pallas_call(
        hidden_kernel,
        grid=(n_ff // tile,),
        in_specs=[
            resident(two.shape),
            pl.BlockSpec((width, tile), lambda j: (0, j + skip)),
            pl.BlockSpec((1, tile), lambda j: (0, j + skip)),
        ],
        out_specs=[columns, columns],
        out_shape=[jax.ShapeDtypeStruct((total, n_ff), BF)] * 2,
        cost_estimate=cost(2 * total * width * n_ff, 2 * width * n_ff + 8 * total * n_ff, total * n_ff),
        compiler_params=big(),
        name="hidden",
    )(two, w, bias)


def arrange_kernel(me_ref, *refs):
    blocks, out_ref = refs[:-1], refs[-1]
    n = (len(blocks) + 1) // 2
    for s in range(n):
        part = part_of(me_ref, s)
        if s == 0:
            out_ref[part] = blocks[0][...]
        else:
            out_ref[part] = blocks[s][...] + blocks[2 * n - 1 - s][...]


def arrange(chain):
    n = chain.n
    rows, width = chain.x.shape
    block = 64
    me = jnp.stack([chain.me, jnp.int32(n)])
    blocks = [chain.x] + chain.left + chain.right
    return pl.pallas_call(
        arrange_kernel,
        grid_spec=pltpu.PrefetchScalarGridSpec(
            num_scalar_prefetch=1,
            grid=(rows // block,),
            in_specs=[pl.BlockSpec((block, width), lambda i, me: (i, 0))] * len(blocks),
            out_specs=pl.BlockSpec((n, block, width), lambda i, me: (0, i, 0)),
        ),
        out_shape=jax.ShapeDtypeStruct((n, rows, width), BF),
        cost_estimate=cost(0, 6 * n * rows * width),
        compiler_params=big(),
        name="arrange",
    )(me, *blocks)


def nt(a, b):
    return lax.dot_general(a, b, (((1,), (1,)), ((), ())), preferred_element_type=F32)


def tn(a, b):
    return lax.dot_general(a, b, (((0,), (0,)), ((), ())), preferred_element_type=F32)


def resident(shape):
    return pl.BlockSpec(shape, lambda j: (0,) * len(shape), pipeline_mode=pl.Buffered(1))


def head_rows(dense_ref, h):
    n, _, e, cols = dense_ref.shape
    return dense_ref[:, h].reshape(n * e, cols)


def branch_kernel(mixed_ref, act_ref, dense_ref, w_ref, *refs):
    out_ref = refs[-1]
    total = nt(act_ref[...], w_ref[...])
    for h in range(dense_ref.shape[1]):
        total += jnp.dot(
            mixed_ref[:, h * HD : (h + 1) * HD],
            head_rows(dense_ref, h),
            preferred_element_type=F32,
        )
    out_ref[...] = total.astype(BF).reshape(out_ref.shape)


def branch_of(mixed, act, dense, w_fc2, slot, shape, before=None):
    total, width, tile = act.shape[0], w_fc2.shape[0], 512
    parts, _, rows, _ = shape
    return pl.pallas_call(
        branch_kernel,
        grid=(width // tile,),
        in_specs=[
            resident(mixed.shape),
            resident(act.shape),
            pl.BlockSpec(dense.shape[:3] + (tile,), lambda j: (0, 0, 0, j)),
            pl.BlockSpec((tile, w_fc2.shape[1]), lambda j: (j, 0)),
        ]
        + ([] if before is None else [pl.BlockSpec(memory_space=pl.ANY)]),
        out_specs=pl.BlockSpec((parts, 1, rows, tile), lambda j: (0, slot, 0, j)),
        out_shape=jax.ShapeDtypeStruct(shape, BF),
        input_output_aliases={} if before is None else {4: 0},
        cost_estimate=cost(2 * total * (dense.size + w_fc2.size), 2 * (act.size * 3 + w_fc2.size)),
        compiler_params=big(),
        name="branch",
    )(mixed, act, dense, w_fc2, *([] if before is None else [before]))


def back_in_kernel(g_ref, dense_ref, w_ref, slope_ref, dmix_ref, pre_ref, bias_ref):
    @pl.when(pl.program_id(0) == 0)
    def _():
        for h in range(dense_ref.shape[1]):
            dmix_ref[:, h * HD : (h + 1) * HD] = nt(g_ref[...], head_rows(dense_ref, h)).astype(BF)

    d_act = jnp.dot(g_ref[...], w_ref[...], preferred_element_type=F32)
    d_pre = (d_act * slope_ref[...].astype(F32)).astype(BF)
    pre_ref[...] = d_pre
    bias_ref[...] = jnp.sum(d_pre.astype(F32), axis=0, keepdims=True)


def back_in_of(g, dense, w_fc2, slope):
    total, width = g.shape
    n_ff, tile = w_fc2.shape[1], 512
    heads = dense.shape[1]
    columns = pl.BlockSpec((total, tile), lambda j: (0, j))
    return pl.pallas_call(
        back_in_kernel,
        grid=(n_ff // tile,),
        in_specs=[
            resident(g.shape),
            resident(dense.shape),
            pl.BlockSpec((width, tile), lambda j: (0, j)),
            columns,
        ],
        out_specs=[
            pl.BlockSpec((total, heads * HD), lambda j: (0, 0)),
            columns,
            pl.BlockSpec((1, tile), lambda j: (0, j)),
        ],
        out_shape=[
            jax.ShapeDtypeStruct((total, heads * HD), BF),
            jax.ShapeDtypeStruct((total, n_ff), BF),
            jax.ShapeDtypeStruct((1, n_ff), F32),
        ],
        cost_estimate=cost(2 * total * (dense.size + w_fc2.size), 2 * (g.size * 3 + w_fc2.size)),
        compiler_params=big(),
        name="back_in",
    )(g, dense, w_fc2, slope)


def back_out_kernel(vectors_ref, dqkv_ref, pre_ref, w_ref, unit_ref, e_ref, sums_ref):
    n_qkv = dqkv_ref.shape[1]
    one = nt(dqkv_ref[...], w_ref[:, :n_qkv])
    two = nt(pre_ref[...], w_ref[:, n_qkv:])
    unit = unit_ref[...].astype(F32)
    e_ref[...] = (one * vectors_ref[0:1] + two * vectors_ref[2:3]).astype(BF)
    sums_ref[0:1] = jnp.sum(one * unit, axis=0, keepdims=True)
    sums_ref[1:2] = jnp.sum(one, axis=0, keepdims=True)
    sums_ref[2:3] = jnp.sum(two * unit, axis=0, keepdims=True)
    sums_ref[3:4] = jnp.sum(two, axis=0, keepdims=True)


def back_out_of(vectors, dqkv, pre, w, unit):
    total, width = unit.shape
    tile = 256
    columns = pl.BlockSpec((total, tile), lambda j: (0, j))
    return pl.pallas_call(
        back_out_kernel,
        grid=(width // tile,),
        in_specs=[
            pl.BlockSpec((vectors.shape[0], tile), lambda j: (0, j)),
            resident(dqkv.shape),
            resident(pre.shape),
            pl.BlockSpec((tile, w.shape[1]), lambda j: (j, 0)),
            columns,
        ],
        out_specs=[columns, pl.BlockSpec((4, tile), lambda j: (0, j))],
        out_shape=[
            jax.ShapeDtypeStruct((total, width), BF),
            jax.ShapeDtypeStruct((4, width), F32),
        ],
        cost_estimate=cost(2 * total * w.size, 2 * (unit.size * 4 + w.size)),
        compiler_params=big(),
        name="back_out",
    )(vectors, dqkv, pre, w, unit)


def grad_kernel(count, me_ref, *refs):
    lhs, rhs, out_ref = refs[:count], refs[count : 2 * count], refs[-1]
    total = tn(lhs[0][...], rhs[0][...])
    for a, b in zip(lhs[1:], rhs[1:]):
        total += tn(a[...], b[...])
    if len(refs) > 2 * count + 1:
        total += refs[2 * count][0].astype(F32)
    out_ref[0] = total.astype(BF)


def grad_of(parity, lhs, rhs, cuts, name, got=None):
    total, m = lhs[0].shape
    n, tile, half = rhs[0].shape[1], m // cuts, cuts // 2
    block = pl.BlockSpec((1, tile, n), lambda j, me: (j, 0, 0))
    return pl.pallas_call(
        functools.partial(grad_kernel, len(lhs)),
        grid_spec=pltpu.PrefetchScalarGridSpec(
            num_scalar_prefetch=1,
            grid=(half,),
            in_specs=[pl.BlockSpec((total, tile), lambda j, me: (0, 2 * j + me[0]))] * len(lhs)
            + [
                pl.BlockSpec(r.shape, lambda j, me: (0, 0), pipeline_mode=pl.Buffered(1))
                for r in rhs
            ]
            + ([] if got is None else [block]),
            out_specs=block,
        ),
        out_shape=jax.ShapeDtypeStruct((half, tile, n), BF),
        cost_estimate=cost(len(lhs) * total * m * n, 4 * total * (m + n) + 2 * m * n),
        compiler_params=big(),
        name=name,
    )(parity, *lhs, *rhs, *([] if got is None else [got]))


def head_grad_kernel(count, me_ref, *refs):
    lhs, rhs, (sent_ref, kept_ref) = refs[:count], refs[count : 2 * count], refs[-2:]
    total = tn(lhs[0][...], rhs[0][...])
    for a, b in zip(lhs[1:], rhs[1:]):
        total += tn(a[...], b[...])
    half, _, e, n = sent_ref.shape
    total = total.astype(BF).reshape(half, 2, e, n)
    even = me_ref[0] == 0
    kept_ref[:, 0] = jnp.where(even, total[:, 0], total[:, 1])
    sent_ref[:, 0] = jnp.where(even, total[:, 1], total[:, 0])


def head_grad_of(parity, lhs, rhs, cuts, name):
    total, m = lhs[0].shape
    n, e = rhs[0].shape[1], HD // cuts
    shape = jax.ShapeDtypeStruct((cuts // 2, m // HD, e, n), BF)
    return pl.pallas_call(
        functools.partial(head_grad_kernel, len(lhs)),
        grid_spec=pltpu.PrefetchScalarGridSpec(
            num_scalar_prefetch=1,
            grid=(m // HD,),
            in_specs=[pl.BlockSpec((total, HD), lambda j, me: (0, j))] * len(lhs)
            + [
                pl.BlockSpec(r.shape, lambda j, me: (0, 0), pipeline_mode=pl.Buffered(1))
                for r in rhs
            ],
            out_specs=[pl.BlockSpec((cuts // 2, 1, e, n), lambda j, me: (0, j, 0, 0))] * 2,
        ),
        out_shape=[shape, shape],
        cost_estimate=cost(2 * len(lhs) * total * m * n, 4 * total * (m + n) + 2 * m * n),
        compiler_params=big(),
        name=name,
    )(parity, *lhs, *rhs)


def unit_of(rows):
    centred = rows - jnp.mean(rows, axis=-1, keepdims=True)
    scaling = lax.rsqrt(jnp.mean(centred * centred, axis=-1, keepdims=True) + EPSILON)
    return centred * scaling, scaling


def per_device(
    hidden_in,
    lengths,
    dealing,
    cotangent,
    attn_gain,
    attn_shift,
    ffn_gain,
    ffn_shift,
    qkv_weight,
    qkv_bias,
    dense_weight,
    dense_bias,
    fc1_weight,
    fc1_bias,
    fc2_weight,
    fc2_bias,
):
    n_t, n_d = lax.axis_size("tensor"), lax.axis_size("dp")
    my_t, my_d = lax.axis_index("tensor"), lax.axis_index("dp")
    micros, seqs, piece, width = hidden_in.shape
    heads = qkv_weight.shape[1]
    rows = n_d * piece
    n_blocks = 4

    def deal(x):
        return lax.all_to_all(x, "dp", split_axis=0, concat_axis=0, tiled=True).reshape(rows, width)

    def undeal(x):
        x = x.reshape(x.shape[0], seqs, piece, width)
        return lax.all_to_all(x, "dp", split_axis=1, concat_axis=1, tiled=True)

    env = {}

    def stage(chains, computes=()):
        for chain in chains:
            chain.step()
        for fn in computes:
            fn()
        keys = list(env)
        values = [env[k] for k in keys]
        for chain in chains:
            values += chain.live()
        out = list(lax.optimization_barrier(tuple(values)))
        env.update(zip(keys, out))
        at = len(keys)
        for chain in chains:
            count = len(chain.live())
            chain.set_live(out[at : at + count])
            at += count

    def after(x):
        return lax.optimization_barrier((x, env["mark"]))[0]

    eighth = width // (n_d * n_t)
    n_six = 6 * eighth
    env["x0"] = deal(hidden_in[0])
    env["mark"] = jnp.concatenate(
        [attn_gain, attn_shift, ffn_gain, ffn_shift, dense_bias, fc2_bias]
        + [qkv_bias.reshape(-1), fc1_bias.reshape(-1)]
    )
    n_qkv = heads * 3 * HD
    env["near"] = jnp.concatenate([qkv_weight.reshape(-1, n_qkv), fc1_weight], axis=1)
    stage([])

    w_near = lax.all_gather(env.pop("near"), "dp", axis=0, tiled=True)

    parts = jnp.arange(n_t, dtype=jnp.int32)
    local = jnp.arange(rows, dtype=jnp.int32)
    positions = ((local // piece) * n_t + parts[:, None]) * piece + local % piece
    freqs = jnp.exp(jnp.arange(ROT // 2, dtype=F32) * (-2.0 * math.log(ROPE_BASE) / ROT))
    phases = positions.astype(F32)[..., None] * freqs
    flat = jnp.zeros((n_t, rows, 128 - ROT), F32)
    cosines = jnp.concatenate([jnp.cos(phases), jnp.cos(phases), flat + 1.0], axis=-1)
    sines = jnp.concatenate([-jnp.sin(phases), jnp.sin(phases), flat], axis=-1)
    picked = dealing == my_d
    seq_lens = jnp.sum(jnp.where(picked, lengths, 0), axis=1)
    posq = positions[..., None]

    def tables(m):
        keyed = jnp.where(positions < seq_lens[m], positions, FAR)
        span = rows // n_blocks
        lists = []
        for b in range(n_blocks):
            seen = keyed[:, : span * (b + 1)].reshape(1, -1)
            lists.append(jnp.pad(seen, ((0, 0), (0, n_t * rows - seen.shape[1]))))
        return (posq, jnp.stack(lists), cosines, sines)

    all_tables = [tables(m) for m in range(micros)]
    sum_g = jnp.sum(cotangent.astype(F32), axis=(0, 1, 2))

    chains = {"x0": GatherChain(env["x0"], "tensor", n_t)}
    pending = {}

    def join(*keys):
        def fn():
            for key in keys:
                env[key] = pending.pop(key)

        return fn

    def vectors_over_dp():
        env["small"] = direct_gather(env["mark"], "dp", n_d)

    def vectors_over_tensor():
        six = env["small"][:, :n_six].reshape(-1)
        env["six"] = direct_gather(six, "tensor", n_t)

    def vectors_whole():
        vectors = env.pop("six").reshape(n_t, n_d, 6, eighth).transpose(2, 1, 0, 3)
        env["vectors"] = vectors.reshape(6, width).astype(F32)
        rest = env.pop("small")[:, n_six:].astype(F32)
        n_qb = qkv_bias.size
        env["bias"] = jnp.concatenate(
            [
                rest[:, :n_qb].reshape(n_d, heads, -1).transpose(1, 0, 2).reshape(1, -1),
                rest[:, n_qb:].reshape(n_d, heads, -1).transpose(1, 0, 2).reshape(1, -1),
            ],
            axis=1,
        )

    def stack_two():
        env["two"] = jnp.stack([after(hidden_in[1]), cotangent[0]])

    def deal_two():
        stacked = env.pop("two")
        pending["two"] = lax.all_to_all(stacked, "dp", split_axis=1, concat_axis=1, tiled=True)

    last = n_t - 2

    def at(i, *plan):
        if i < last:
            return list(plan[i]) if i < len(plan) else []
        return [fn for entry in plan[i:] for fn in entry]

    for i in range(n_t - 1):
        stage(
            [chains["x0"]],
            at(i, [vectors_over_dp, stack_two], [vectors_over_tensor, deal_two], [vectors_whole, join("two")]),
        )
    w_fc2 = lax.all_gather(after(fc2_weight.T), "dp", axis=0, tiled=True)
    w_dense = lax.all_gather(after(dense_weight), "dp", axis=0, tiled=False)
    two = env.pop("two").reshape(2, rows, width)
    own_x, own_g = [env.pop("x0"), two[0]], [two[1], None]
    env["mark"] = vectors = env.pop("vectors")
    out_shift = vectors[4] + vectors[5]
    n_qb = qkv_bias.size

    def norm_qkv_of(m):
        def fn():
            outs = norm_qkv(chains[f"x{m}"], env["mark"], env["bias"], w_near, n_qkv)
            for key, value in zip(("one", "two", "unit", "qkv"), outs):
                env[f"{key}{m}"] = value if key == "qkv" else value.reshape(n_t * rows, -1)

        return fn

    def hidden(m):
        def fn():
            env[f"act{m}"], env[f"slope{m}"] = hidden_of(
                env[f"two{m}"], w_near, env["bias"], n_qkv
            )

        return fn

    def attend_of(m):
        def fn():
            low, mixed = attend(all_tables[m], env.pop(f"qkv{m}"))
            env[f"low{m}"], env[f"mixed{m}"] = low, mixed.reshape(n_t * rows, -1)

        return fn

    def branch(m):
        def fn():
            env["branch"] = branch_of(
                env[f"mixed{m}"],
                env[f"act{m}"],
                w_dense,
                w_fc2,
                m,
                (n_t, micros, rows, width),
                env.get("branch"),
            )

        return fn

    def scattered_rows(name):
        terms = env.pop(name).reshape(-1, width)
        return lax.psum_scatter(terms, "tensor", scatter_dimension=0, tiled=True)

    def output_of(m):
        total = env["so"].reshape(micros, rows, width)[m].astype(F32)
        return (own_x[m].astype(F32) + total + out_shift).astype(BF)

    def arrange_g(m):
        def fn():
            env[f"g{m}"] = arrange(chains[f"g{m}"]).reshape(n_t * rows, width)

        return fn

    def back_in(m):
        def fn():
            if f"g{m}" not in env:
                arrange_g(m)()
            dmix, env[f"pre{m}"], env[f"b1{m}"] = back_in_of(
                env[f"g{m}"], w_dense, w_fc2, env.pop(f"slope{m}")
            )
            env[f"dmix{m}"] = dmix.reshape(n_t, rows, -1)

        return fn

    def back_attend(m):
        def fn():
            d_qkv, env[f"bq{m}"] = attend_back(
                all_tables[m], env.pop(f"low{m}"), env.pop(f"dmix{m}")
            )
            env[f"dqkv{m}"] = d_qkv.reshape(n_t * rows, -1)

        return fn

    def back_out(m):
        def fn():
            env[f"e{m}"], env[f"sums{m}"] = back_out_of(
                env["mark"], env[f"dqkv{m}"], env[f"pre{m}"], w_near, env.pop(f"unit{m}")
            )

        return fn

    def input_of(m):
        total = env.pop(f"si{m}").astype(F32)
        unit, scaling = unit_of(own_x[m].astype(F32))
        back = scaling * (
            total
            - jnp.mean(total, axis=-1, keepdims=True)
            - unit * jnp.mean(total * unit, axis=-1, keepdims=True)
        )
        return (own_g[m].astype(F32) + back).astype(BF)

    def output_rows():
        pending["rows"] = undeal(jnp.stack([output_of(0), output_of(1)]))

    def pair(key):
        return [env[f"{key}{m}"] for m in range(micros)]

    parity = (my_d % 2)[None]
    swap = [(i, i ^ 1) for i in range(n_d)]
    same_parity = [list(range(p, n_d, 2)) for p in range(2)]

    sides = {"w2": ("g", "act"), "w1": ("two", "pre"), "wq": ("one", "dqkv")}

    def sent_grads(key):
        def fn():
            lhs, rhs = (pair(side) for side in sides[key])
            sent = grad_of(1 - parity, lhs, rhs, n_d, f"grad_{key}_sent")
            env[f"{key}_got"] = lax.ppermute(sent, "dp", swap)

        return fn

    def sent_only(key):
        def fn():
            lhs, rhs = (pair(side) for side in sides[key])
            env[f"{key}_sent"] = grad_of(1 - parity, lhs, rhs, n_d, f"grad_{key}_sent")

        return fn

    def kept_grads(key):
        def fn():
            lhs, rhs = (pair(side) for side in sides[key])
            got = env.pop(f"{key}_got")
            env[f"{key}_pair"] = grad_of(parity, lhs, rhs, n_d, f"grad_{key}_kept", got)

        return fn

    def dense_grads():
        halves = head_grad_of(parity, pair("mixed"), pair("g"), n_d, "grad_dense")
        env["wd_sent"], env["wd_kept"] = (h.reshape(n_d // 2, -1, width) for h in halves)

    def swapped(key):
        def fn():
            env[f"{key}_got"] = lax.ppermute(env.pop(f"{key}_sent"), "dp", swap)

        return fn

    def spread(key):
        if f"{key}_pair" in env:
            pair_sums = env.pop(f"{key}_pair")
        else:
            pair_sums = env.pop(f"{key}_kept").astype(F32) + env.pop(f"{key}_got").astype(F32)
        return lax.all_to_all(
            pair_sums.astype(BF),
            "dp",
            split_axis=0,
            concat_axis=0,
            axis_index_groups=same_parity,
            tiled=True,
        )

    def summed(key):
        return jnp.sum(env.pop(key).astype(F32), axis=0)

    def fc2_final():
        env["grad_fc2"] = summed("w2").T

    def fc1_final():
        env["grad_fc1"] = summed("w1")

    def qkv_final():
        env["grad_qkv"] = summed("wq").reshape(-1, heads, 3 * HD)

    def dense_final():
        env["grad_dense"] = summed("wd").reshape(heads, -1, width)

    def steps_of(these, *plan):
        for i in range(these[0].steps()):
            stage(these, at(i, *plan))

    def gather_chain(name, x):
        chains[name] = GatherChain(after(x), "tensor", n_t)
        return chains[name]

    def deal_g():
        env["own_g1"] = deal(after(cotangent[1]))

    def spread_later(*keys):
        for key in keys:
            pending[key] = spread(key)

    def steps_of(these, *plan):
        for i in range(these[0].steps()):
            stage(these, at(i, *plan))

    steps_of(
        [gather_chain("x1", own_x[1]), gather_chain("g0", own_g[0])],
        [norm_qkv_of(0), hidden(0)],
        [attend_of(0), deal_g],
        [branch(0)],
    )
    own_g[1] = env.pop("own_g1")
    steps_of(
        [gather_chain("g1", own_g[1])],
        [norm_qkv_of(1)],
        [hidden(1), attend_of(1)],
        [branch(1), arrange_g(0)],
    )
    pending["so"] = scattered_rows("branch")
    stage([], [arrange_g(1), sent_grads("w2"), back_in(0)])
    stage([], [kept_grads("w2")])
    spread_later("w2")
    stage([], [back_attend(0), back_out(0), back_in(1), dense_grads, join("w2")])
    pending["si0"] = scattered_rows("e0")
    stage([], [sent_grads("w1"), swapped("wd"), back_attend(1)])
    spread_later("wd")
    stage([], [kept_grads("w1"), join("wd")])
    spread_later("w1")
    stage([], [sent_only("wq"), back_out(1), join("w1", "so")])
    pending["si1"] = scattered_rows("e1")
    output_rows()
    stage([], [swapped("wq"), fc2_final, kept_grads("wq"), join("rows")])
    spread_later("wq")
    sums = jnp.concatenate([env["sums0"] + env["sums1"], sum_g[None]], axis=0)
    sums = sums.reshape(5, n_d, n_t, eighth).transpose(1, 2, 0, 3).reshape(n_d, -1)
    qkvb = (env["bq0"] + env["bq1"]).reshape(heads, n_d, -1).transpose(1, 0, 2).reshape(n_d, -1)
    fc1b = (env["b10"] + env["b11"]).reshape(heads, n_d, -1).transpose(1, 0, 2).reshape(n_d, -1)
    small = jnp.concatenate([sums, qkvb, fc1b], axis=1)
    n_sum = 5 * n_t * eighth

    def small_over_dp():
        for s, pairs in enumerate(shifts(n_d), 1):
            sent = lax.dynamic_index_in_dim(small, (my_d + s) % n_d, 0, keepdims=False)
            env[f"small{s}"] = lax.ppermute(sent, "dp", pairs)
        env["small0"] = lax.dynamic_index_in_dim(small, my_d, 0, keepdims=False)

    def small_over_tensor():
        env["small"] = sum(env.pop(f"small{s}") for s in range(n_d))
        env["mine"] = direct_scatter(env["small"][:n_sum].reshape(n_t, -1), "tensor", n_t)

    stage([], [small_over_dp, fc1_final, dense_final, join("wq", "si0")])
    stage([], [join("si1")])
    grads_in = undeal(jnp.stack([input_of(0), input_of(1)]))
    small_over_tensor()
    qkv_final()
    small_out = env["small"]

    outputs = env["rows"]

    small = small_out
    mine = env["mine"].reshape(5, eighth)
    qkvb = small[n_sum : n_sum + n_qb].reshape(heads, -1)
    fc1b = small[n_sum + n_qb :].reshape(heads, -1)

    return (
        outputs,
        grads_in,
        mine[0],
        mine[1],
        mine[2],
        mine[3],
        env["grad_qkv"],
        qkvb,
        env["grad_dense"],
        mine[4],
        env["grad_fc1"],
        fc1b,
        env["grad_fc2"],
        mine[4],
    )


def solution(mesh):
    rows = P(None, None, ("dp", "tensor"), None)
    vector = P(("dp", "tensor"))
    return jax.shard_map(
        per_device,
        mesh=mesh,
        in_specs=(
            rows,
            P(),
            P(),
            rows,
            vector,
            vector,
            vector,
            vector,
            P("dp", "tensor", None),
            P("tensor", "dp"),
            P("tensor", "dp", None),
            vector,
            P("dp", "tensor"),
            P("tensor", "dp"),
            P("tensor", "dp"),
            vector,
        ),
        out_specs=(
            rows,
            rows,
            vector,
            vector,
            vector,
            vector,
            P("dp", "tensor", None),
            P("tensor", "dp"),
            P("tensor", "dp", None),
            vector,
            P("dp", "tensor"),
            P("tensor", "dp"),
            P("tensor", "dp"),
            vector,
        ),
        check_vma=False,
    )
```
